256 devices in a mesh: ord: 64 (over y, z, core), blk: 4 (over x).
Axes of the slice: x: 4, y: 4, z: 8, core: 2. Of those that a mesh axis runs over, the one named last changes fastest.
Arguments:
- panel: bfloat16 [2880, 64, 2880], P('ord', 'blk'), as said below
- gauss: bfloat16 [2, 16, 2880, 2880], P(None, None, 'ord', 'blk'), may hold values from -2.3841858e-06 to 2.3841858e-06
- height: float32 [16], replicated, may hold values from 0.25 to 2.5
- order_map: int32 [2880], replicated, may hold values from 0 to 2879, as said below
- cycle_map: int32 [64], P('blk'), may hold values from 360 to 2519, as said below
Outputs:
- field: bfloat16 [5760, 3072], P('ord', 'blk')
The draws below stay inside these ranges and needn't reach their ends.
Inputs may be any that keep to these rules, and one draw needn't show every extreme that they name: `order_map`: a permutation of 0 to 2879; the 45 slots of each index of ord hold consecutive orders in ascending order. `panel`: entries at degrees below the order of their slot are zero. `cycle_map`: distinct cycle numbers.
All inputs are finite; a program needn't handle non-finite values.
Results may differ from the reference program's by a relative error of at most 0.0068.
Values may be sent and summed in bfloat16 or wider, within the bound.
No kernel may reach another device: no remote copies, remote signals or barrier semaphores. Data moves between devices by JAX's collectives and lax.ppermute only.
A program may use at most 128 MiB of HBM per device.

```python
import math
import jax
import jax.numpy as jnp
from jax import lax

ORDERS = 2880
SHELLS = 16
CYCLES = 64
ORD_DEV = 45
NLON = 5760


def order_runs(key):
    runs = ORDERS // ORD_DEV
    shuffled = jax.random.permutation(key, runs).astype(jnp.int32)
    slots = shuffled[:, None] * ORD_DEV + jnp.arange(ORD_DEV).astype(jnp.int32)[None, :]
    return slots.reshape(ORDERS).astype(jnp.int32)


def draw_order_map(key, part):
    return order_runs(jax.random.fold_in(key, 11))


def draw_panel(key, part):
    orders = order_runs(jax.random.fold_in(key, 11))
    sub = jax.random.fold_in(key, 12)
    values = jax.random.normal(sub, (ORDERS, CYCLES, ORDERS), jnp.float32)
    degree = jnp.arange(ORDERS).astype(jnp.int32)
    keep = degree[None, None, :] >= orders[:, None, None]
    return jnp.where(keep, values, 0.0).astype(jnp.bfloat16)


def draw_cycle_map(key, part):
    band = 3 * ORDERS // 4
    chosen = jax.random.permutation(jax.random.fold_in(key, 13), band).astype(jnp.int32)
    return (chosen[:CYCLES] + ORDERS // 8).astype(jnp.int32)


def levels(own_key, dims, pieces, smallest, largest):
    def one(dim, blocks):
        heights = jax.random.uniform(jax.random.fold_in(jax.random.fold_in(own_key, 6), dim), (blocks,), jnp.float32, smallest / len(pieces), largest / len(pieces))
        return jnp.repeat(jnp.exp(heights), dims[dim] // blocks).reshape((-1,) + (1,) * (len(dims) - dim - 1))

    factor_of = one(*pieces[0])
    for cut in pieces[1:]:
        factor_of = factor_of * one(*cut)
    return factor_of


def normal_values(stream_key, shape, scale, bound, pieces=(), kind=jnp.bfloat16):
    values = scale * jax.random.normal(stream_key, shape, jnp.float32)
    if pieces:
        values = values * levels(stream_key, shape, pieces, -0.22, 0.18)
    return jnp.clip(values, -bound, bound).astype(kind)


def setup_inputs(seed: int = 0) -> dict:
    key_list = jax.random.split(jax.random.key(seed), 6)
    panel = draw_panel(jax.random.fold_in(key_list[5], 71), 0)
    gauss = normal_values(key_list[1], (2, SHELLS, ORDERS, ORDERS), (ORDERS ** 4 // 10) ** -0.5, 2.384185791015625e-06, ((2, 64), (3, 4)))
    height = jnp.clip(jnp.exp(jax.random.uniform(key_list[2], (SHELLS,), jnp.float32, math.log(0.25), math.log(2.5))), 0.25, 2.5)
    order_map = draw_order_map(jax.random.fold_in(key_list[5], 71), 0)
    cycle_map = draw_cycle_map(jax.random.fold_in(key_list[5], 71), 0)
    return {"panel": panel, "gauss": gauss, "height": height, "order_map": order_map, "cycle_map": cycle_map}


def cycle_angles(cycle_map):
    theta = math.pi * (cycle_map.astype(jnp.float32) + 0.5) / ORDERS
    return (jnp.cos(theta), jnp.sin(theta))

def legendre_tables(current, before, degree, orders, cosine, sine):
    deg = degree[None, None, :]
    order = orders[:, None, None]
    radial = (deg + 1.0) * current
    polar = -(deg * cosine[None, :, None] * current - jnp.sqrt(jnp.maximum(deg * deg - order * order, 0.0)) * before) / sine[None, :, None]
    azimuth = order * current / sine[None, :, None]
    return jnp.stack([radial, polar, azimuth], 2).astype(jnp.bfloat16)

def weighted(coef, degree, height):
    radial = jnp.exp(-(degree[None, :] + 2.0) * height[:, None] / ORDERS)
    return (coef.astype(jnp.float32) * radial[None, :, None, :]).astype(jnp.bfloat16)

def assemble(total, cycles, shells):
    count = total.shape[1]
    parts = total.reshape(2, count, cycles, 3, shells)
    g_part = parts[0]
    h_part = parts[1]
    cosine_part = jnp.concatenate([g_part[:, :, :2], -h_part[:, :, 2:]], 2)
    sine_part = jnp.concatenate([h_part[:, :, :2], g_part[:, :, 2:]], 2)
    return jnp.stack([cosine_part, sine_part]).reshape(2, count, cycles * 3 * shells).astype(jnp.bfloat16)

def fourier_tables(order_map, position):
    phase = order_map.astype(jnp.int32)[:, None] * position.astype(jnp.int32)[None, :] % NLON
    angle = phase.astype(jnp.float32) * (2.0 * math.pi / NLON)
    return jnp.stack([jnp.cos(angle), jnp.sin(angle)]).astype(jnp.bfloat16)

def reference(panel, gauss, height, order_map, cycle_map):
    cosine, sine = cycle_angles(cycle_map)
    degree = jnp.arange(ORDERS).astype(jnp.float32)

    def one_slot(slot):
        slot = slot.astype(jnp.int32)
        current = lax.dynamic_slice_in_dim(panel, slot, 1, 0).astype(jnp.float32)
        before = jnp.concatenate([jnp.zeros((1, CYCLES, 1), jnp.float32), current[:, :, :-1]], 2)
        order = lax.dynamic_slice_in_dim(order_map, slot, 1, 0).astype(jnp.float32)
        tables = legendre_tables(current, before, degree, order, cosine, sine).reshape(1, CYCLES * 3, ORDERS)
        coef = lax.dynamic_slice_in_dim(gauss, slot, 1, 2)
        weights = weighted(coef, degree, height)
        total = jnp.einsum('okl,gsol->goks', tables.astype(jnp.float32), weights.astype(jnp.float32))
        return assemble(total, CYCLES, SHELLS)[:, 0]
    spectra = lax.map(one_slot, jnp.arange(ORDERS).astype(jnp.int32))
    spectra = jnp.transpose(spectra, (1, 0, 2))
    tables = fourier_tables(order_map, jnp.arange(NLON).astype(jnp.int32))
    field = lax.dot_general(tables.astype(jnp.float32), spectra.astype(jnp.float32), (((0, 1), (0, 1)), ((), ())), precision=lax.Precision.HIGHEST)
    return field.astype(jnp.bfloat16)
```

```python
import functools
import math

import jax
import jax.numpy as jnp
from jax import lax
from jax.experimental import pallas as pl
from jax.experimental.pallas import tpu as pltpu
from jax.sharding import PartitionSpec as P

ORDERS = 2880
RUN = 45
QUARTER = 720
START = 1408
WIDE = 1536
NLON = 5760
GROUP = 5
GAUSS_PAIRS = [(0, 1), (1, 0), (2, 3), (3, 2)]
PANEL_PAIRS = [(1, 2), (2, 1), (3, 0), (0, 3)]


def sums_kernel(where_ref, order_ref, height_ref, own_ref, other_ref, near_ref, far_ref, out_ref,
                gs_ref, gn_ref, decay_ref):
    step = pl.program_id(0)
    half = where_ref[0]
    odd = where_ref[1] == 1
    first = (half * START).astype(jnp.float32)
    degree = lax.broadcasted_iota(jnp.int32, (1, WIDE), 1).astype(jnp.float32) + first

    @pl.when(step == 0)
    def _():
        gs_ref[...] = jnp.zeros_like(gs_ref)
        gn_ref[...] = jnp.zeros_like(gn_ref)
        height = height_ref[...]
        here = jnp.exp(-(degree + 2.0) * height / ORDERS)
        decay_ref[0] = here
        decay_ref[1] = here * (degree + 1.0)
        decay_ref[2] = jnp.exp(-(degree + 3.0) * height / ORDERS)

    low = jnp.where(odd, other_ref[...], own_ref[...])
    high = jnp.where(odd, own_ref[...], other_ref[...])

    @pl.when(half == 0)
    def _():
        gs_ref[:, :, :, 0:720] = low
        gs_ref[:, :, :, 720:1440] = high
        gn_ref[:, :, :, 0:719] = low[:, :, :, 1:]
        gn_ref[:, :, :, 719:1439] = high

    @pl.when(half == 1)
    def _():
        gs_ref[:, :, :, 32:752] = low
        gs_ref[:, :, :, 752:1472] = high
        gn_ref[:, :, :, 31:751] = low
        gn_ref[:, :, :, 751:1471] = high

    for o in range(GROUP):
        m = order_ref[step * GROUP + o].astype(jnp.float32)
        root = jnp.sqrt(jnp.maximum((degree + 1.0) * (degree + 1.0) - m * m, 0.0))
        slope = decay_ref[2] * root
        g = [gs_ref[k, o].astype(jnp.float32) for k in range(2)]
        n = [gn_ref[k, o].astype(jnp.float32) for k in range(2)]
        weights = jnp.concatenate(
            [g[0] * decay_ref[1], g[1] * decay_ref[1], g[0] * decay_ref[0], g[1] * decay_ref[0],
             n[0] * slope, n[1] * slope], 0).astype(jnp.bfloat16)
        table = jnp.concatenate([near_ref[o], far_ref[o]], 0)
        out_ref[o] = lax.dot_general(
            table, weights, (((1,), (1,)), ((), ())), preferred_element_type=jnp.float32)


def partial_sums(where, orders, height, own, other, near, far):
    count = near.shape[0]
    smem = pl.BlockSpec(memory_space=pltpu.SMEM)
    coef = pl.BlockSpec((2, GROUP, 16, QUARTER), lambda i: (0, i, 0, 0))
    tab = pl.BlockSpec((GROUP, 16, WIDE), lambda i: (i, 0, 0))
    return pl.pallas_call(
        sums_kernel,
        out_shape=jax.ShapeDtypeStruct((count, 32, 96), jnp.float32),
        grid=(count // GROUP,),
        in_specs=[smem, smem, pl.BlockSpec((16, 1), lambda i: (0, 0)), coef, coef, tab, tab],
        out_specs=pl.BlockSpec((GROUP, 32, 96), lambda i: (i, 0, 0)),
        scratch_shapes=[
            pltpu.VMEM((2, GROUP, 16, WIDE), jnp.bfloat16),
            pltpu.VMEM((2, GROUP, 16, WIDE), jnp.bfloat16),
            pltpu.VMEM((3, 16, WIDE), jnp.float32),
        ],
        compiler_params=pltpu.CompilerParams(vmem_limit_bytes=40 << 20),
        name="partial_sums",
    )(where, orders, height, own, other, near, far)


def turn(phase, period):
    angle = (phase % period).astype(jnp.float32) * (2.0 * math.pi / period)
    return jnp.cos(angle), jnp.sin(angle)


def body(panel, gauss, height, order_map, cycle_map):
    count, cycles, _ = panel.shape
    shells = height.shape[0]
    spot = lax.axis_index("blk")
    here = lax.axis_index("ord")
    half = spot // 2
    own = jnp.transpose(gauss, (0, 2, 1, 3))
    other = lax.ppermute(own, "blk", GAUSS_PAIRS)
    upper = jnp.pad(panel[:, :, START:], ((0, 0), (0, 0), (0, START + WIDE - ORDERS)))
    lower = panel[:, :, :WIDE]
    sent = jnp.where(half == 0, upper, lower)
    near = jnp.where(half == 0, lower, upper)
    far = lax.ppermute(sent, "blk", PANEL_PAIRS)
    orders_int = lax.dynamic_slice_in_dim(order_map, here * count, count, 0)
    where = jnp.stack([half, spot % 2]).astype(jnp.int32)
    raw = partial_sums(where, orders_int, height[:, None], own, other, near, far)
    total = raw[:, :cycles] + lax.ppermute(raw[:, cycles:], "blk", PANEL_PAIRS)
    theta = math.pi * (cycle_map.astype(jnp.float32) + 0.5) / ORDERS
    cosine = jnp.cos(theta)[None, :, None]
    sine = jnp.sin(theta)[None, :, None]
    m = orders_int.astype(jnp.float32)[:, None, None]
    s0, s2, s3 = total[:, :, 0:32], total[:, :, 32:64], total[:, :, 64:96]
    s1 = -(cosine * (s0 - s2) - s3) / sine
    s2 = m * s2 / sine
    g, h = slice(0, shells), slice(shells, 2 * shells)
    spectra = jnp.stack([
        jnp.stack([s0[..., g], s1[..., g], -s2[..., h]], 2),
        jnp.stack([s0[..., h], s1[..., h], s2[..., g]], 2),
    ]).reshape(2, count, cycles * 3 * shells).astype(jnp.bfloat16)

    parts = ORDERS // count
    items = cycles * 3 * shells // parts
    chunk = jnp.transpose(spectra.reshape(2, count, parts, items), (2, 0, 1, 3))
    spread = lax.all_to_all(chunk.reshape(parts, 2, count * items), "ord", 0, 0, tiled=True)
    spread = spread.astype(jnp.float32)
    runs = order_map[::RUN] // RUN
    b = jnp.arange(128)
    q = jnp.arange(RUN)
    cos1, sin1 = turn(b[:, None] * runs[None, :], 128)
    table = jnp.concatenate(
        [jnp.concatenate([cos1, sin1], 1), jnp.concatenate([sin1, -cos1], 1)], 0)
    flat = jnp.concatenate([spread[:, 0], spread[:, 1]], 0)
    mid = jnp.dot(table, flat, precision=lax.Precision.HIGHEST).reshape(2, 128, count, items)
    cos2, sin2 = turn(b[:, None] * q[None, :], NLON)
    cos2, sin2 = cos2[:, :, None], sin2[:, :, None]
    real = mid[0] * cos2 - mid[1] * sin2
    imag = mid[0] * sin2 + mid[1] * cos2
    cos3, sin3 = turn(q[:, None] * q[None, :], RUN)
    field = lax.dot_general(
        jnp.concatenate([cos3, -sin3], 1), jnp.concatenate([real, imag], 1),
        (((1,), (1,)), ((), ())), precision=lax.Precision.HIGHEST)
    field = field.reshape(NLON, items).astype(jnp.bfloat16)
    return lax.all_to_all(field, "ord", split_axis=0, concat_axis=1, tiled=True)


def solution(mesh):
    return jax.shard_map(
        body,
        mesh=mesh,
        in_specs=(P("ord", "blk", None), P(None, None, "ord", "blk"), P(), P(), P("blk")),
        out_specs=P("ord", "blk"),
        check_vma=False,
    )
```

```python
import functools
import math

import jax
import jax.numpy as jnp
from jax import lax
from jax.experimental import pallas as pl
from jax.experimental.pallas import tpu as pltpu
from jax.sharding import PartitionSpec as P

ORDERS = 2880
RUN = 45
QUARTER = 720
START = 1408
WIDE = 1536
KEPT = 1472
NLON = 5760
GROUP = 5
CHUNKS = (0, 30, 40, 45)
GAUSS_PAIRS = [(0, 1), (1, 0), (2, 3), (3, 2)]
PANEL_PAIRS = [(1, 2), (2, 1), (3, 0), (0, 3)]


def sums_kernel(where_ref, order_ref, height_ref, own_ref, other_ref, panel_ref, far_ref, after_ref,
                keep_ref, send_ref, gs_ref, gn_ref, decay_ref, table_ref, *, base):
    step = pl.program_id(0)
    half = where_ref[0]
    odd = where_ref[1] == 1
    first = (half * START).astype(jnp.float32)
    degree = lax.broadcasted_iota(jnp.int32, (1, WIDE), 1).astype(jnp.float32) + first

    @pl.when(step == 0)
    def _():
        gs_ref[...] = jnp.zeros_like(gs_ref)
        gn_ref[...] = jnp.zeros_like(gn_ref)
        table_ref[...] = jnp.zeros_like(table_ref)
        height = height_ref[...]
        here = jnp.exp(-(degree + 2.0) * height / ORDERS)
        decay_ref[0] = here
        decay_ref[1] = here * (degree + 1.0)
        decay_ref[2] = jnp.exp(-(degree + 3.0) * height / ORDERS)

    low = jnp.where(odd, other_ref[...], own_ref[...])
    high = jnp.where(odd, own_ref[...], other_ref[...])
    table_ref[:, 16:32, 0:KEPT] = far_ref[...]

    @pl.when(half == 0)
    def _():
        table_ref[:, 0:16, 0:KEPT] = panel_ref[:, :, 0:KEPT]
        gs_ref[:, :, :, 0:720] = low
        gs_ref[:, :, :, 720:1440] = high
        gn_ref[:, :, :, 0:719] = low[:, :, :, 1:]
        gn_ref[:, :, :, 719:1439] = high

    @pl.when(half == 1)
    def _():
        table_ref[:, 0:16, 0:KEPT] = panel_ref[:, :, START:ORDERS]
        gs_ref[:, :, :, 32:752] = low
        gs_ref[:, :, :, 752:1472] = high
        gn_ref[:, :, :, 31:751] = low
        gn_ref[:, :, :, 751:1471] = high

    for o in range(GROUP):
        m = order_ref[base + step * GROUP + o].astype(jnp.float32)
        root = jnp.sqrt(jnp.maximum((degree + 1.0) * (degree + 1.0) - m * m, 0.0))
        slope = decay_ref[2] * root
        g = [gs_ref[k, o].astype(jnp.float32) for k in range(2)]
        n = [gn_ref[k, o].astype(jnp.float32) for k in range(2)]
        weights = jnp.concatenate(
            [g[0] * decay_ref[1], g[1] * decay_ref[1], g[0] * decay_ref[0], g[1] * decay_ref[0],
             n[0] * slope, n[1] * slope], 0).astype(jnp.bfloat16)
        sums = lax.dot_general(
            table_ref[o], weights, (((1,), (1,)), ((), ())), preferred_element_type=jnp.float32)
        keep_ref[o] = sums[:16]
        send_ref[o] = sums[16:].astype(jnp.bfloat16)


def partial_sums(where, orders, height, own, other, panel, far, after, base):
    count = far.shape[0]
    skip = base // GROUP
    smem = pl.BlockSpec(memory_space=pltpu.SMEM)
    out = pl.BlockSpec((GROUP, 16, 96), lambda i: (i, 0, 0))
    return pl.pallas_call(
        functools.partial(sums_kernel, base=base),
        out_shape=[jax.ShapeDtypeStruct((count, 16, 96), jnp.float32),
                   jax.ShapeDtypeStruct((count, 16, 96), jnp.bfloat16)],
        grid=(count // GROUP,),
        in_specs=[
            smem, smem, pl.BlockSpec((16, 1), lambda i: (0, 0)),
            pl.BlockSpec((2, GROUP, 16, QUARTER), lambda i: (0, i + skip, 0, 0)),
            pl.BlockSpec((2, GROUP, 16, QUARTER), lambda i: (0, i, 0, 0)),
            pl.BlockSpec((GROUP, 16, ORDERS), lambda i: (i + skip, 0, 0)),
            pl.BlockSpec((GROUP, 16, KEPT), lambda i: (i, 0, 0)),
            pl.BlockSpec(memory_space=pl.ANY),
        ],
        out_specs=[out, out],
        scratch_shapes=[
            pltpu.VMEM((2, GROUP, 16, WIDE), jnp.bfloat16),
            pltpu.VMEM((2, GROUP, 16, WIDE), jnp.bfloat16),
            pltpu.VMEM((3, 16, WIDE), jnp.float32),
            pltpu.VMEM((GROUP, 32, WIDE), jnp.bfloat16),
        ],
        compiler_params=pltpu.CompilerParams(vmem_limit_bytes=24 << 20),
        cost_estimate=pl.CostEstimate(
            flops=count * 32 * 96 * WIDE * 2, bytes_accessed=count * 200000, transcendentals=0),
        name="partial_sums",
    )(where, orders, height, own, other, panel, far, after)


def turn(phase, period):
    angle = (phase % period).astype(jnp.float32) * (2.0 * math.pi / period)
    return jnp.cos(angle), jnp.sin(angle)


def body(panel, gauss, height, order_map, cycle_map):
    count, cycles, _ = panel.shape
    shells = height.shape[0]
    spot = lax.axis_index("blk")
    here = lax.axis_index("ord")
    half = spot // 2
    own = jnp.transpose(gauss, (0, 2, 1, 3))
    orders_int = lax.dynamic_slice_in_dim(order_map, here * count, count, 0)
    where = jnp.stack([half, spot % 2]).astype(jnp.int32)
    spans = list(zip(CHUNKS[:-1], CHUNKS[1:]))
    arrived = []
    late = jnp.zeros((), jnp.int32)
    for a, b in spans:
        part = lax.dynamic_slice_in_dim(own, a + late, b - a, 1)
        other = lax.ppermute(part, "blk", GAUSS_PAIRS)
        sent = jnp.where(half + late == 0, panel[a:b, :, START:], panel[a:b, :, :KEPT])
        arrived.append((other, lax.ppermute(sent, "blk", PANEL_PAIRS)))
        late = jnp.isnan(sent[0, 0, 0]).astype(jnp.int32)
    totals = []
    keep = own
    for (a, b), (other, far) in zip(spans, arrived):
        keep, send = partial_sums(where, orders_int, height[:, None], own, other, panel, far, keep, a)
        totals.append(keep + lax.ppermute(send, "blk", PANEL_PAIRS).astype(jnp.float32))
    total = jnp.concatenate(totals, 0)
    theta = math.pi * (cycle_map.astype(jnp.float32) + 0.5) / ORDERS
    cosine = jnp.cos(theta)[None, :, None]
    sine = jnp.sin(theta)[None, :, None]
    m = orders_int.astype(jnp.float32)[:, None, None]
    s0, s2, s3 = total[:, :, 0:32], total[:, :, 32:64], total[:, :, 64:96]
    s1 = -(cosine * (s0 - s2) - s3) / sine
    s2 = m * s2 / sine
    g, h = slice(0, shells), slice(shells, 2 * shells)
    spectra = jnp.stack([
        jnp.stack([s0[..., g], s1[..., g], -s2[..., h]], 2),
        jnp.stack([s0[..., h], s1[..., h], s2[..., g]], 2),
    ]).reshape(2, count, cycles * 3 * shells).astype(jnp.bfloat16)

    parts = ORDERS // count
    items = cycles * 3 * shells // parts
    chunk = jnp.transpose(spectra.reshape(2, count, parts, items), (2, 0, 1, 3))
    spread = lax.all_to_all(chunk.reshape(parts, 2, count * items), "ord", 0, 0, tiled=True)
    spread = spread.astype(jnp.float32)
    runs = order_map[::RUN] // RUN
    b = jnp.arange(128)
    q = jnp.arange(RUN)
    cos1, sin1 = turn(b[:, None] * runs[None, :], 128)
    table = jnp.concatenate(
        [jnp.concatenate([cos1, sin1], 1), jnp.concatenate([sin1, -cos1], 1)], 0)
    flat = jnp.concatenate([spread[:, 0], spread[:, 1]], 0)
    mid = jnp.dot(table, flat, precision=lax.Precision.HIGHEST).reshape(2, 128, count, items)
    cos2, sin2 = turn(b[:, None] * q[None, :], NLON)
    cos2, sin2 = cos2[:, :, None], sin2[:, :, None]
    real = mid[0] * cos2 - mid[1] * sin2
    imag = mid[0] * sin2 + mid[1] * cos2
    cos3, sin3 = turn(q[:, None] * q[None, :], RUN)
    field = lax.dot_general(
        jnp.concatenate([cos3, -sin3], 1), jnp.concatenate([real, imag], 1),
        (((1,), (1,)), ((), ())), precision=lax.Precision.HIGHEST)
    field = field.reshape(NLON, items).astype(jnp.bfloat16)
    return lax.all_to_all(field, "ord", split_axis=0, concat_axis=1, tiled=True)


def solution(mesh):
    return jax.shard_map(
        body,
        mesh=mesh,
        in_specs=(P("ord", "blk", None), P(None, None, "ord", "blk"), P(), P(), P("blk")),
        out_specs=P("ord", "blk"),
        check_vma=False,
    )
```

```python
import functools
import math

import jax
import jax.numpy as jnp
from jax import lax
from jax.experimental import pallas as pl
from jax.experimental.pallas import tpu as pltpu
from jax.sharding import PartitionSpec as P

ORDERS = 2880
RUN = 45
QUARTER = 720
START = 1408
WIDE = 1536
KEPT = 1472
NLON = 5760
GROUP = 5
CHUNKS = (0, 20, 35, 45)
GAUSS_PAIRS = [(0, 1), (1, 0), (2, 3), (3, 2)]
PANEL_PAIRS = [(1, 2), (2, 1), (3, 0), (0, 3)]


def sums_kernel(where_ref, order_ref, height_ref, angle_ref, own_ref, other_ref, panel_ref, far_ref,
                *rest, base):
    keep_ref, send_ref, gs_ref, gn_ref, decay_ref, table_ref = rest[-6:]
    step = pl.program_id(0)
    half = where_ref[0]
    odd = where_ref[1] == 1
    first = (half * START).astype(jnp.float32)
    degree = lax.broadcasted_iota(jnp.int32, (1, WIDE), 1).astype(jnp.float32) + first

    @pl.when(step == 0)
    def _():
        gs_ref[...] = jnp.zeros_like(gs_ref)
        gn_ref[...] = jnp.zeros_like(gn_ref)
        table_ref[...] = jnp.zeros_like(table_ref)
        height = height_ref[...]
        here = jnp.exp(-(degree + 2.0) * height / ORDERS)
        decay_ref[0] = here
        decay_ref[1] = here * (degree + 1.0)
        decay_ref[2] = jnp.exp(-(degree + 3.0) * height / ORDERS)

    low = jnp.where(odd, other_ref[...], own_ref[...])
    high = jnp.where(odd, own_ref[...], other_ref[...])
    table_ref[:, 16:32, 0:KEPT] = far_ref[...]

    @pl.when(half == 0)
    def _():
        table_ref[:, 0:16, 0:KEPT] = panel_ref[:, :, 0:KEPT]
        gs_ref[:, :, :, 0:720] = low
        gs_ref[:, :, :, 720:1440] = high
        gn_ref[:, :, :, 0:719] = low[:, :, :, 1:]
        gn_ref[:, :, :, 719:1439] = high

    @pl.when(half == 1)
    def _():
        table_ref[:, 0:16, 0:KEPT] = panel_ref[:, :, START:ORDERS]
        gs_ref[:, :, :, 32:752] = low
        gs_ref[:, :, :, 752:1472] = high
        gn_ref[:, :, :, 31:751] = low
        gn_ref[:, :, :, 751:1471] = high

    cosine = angle_ref[:, 0:1]
    inverse = angle_ref[:, 1:2]
    lane = lax.broadcasted_iota(jnp.int32, (32, 128), 1)
    for o in range(GROUP):
        m = order_ref[base + step * GROUP + o].astype(jnp.float32)
        root = jnp.sqrt(jnp.maximum((degree + 1.0) * (degree + 1.0) - m * m, 0.0))
        slope = decay_ref[2] * root
        g = [gs_ref[k, o].astype(jnp.float32) for k in range(2)]
        n = [gn_ref[k, o].astype(jnp.float32) for k in range(2)]
        main = [(g[k] * decay_ref[1]).astype(jnp.bfloat16) for k in range(2)]
        bare = [(g[k] * decay_ref[0]).astype(jnp.bfloat16) for k in range(2)]
        tilt = [(n[k] * slope).astype(jnp.bfloat16) for k in range(2)]
        weights = jnp.concatenate(main + bare + [-bare[1], bare[0]] + tilt, 0)
        sums = lax.dot_general(
            table_ref[o], weights, (((1,), (1,)), ((), ())), preferred_element_type=jnp.float32)
        polar = (pltpu.roll(sums, 64, 1) - cosine * (pltpu.roll(sums, 32, 1) - sums)) * inverse
        mixed = jnp.where(lane < 32, sums, jnp.where(lane < 64, polar, m * inverse * sums))
        keep_ref[o] = mixed[:16, :96]
        send_ref[o] = mixed[16:, :96].astype(jnp.bfloat16)


def partial_sums(where, orders, height, angles, own, other, panel, far, after, base):
    count = far.shape[0]
    skip = base // GROUP
    smem = pl.BlockSpec(memory_space=pltpu.SMEM)
    out = pl.BlockSpec((GROUP, 16, 96), lambda i: (i, 0, 0))
    return pl.pallas_call(
        functools.partial(sums_kernel, base=base),
        out_shape=[jax.ShapeDtypeStruct((count, 16, 96), jnp.float32),
                   jax.ShapeDtypeStruct((count, 16, 96), jnp.bfloat16)],
        grid=(count // GROUP,),
        in_specs=[
            smem, smem, pl.BlockSpec((16, 1), lambda i: (0, 0)),
            pl.BlockSpec((32, 2), lambda i: (0, 0)),
            pl.BlockSpec((2, GROUP, 16, QUARTER), lambda i: (0, i + skip, 0, 0)),
            pl.BlockSpec((2, GROUP, 16, QUARTER), lambda i: (0, i, 0, 0)),
            pl.BlockSpec((GROUP, 16, ORDERS), lambda i: (i + skip, 0, 0)),
            pl.BlockSpec((GROUP, 16, KEPT), lambda i: (i, 0, 0)),
        ] + [pl.BlockSpec(memory_space=pl.ANY)] * len(after),
        out_specs=[out, out],
        scratch_shapes=[
            pltpu.VMEM((2, GROUP, 16, WIDE), jnp.bfloat16),
            pltpu.VMEM((2, GROUP, 16, WIDE), jnp.bfloat16),
            pltpu.VMEM((3, 16, WIDE), jnp.float32),
            pltpu.VMEM((GROUP, 32, WIDE), jnp.bfloat16),
        ],
        compiler_params=pltpu.CompilerParams(vmem_limit_bytes=24 << 20),
        cost_estimate=pl.CostEstimate(
            flops=count * 32 * 96 * WIDE * 2, bytes_accessed=count * 200000, transcendentals=0),
        name="partial_sums",
    )(where, orders, height, angles, own, other, panel, far, *after)


def turn(phase, period):
    angle = (phase % period).astype(jnp.float32) * (2.0 * math.pi / period)
    return jnp.cos(angle), jnp.sin(angle)


def body(panel, gauss, height, order_map, cycle_map):
    count, cycles, _ = panel.shape
    shells = height.shape[0]
    spot = lax.axis_index("blk")
    here = lax.axis_index("ord")
    half = spot // 2
    own = jnp.transpose(gauss, (0, 2, 1, 3))
    orders_int = lax.dynamic_slice_in_dim(order_map, here * count, count, 0)
    where = jnp.stack([half, spot % 2]).astype(jnp.int32)
    spans = list(zip(CHUNKS[:-1], CHUNKS[1:]))
    arrived = []
    late, next_ = 0, 0
    for a, b in spans:
        part = lax.dynamic_slice_in_dim(own, a + next_, b - a, 1)
        other = lax.ppermute(part, "blk", GAUSS_PAIRS)
        sent = jnp.where(half + late == 0, panel[a:b, :, START:], panel[a:b, :, :KEPT])
        arrived.append((other, lax.ppermute(sent, "blk", PANEL_PAIRS)))
        late = jnp.isnan(sent[0, 0, 0]).astype(jnp.int32)
        next_ = jnp.isnan(part[0, 0, 0, 0]).astype(jnp.int32)
    facing = lax.ppermute(cycle_map, "blk", PANEL_PAIRS)
    theta = math.pi * (jnp.concatenate([cycle_map, facing]).astype(jnp.float32) + 0.5) / ORDERS
    angles = jnp.stack([jnp.cos(theta), 1.0 / jnp.sin(theta)], 1)
    kept, added = [], []
    for c, ((a, b), (other, far)) in enumerate(zip(spans, arrived)):
        after = (kept[-1:] or [own]) + (added[c - 2:c - 1] if c >= 2 else [])
        keep, send = partial_sums(
            where, orders_int, height[:, None], angles, own, other, panel, far, after, a)
        kept.append(keep)
        added.append(lax.ppermute(send, "blk", PANEL_PAIRS))
    total = jnp.concatenate(kept, 0) + jnp.concatenate(added, 0).astype(jnp.float32)
    total = lax.optimization_barrier(total.astype(jnp.bfloat16))
    split = (count, cycles, 3, 2, 4, shells // 4)
    chunk = jnp.transpose(total.reshape(split), (1, 4, 3, 2, 5, 0))

    parts = ORDERS // count
    items = cycles * 3 * shells // parts
    runs = order_map[::RUN] // RUN
    b = jnp.arange(128)
    q = jnp.arange(RUN)
    cos1, sin1 = turn(b[:, None] * runs[None, :], 128)
    table = jnp.concatenate(
        [jnp.concatenate([cos1, sin1], 1), jnp.concatenate([sin1, -cos1], 1)], 0)
    cos2, sin2 = turn(b[:, None] * q[None, :], NLON)
    cos3, sin3 = turn(q[:, None] * q[None, :], RUN)
    last = jnp.concatenate([cos3, -sin3], 1)

    chunk = chunk.reshape(parts, 2, items * count)
    chunk, table, cos2, sin2, last = lax.optimization_barrier((chunk, table, cos2, sin2, last))
    spread = lax.all_to_all(chunk, "ord", 0, 0, tiled=True).astype(jnp.float32)
    flat = jnp.concatenate([spread[:, 0], spread[:, 1]], 0)
    mid = jnp.dot(table, flat, precision=lax.Precision.HIGHEST).reshape(2, 128, items, count)
    cos2, sin2 = cos2[:, None, :], sin2[:, None, :]
    real = mid[0] * cos2 - mid[1] * sin2
    imag = mid[0] * sin2 + mid[1] * cos2
    field = lax.dot_general(
        last, jnp.concatenate([real, imag], 2),
        (((1,), (2,)), ((), ())), precision=lax.Precision.HIGHEST)
    field = field.reshape(parts, NLON // parts, items).astype(jnp.bfloat16)
    field = lax.all_to_all(field, "ord", 0, 0, tiled=True)
    field = field.reshape(cycles, 4, NLON // parts, 3, shells // 4)
    return jnp.transpose(field, (2, 0, 3, 1, 4)).reshape(NLON // parts, cycles * 3 * shells)


def solution(mesh):
    return jax.shard_map(
        body,
        mesh=mesh,
        in_specs=(P("ord", "blk", None), P(None, None, "ord", "blk"), P(), P(), P("blk")),
        out_specs=P("ord", "blk"),
        check_vma=False,
    )
```

```python
import functools
import math

import jax
import jax.numpy as jnp
from jax import lax
from jax.experimental import pallas as pl
from jax.experimental.pallas import tpu as pltpu
from jax.sharding import PartitionSpec as P

ORDERS = 2880
RUN = 45
QUARTER = 720
START = 1408
WIDE = 1536
KEPT = 1472
NLON = 5760
GROUP = 5
CHUNKS = (0, 10, 20, 30, 40, 45)
GAUSS_PAIRS = [(0, 1), (1, 0), (2, 3), (3, 2)]
PANEL_PAIRS = [(1, 2), (2, 1), (3, 0), (0, 3)]


def sums_kernel(where_ref, order_ref, height_ref, angle_ref, own_ref, other_ref, panel_ref, far_ref,
                *rest, base):
    keep_ref, send_ref, gs_ref, gn_ref, decay_ref, table_ref = rest[-6:]
    step = pl.program_id(0)
    half = where_ref[0]
    odd = where_ref[1] == 1
    first = (half * START).astype(jnp.float32)
    degree = lax.broadcasted_iota(jnp.int32, (1, WIDE), 1).astype(jnp.float32) + first

    @pl.when(step == 0)
    def _():
        gs_ref[...] = jnp.zeros_like(gs_ref)
        gn_ref[...] = jnp.zeros_like(gn_ref)
        table_ref[...] = jnp.zeros_like(table_ref)
        height = height_ref[...]
        here = jnp.exp(-(degree + 2.0) * height / ORDERS)
        decay_ref[0] = here
        decay_ref[1] = here * (degree + 1.0)
        decay_ref[2] = jnp.exp(-(degree + 3.0) * height / ORDERS)

    low = jnp.where(odd, other_ref[...], own_ref[...])
    high = jnp.where(odd, own_ref[...], other_ref[...])
    table_ref[:, 16:32, 0:KEPT] = far_ref[...]

    @pl.when(half == 0)
    def _():
        table_ref[:, 0:16, 0:KEPT] = panel_ref[:, :, 0:KEPT]
        gs_ref[:, :, :, 0:720] = low
        gs_ref[:, :, :, 720:1440] = high
        gn_ref[:, :, :, 0:719] = low[:, :, :, 1:]
        gn_ref[:, :, :, 719:1439] = high

    @pl.when(half == 1)
    def _():
        table_ref[:, 0:16, 0:KEPT] = panel_ref[:, :, START:ORDERS]
        gs_ref[:, :, :, 32:752] = low
        gs_ref[:, :, :, 752:1472] = high
        gn_ref[:, :, :, 31:751] = low
        gn_ref[:, :, :, 751:1471] = high

    cosine = angle_ref[:, 0:1]
    inverse = angle_ref[:, 1:2]
    lane = lax.broadcasted_iota(jnp.int32, (32, 128), 1)
    for o in range(GROUP):
        m = order_ref[base + step * GROUP + o].astype(jnp.float32)
        root = jnp.sqrt(jnp.maximum((degree + 1.0) * (degree + 1.0) - m * m, 0.0))
        slope = decay_ref[2] * root
        g = [gs_ref[k, o].astype(jnp.float32) for k in range(2)]
        n = [gn_ref[k, o].astype(jnp.float32) for k in range(2)]
        main = [(g[k] * decay_ref[1]).astype(jnp.bfloat16) for k in range(2)]
        bare = [(g[k] * decay_ref[0]).astype(jnp.bfloat16) for k in range(2)]
        tilt = [(n[k] * slope).astype(jnp.bfloat16) for k in range(2)]
        weights = jnp.concatenate(main + bare + [-bare[1], bare[0]] + tilt, 0)
        sums = lax.dot_general(
            table_ref[o], weights, (((1,), (1,)), ((), ())), preferred_element_type=jnp.float32)
        polar = (pltpu.roll(sums, 64, 1) - cosine * (pltpu.roll(sums, 32, 1) - sums)) * inverse
        mixed = jnp.where(lane < 32, sums, jnp.where(lane < 64, polar, m * inverse * sums))
        keep_ref[o] = mixed[:16, :96]
        send_ref[o] = mixed[16:, :96].astype(jnp.bfloat16)


def partial_sums(where, orders, height, angles, own, other, panel, far, after, base):
    count = far.shape[0]
    skip = base // GROUP
    smem = pl.BlockSpec(memory_space=pltpu.SMEM)
    out = pl.BlockSpec((GROUP, 16, 96), lambda i: (i, 0, 0))
    return pl.pallas_call(
        functools.partial(sums_kernel, base=base),
        out_shape=[jax.ShapeDtypeStruct((count, 16, 96), jnp.float32),
                   jax.ShapeDtypeStruct((count, 16, 96), jnp.bfloat16)],
        grid=(count // GROUP,),
        in_specs=[
            smem, smem, pl.BlockSpec((16, 1), lambda i: (0, 0)),
            pl.BlockSpec((32, 2), lambda i: (0, 0)),
            pl.BlockSpec((2, GROUP, 16, QUARTER), lambda i: (0, i + skip, 0, 0)),
            pl.BlockSpec((2, GROUP, 16, QUARTER), lambda i: (0, i, 0, 0)),
            pl.BlockSpec((GROUP, 16, ORDERS), lambda i: (i + skip, 0, 0)),
            pl.BlockSpec((GROUP, 16, KEPT), lambda i: (i, 0, 0)),
        ] + [pl.BlockSpec(memory_space=pl.ANY)] * len(after),
        out_specs=[out, out],
        scratch_shapes=[
            pltpu.VMEM((2, GROUP, 16, WIDE), jnp.bfloat16),
            pltpu.VMEM((2, GROUP, 16, WIDE), jnp.bfloat16),
            pltpu.VMEM((3, 16, WIDE), jnp.float32),
            pltpu.VMEM((GROUP, 32, WIDE), jnp.bfloat16),
        ],
        compiler_params=pltpu.CompilerParams(vmem_limit_bytes=24 << 20),
        cost_estimate=pl.CostEstimate(
            flops=count * 32 * 96 * WIDE * 2, bytes_accessed=count * 200000, transcendentals=0),
        name="partial_sums",
    )(where, orders, height, angles, own, other, panel, far, *after)


def turn(phase, period):
    angle = (phase % period).astype(jnp.float32) * (2.0 * math.pi / period)
    return jnp.cos(angle), jnp.sin(angle)


def body(panel, gauss, height, order_map, cycle_map):
    count, cycles, _ = panel.shape
    shells = height.shape[0]
    spot = lax.axis_index("blk")
    here = lax.axis_index("ord")
    half = spot // 2
    own = jnp.transpose(gauss, (0, 2, 1, 3))
    orders_int = lax.dynamic_slice_in_dim(order_map, here * count, count, 0)
    where = jnp.stack([half, spot % 2]).astype(jnp.int32)
    spans = list(zip(CHUNKS[:-1], CHUNKS[1:]))
    arrived = []
    facing = lax.ppermute(cycle_map, "blk", PANEL_PAIRS)
    late, next_ = 0, 0
    for a, b in spans:
        part = lax.dynamic_slice_in_dim(own, a + next_, b - a, 1)
        other = lax.ppermute(part, "blk", GAUSS_PAIRS)
        sent = jnp.where(half + late == 0, panel[a:b, :, START:], panel[a:b, :, :KEPT])
        arrived.append((other, lax.ppermute(sent, "blk", PANEL_PAIRS)))
        late = jnp.isnan(sent[0, 0, 0]).astype(jnp.int32)
        next_ = jnp.isnan(part[0, 0, 0, 0]).astype(jnp.int32)
    theta = math.pi * (jnp.concatenate([cycle_map, facing]).astype(jnp.float32) + 0.5) / ORDERS
    angles = jnp.stack([jnp.cos(theta), 1.0 / jnp.sin(theta)], 1)
    kept, added = [], []
    for c, ((a, b), (other, far)) in enumerate(zip(spans, arrived)):
        after = (kept[-1:] or [own]) + (added[c - 2:c - 1] if c >= 2 else [])
        keep, send = partial_sums(
            where, orders_int, height[:, None], angles, own, other, panel, far, after, a)
        kept.append(keep)
        added.append(lax.ppermute(send, "blk", PANEL_PAIRS))
    total = jnp.concatenate(kept, 0) + jnp.concatenate(added, 0).astype(jnp.float32)
    total = lax.optimization_barrier(total.astype(jnp.bfloat16))
    split = (count, cycles, 3, 2, 4, shells // 4)
    chunk = jnp.transpose(total.reshape(split), (1, 4, 3, 2, 5, 0))

    parts = ORDERS // count
    items = cycles * 3 * shells // parts
    runs = order_map[::RUN] // RUN
    b = jnp.arange(128)
    q = jnp.arange(RUN)
    cos1, sin1 = turn(b[:, None] * runs[None, :], 128)
    table = jnp.concatenate(
        [jnp.concatenate([cos1, sin1], 1), jnp.concatenate([sin1, -cos1], 1)], 0)
    cos2, sin2 = turn(b[:, None] * q[None, :], NLON)
    cos3, sin3 = turn(q[:, None] * q[None, :], RUN)
    last = jnp.concatenate([cos3, -sin3], 1)

    chunk = chunk.reshape(parts, 2, items * count)
    chunk, table, cos2, sin2, last = lax.optimization_barrier((chunk, table, cos2, sin2, last))
    spread = lax.all_to_all(chunk, "ord", 0, 0, tiled=True).astype(jnp.float32)
    flat = jnp.concatenate([spread[:, 0], spread[:, 1]], 0)
    mid = jnp.dot(table, flat, precision=lax.Precision.HIGHEST).reshape(2, 128, items, count)
    cos2, sin2 = cos2[:, None, :], sin2[:, None, :]
    real = mid[0] * cos2 - mid[1] * sin2
    imag = mid[0] * sin2 + mid[1] * cos2
    field = lax.dot_general(
        last, jnp.concatenate([real, imag], 2),
        (((1,), (2,)), ((), ())), precision=lax.Precision.HIGHEST)
    field = field.reshape(parts, NLON // parts, items).astype(jnp.bfloat16)
    field = lax.all_to_all(field, "ord", 0, 0, tiled=True)
    field = field.reshape(cycles, 4, NLON // parts, 3, shells // 4)
    return jnp.transpose(field, (2, 0, 3, 1, 4)).reshape(NLON // parts, cycles * 3 * shells)


def solution(mesh):
    return jax.shard_map(
        body,
        mesh=mesh,
        in_specs=(P("ord", "blk", None), P(None, None, "ord", "blk"), P(), P(), P("blk")),
        out_specs=P("ord", "blk"),
        check_vma=False,
    )
```

```python
import functools
import math

import jax
import jax.numpy as jnp
from jax import lax
from jax.experimental import pallas as pl
from jax.experimental.pallas import tpu as pltpu
from jax.sharding import PartitionSpec as P

ORDERS = 2880
RUN = 45
QUARTER = 720
START = 1408
WIDE = 1536
KEPT = 1472
NLON = 5760
GROUP = 5
CHUNKS = (0, 25, 40, 45)
GAUSS_TAIL = 2 * GROUP * 640
GAUSS_LANES = GAUSS_TAIL + 896
PANEL_TAIL = GROUP * START
PANEL_LANES = PANEL_TAIL + 384
GAUSS_PAIRS = [(0, 1), (1, 0), (2, 3), (3, 2)]
PANEL_PAIRS = [(1, 2), (2, 1), (3, 0), (0, 3)]


def pack_kernel(spot_ref, gauss_ref, main_ref, tail_ref, *rest):
    gauss_out, panel_out = rest[-2:]
    for o in range(GROUP):
        for k in range(2):
            j = k * GROUP + o
            gauss_out[0, :, 640 * j:640 * (j + 1)] = gauss_ref[k, o, :, 0:640]
            gauss_out[0, :, GAUSS_TAIL + 80 * j:GAUSS_TAIL + 80 * (j + 1)] = gauss_ref[k, o, :, 640:720]
        panel_out[0, :, START * o:START * (o + 1)] = main_ref[o]
        panel_out[0, :, PANEL_TAIL + 64 * o:PANEL_TAIL + 64 * (o + 1)] = tail_ref[o, :, 0:64]


def panel_specs(skip, upper):
    return [
        pl.BlockSpec((GROUP, 16, START), lambda i, spot: (i + skip, 0, upper(spot[0]))),
        pl.BlockSpec((GROUP, 16, 128), lambda i, spot: (i + skip, 0, 11 + 11 * upper(spot[0]))),
    ]


def pack(spot, own, panel, after, base, count):
    skip = base // GROUP
    steps = count // GROUP
    return pl.pallas_call(
        pack_kernel,
        out_shape=[jax.ShapeDtypeStruct((steps, 16, GAUSS_LANES), jnp.bfloat16),
                   jax.ShapeDtypeStruct((steps, 16, PANEL_LANES), jnp.bfloat16)],
        grid_spec=pltpu.PrefetchScalarGridSpec(
            num_scalar_prefetch=1,
            grid=(steps,),
            in_specs=[pl.BlockSpec((2, GROUP, 16, QUARTER), lambda i, spot: (0, i + skip, 0, 0))]
            + panel_specs(skip, lambda blk: 1 - blk // 2)
            + [pl.BlockSpec(memory_space=pl.ANY)] * len(after),
            out_specs=[pl.BlockSpec((1, 16, GAUSS_LANES), lambda i, spot: (i, 0, 0)),
                       pl.BlockSpec((1, 16, PANEL_LANES), lambda i, spot: (i, 0, 0))],
        ),
        cost_estimate=pl.CostEstimate(flops=0, bytes_accessed=count * 200000, transcendentals=0),
        name="pack",
    )(spot, own, panel, panel, *after)


def sums_kernel(spot_ref, order_ref, height_ref, angle_ref, own_ref, other_ref, main_ref, tail_ref,
                far_ref, *rest, base):
    keep_ref, send_ref, gs_ref, gn_ref, decay_ref, table_ref, mate_ref = rest[-7:]
    step = pl.program_id(0)
    half = spot_ref[0] // 2
    odd = spot_ref[0] % 2 == 1
    first = (half * START).astype(jnp.float32)
    degree = lax.broadcasted_iota(jnp.int32, (1, WIDE), 1).astype(jnp.float32) + first

    @pl.when(step == 0)
    def _():
        gs_ref[...] = jnp.zeros_like(gs_ref)
        gn_ref[...] = jnp.zeros_like(gn_ref)
        table_ref[...] = jnp.zeros_like(table_ref)
        height = height_ref[...]
        here = jnp.exp(-(degree + 2.0) * height / ORDERS)
        decay_ref[0] = here
        decay_ref[1] = here * (degree + 1.0)
        decay_ref[2] = jnp.exp(-(degree + 3.0) * height / ORDERS)

    for o in range(GROUP):
        for k in range(2):
            j = k * GROUP + o
            mate_ref[k, o, :, 0:640] = other_ref[0, :, 640 * j:640 * (j + 1)]
            mate_ref[k, o, :, 640:720] = other_ref[0, :, GAUSS_TAIL + 80 * j:GAUSS_TAIL + 80 * (j + 1)]
        table_ref[o, 0:16, 0:START] = main_ref[o]
        table_ref[o, 0:16, START:KEPT] = tail_ref[o, :, 0:64]
        table_ref[o, 16:32, 0:START] = far_ref[0, :, START * o:START * (o + 1)]
        table_ref[o, 16:32, START:KEPT] = far_ref[0, :, PANEL_TAIL + 64 * o:PANEL_TAIL + 64 * (o + 1)]
    low = jnp.where(odd, mate_ref[...], own_ref[...])
    high = jnp.where(odd, own_ref[...], mate_ref[...])

    @pl.when(half == 0)
    def _():
        gs_ref[:, :, :, 0:720] = low
        gs_ref[:, :, :, 720:1440] = high
        gn_ref[:, :, :, 0:719] = low[:, :, :, 1:]
        gn_ref[:, :, :, 719:1439] = high

    @pl.when(half == 1)
    def _():
        gs_ref[:, :, :, 32:752] = low
        gs_ref[:, :, :, 752:1472] = high
        gn_ref[:, :, :, 31:751] = low
        gn_ref[:, :, :, 751:1471] = high

    cosine = angle_ref[:, 0:1]
    inverse = angle_ref[:, 1:2]
    lane = lax.broadcasted_iota(jnp.int32, (32, 128), 1)
    for o in range(GROUP):
        m = order_ref[base + step * GROUP + o].astype(jnp.float32)
        root = jnp.sqrt(jnp.maximum((degree + 1.0) * (degree + 1.0) - m * m, 0.0))
        slope = decay_ref[2] * root
        g = [gs_ref[k, o].astype(jnp.float32) for k in range(2)]
        n = [gn_ref[k, o].astype(jnp.float32) for k in range(2)]
        main = [(g[k] * decay_ref[1]).astype(jnp.bfloat16) for k in range(2)]
        bare = [(g[k] * decay_ref[0]).astype(jnp.bfloat16) for k in range(2)]
        tilt = [(n[k] * slope).astype(jnp.bfloat16) for k in range(2)]
        weights = jnp.concatenate(main + bare + [-bare[1], bare[0]] + tilt, 0)
        sums = lax.dot_general(
            table_ref[o], weights, (((1,), (1,)), ((), ())), preferred_element_type=jnp.float32)
        polar = (pltpu.roll(sums, 64, 1) - cosine * (pltpu.roll(sums, 32, 1) - sums)) * inverse
        mixed = jnp.where(lane < 32, sums, jnp.where(lane < 64, polar, m * inverse * sums))
        keep_ref[o] = mixed[:16, :96]
        send_ref[o] = mixed[16:, :96].astype(jnp.bfloat16)


def partial_sums(spot, orders, height, angles, own, other, panel, far, after, base, count):
    skip = base // GROUP
    smem = pl.BlockSpec(memory_space=pltpu.SMEM)
    out = pl.BlockSpec((GROUP, 16, 96), lambda i, spot: (i, 0, 0))
    return pl.pallas_call(
        functools.partial(sums_kernel, base=base),
        out_shape=[jax.ShapeDtypeStruct((count, 16, 96), jnp.float32),
                   jax.ShapeDtypeStruct((count, 16, 96), jnp.bfloat16)],
        grid_spec=pltpu.PrefetchScalarGridSpec(
            num_scalar_prefetch=1,
            grid=(count // GROUP,),
            in_specs=[
                smem, pl.BlockSpec((16, 1), lambda i, spot: (0, 0)),
                pl.BlockSpec((32, 2), lambda i, spot: (0, 0)),
                pl.BlockSpec((2, GROUP, 16, QUARTER), lambda i, spot: (0, i + skip, 0, 0)),
                pl.BlockSpec((1, 16, GAUSS_LANES), lambda i, spot: (i, 0, 0)),
            ] + panel_specs(skip, lambda blk: blk // 2)
            + [pl.BlockSpec((1, 16, PANEL_LANES), lambda i, spot: (i, 0, 0))]
            + [pl.BlockSpec(memory_space=pl.ANY)] * len(after),
            out_specs=[out, out],
            scratch_shapes=[
                pltpu.VMEM((2, GROUP, 16, WIDE), jnp.bfloat16),
                pltpu.VMEM((2, GROUP, 16, WIDE), jnp.bfloat16),
                pltpu.VMEM((3, 16, WIDE), jnp.float32),
                pltpu.VMEM((GROUP, 32, WIDE), jnp.bfloat16),
                pltpu.VMEM((2, GROUP, 16, QUARTER), jnp.bfloat16),
            ],
        ),
        compiler_params=pltpu.CompilerParams(vmem_limit_bytes=24 << 20),
        cost_estimate=pl.CostEstimate(
            flops=count * 32 * 128 * WIDE * 2, bytes_accessed=count * 200000, transcendentals=0),
        name="partial_sums",
    )(spot, orders, height, angles, own, other, panel, panel, far, *after)


def turn(phase, period):
    angle = (phase % period).astype(jnp.float32) * (2.0 * math.pi / period)
    return jnp.cos(angle), jnp.sin(angle)


def body(panel, gauss, height, order_map, cycle_map):
    count, cycles, _ = panel.shape
    shells = height.shape[0]
    here = lax.axis_index("ord")
    spot = lax.axis_index("blk").astype(jnp.int32).reshape(1)
    own = jnp.transpose(gauss, (0, 2, 1, 3))
    spans = list(zip(CHUNKS[:-1], CHUNKS[1:]))
    arrived, packed = [], ()
    for a, b in spans:
        packed = pack(spot, own, panel, packed[:1], a, b - a)
        arrived.append((lax.ppermute(packed[0], "blk", GAUSS_PAIRS),
                        lax.ppermute(packed[1], "blk", PANEL_PAIRS)))
    orders_int = lax.dynamic_slice_in_dim(order_map, here * count, count, 0)
    facing = lax.ppermute(cycle_map, "blk", PANEL_PAIRS)
    theta = math.pi * (jnp.concatenate([cycle_map, facing]).astype(jnp.float32) + 0.5) / ORDERS
    angles = jnp.stack([jnp.cos(theta), 1.0 / jnp.sin(theta)], 1)
    kept, added = [], []
    for c, ((a, b), (other, far)) in enumerate(zip(spans, arrived)):
        after = (kept[-1:] or [own]) + (added[c - 2:c - 1] if c >= 2 else [])
        keep, send = partial_sums(
            spot, orders_int, height[:, None], angles, own, other, panel, far, after, a, b - a)
        kept.append(keep)
        added.append(lax.ppermute(send, "blk", PANEL_PAIRS))
    total = jnp.concatenate(kept, 0) + jnp.concatenate(added, 0).astype(jnp.float32)
    total = lax.optimization_barrier(total.astype(jnp.bfloat16))
    split = (count, cycles, 3, 2, 4, shells // 4)
    chunk = jnp.transpose(total.reshape(split), (1, 4, 3, 2, 5, 0))

    parts = ORDERS // count
    items = cycles * 3 * shells // parts
    runs = order_map[::RUN] // RUN
    b = jnp.arange(128)
    q = jnp.arange(RUN)
    cos1, sin1 = turn(b[:, None] * runs[None, :], 128)
    table = jnp.concatenate(
        [jnp.concatenate([cos1, sin1], 1), jnp.concatenate([sin1, -cos1], 1)], 0)
    cos2, sin2 = turn(b[:, None] * q[None, :], NLON)
    cos3, sin3 = turn(q[:, None] * q[None, :], RUN)
    last = jnp.concatenate([cos3, -sin3], 1)

    chunk = chunk.reshape(parts, 2, items * count)
    chunk, table, cos2, sin2, last = lax.optimization_barrier((chunk, table, cos2, sin2, last))
    spread = lax.all_to_all(chunk, "ord", 0, 0, tiled=True).astype(jnp.float32)
    flat = jnp.concatenate([spread[:, 0], spread[:, 1]], 0)
    mid = jnp.dot(table, flat, precision=lax.Precision.HIGHEST).reshape(2, 128, items, count)
    cos2, sin2 = cos2[:, None, :], sin2[:, None, :]
    real = mid[0] * cos2 - mid[1] * sin2
    imag = mid[0] * sin2 + mid[1] * cos2
    field = lax.dot_general(
        last, jnp.concatenate([real, imag], 2),
        (((1,), (2,)), ((), ())), precision=lax.Precision.HIGHEST)
    field = field.reshape(parts, NLON // parts, items).astype(jnp.bfloat16)
    field = lax.all_to_all(field, "ord", 0, 0, tiled=True)
    field = field.reshape(cycles, 4, NLON // parts, 3, shells // 4)
    return jnp.transpose(field, (2, 0, 3, 1, 4)).reshape(NLON // parts, cycles * 3 * shells)


def solution(mesh):
    return jax.shard_map(
        body,
        mesh=mesh,
        in_specs=(P("ord", "blk", None), P(None, None, "ord", "blk"), P(), P(), P("blk")),
        out_specs=P("ord", "blk"),
        check_vma=False,
    )
```

```python
import functools
import math

import jax
import jax.numpy as jnp
from jax import lax
from jax.experimental import pallas as pl
from jax.experimental.pallas import tpu as pltpu
from jax.sharding import PartitionSpec as P

ORDERS = 2880
RUN = 45
QUARTER = 720
START = 1408
WIDE = 1536
KEPT = 1472
NLON = 5760
GROUP = 5
CHUNKS = (0, 15, 30, 40, 45)
GAUSS_TAIL = 2 * GROUP * 640
GAUSS_LANES = GAUSS_TAIL + 896
PANEL_TAIL = GROUP * START
PANEL_LANES = PANEL_TAIL + 384
CYCLE_LANE = PANEL_TAIL + 320
GAUSS_PAIRS = [(0, 1), (1, 0), (2, 3), (3, 2)]
PANEL_PAIRS = [(1, 2), (2, 1), (3, 0), (0, 3)]


def pack_kernel(spot_ref, cycle_ref, gauss_ref, main_ref, tail_ref, *rest):
    gauss_out, panel_out = rest[-2:]
    cycle = cycle_ref[...]
    digits = jnp.concatenate([cycle // 64, cycle % 64], 1)
    panel_out[0, :, CYCLE_LANE:CYCLE_LANE + 2] = digits.astype(jnp.float32).astype(jnp.bfloat16)
    for o in range(GROUP):
        for k in range(2):
            j = k * GROUP + o
            gauss_out[0, :, 640 * j:640 * (j + 1)] = gauss_ref[k, o, :, 0:640]
            gauss_out[0, :, GAUSS_TAIL + 80 * j:GAUSS_TAIL + 80 * (j + 1)] = gauss_ref[k, o, :, 640:720]
        panel_out[0, :, START * o:START * (o + 1)] = main_ref[o]
        panel_out[0, :, PANEL_TAIL + 64 * o:PANEL_TAIL + 64 * (o + 1)] = tail_ref[o, :, 0:64]


def panel_specs(skip, upper):
    return [
        pl.BlockSpec((GROUP, 16, START), lambda i, spot: (i + skip, 0, upper(spot[0]))),
        pl.BlockSpec((GROUP, 16, 128), lambda i, spot: (i + skip, 0, 11 + 11 * upper(spot[0]))),
    ]


def pack(spot, cycle, own, panel, after, base, count):
    skip = base // GROUP
    steps = count // GROUP
    return pl.pallas_call(
        pack_kernel,
        out_shape=[jax.ShapeDtypeStruct((steps, 16, GAUSS_LANES), jnp.bfloat16),
                   jax.ShapeDtypeStruct((steps, 16, PANEL_LANES), jnp.bfloat16)],
        grid_spec=pltpu.PrefetchScalarGridSpec(
            num_scalar_prefetch=1,
            grid=(steps,),
            in_specs=[pl.BlockSpec((16, 1), lambda i, spot: (0, 0)),
                      pl.BlockSpec((2, GROUP, 16, QUARTER), lambda i, spot: (0, i + skip, 0, 0))]
            + panel_specs(skip, lambda blk: 1 - blk // 2)
            + [pl.BlockSpec(memory_space=pl.ANY)] * len(after),
            out_specs=[pl.BlockSpec((1, 16, GAUSS_LANES), lambda i, spot: (i, 0, 0)),
                       pl.BlockSpec((1, 16, PANEL_LANES), lambda i, spot: (i, 0, 0))],
        ),
        cost_estimate=pl.CostEstimate(flops=0, bytes_accessed=count * 200000, transcendentals=0),
        name="pack",
    )(spot, cycle, own, panel, panel, *after)


def sums_kernel(spot_ref, order_ref, height_ref, cycle_ref, own_ref, other_ref, main_ref, tail_ref,
                far_ref, *rest, base):
    keep_ref, send_ref, gs_ref, gn_ref, decay_ref, table_ref, mate_ref, angle_ref = rest[-8:]
    step = pl.program_id(0)
    half = spot_ref[0] // 2
    odd = spot_ref[0] % 2 == 1
    first = (half * START).astype(jnp.float32)
    degree = lax.broadcasted_iota(jnp.int32, (1, WIDE), 1).astype(jnp.float32) + first

    @pl.when(step == 0)
    def _():
        gs_ref[...] = jnp.zeros_like(gs_ref)
        gn_ref[...] = jnp.zeros_like(gn_ref)
        table_ref[...] = jnp.zeros_like(table_ref)
        height = height_ref[...]
        here = jnp.exp(-(degree + 2.0) * height / ORDERS)
        decay_ref[0] = here
        decay_ref[1] = here * (degree + 1.0)
        decay_ref[2] = jnp.exp(-(degree + 3.0) * height / ORDERS)
        digits = far_ref[0, :, CYCLE_LANE:CYCLE_LANE + 2].astype(jnp.float32)
        mates = digits[:, 0:1] * 64.0 + digits[:, 1:2]
        cycles = jnp.concatenate([cycle_ref[...].astype(jnp.float32), mates], 0)
        cycles = jnp.broadcast_to(cycles, (32, 128)).T[0:8, :]
        theta = math.pi * (cycles + 0.5) / ORDERS
        angle_ref[0] = jnp.cos(theta)
        angle_ref[1] = 1.0 / jnp.sin(theta)

    for o in range(GROUP):
        for k in range(2):
            j = k * GROUP + o
            mate_ref[k, o, :, 0:640] = other_ref[0, :, 640 * j:640 * (j + 1)]
            mate_ref[k, o, :, 640:720] = other_ref[0, :, GAUSS_TAIL + 80 * j:GAUSS_TAIL + 80 * (j + 1)]
        table_ref[o, 0:16, 0:START] = main_ref[o]
        table_ref[o, 0:16, START:KEPT] = tail_ref[o, :, 0:64]
        table_ref[o, 16:32, 0:START] = far_ref[0, :, START * o:START * (o + 1)]
        table_ref[o, 16:32, START:KEPT] = far_ref[0, :, PANEL_TAIL + 64 * o:PANEL_TAIL + 64 * (o + 1)]
    low = jnp.where(odd, mate_ref[...], own_ref[...])
    high = jnp.where(odd, own_ref[...], mate_ref[...])

    @pl.when(half == 0)
    def _():
        gs_ref[:, :, :, 0:720] = low
        gs_ref[:, :, :, 720:1440] = high
        gn_ref[:, :, :, 0:719] = low[:, :, :, 1:]
        gn_ref[:, :, :, 719:1439] = high

    @pl.when(half == 1)
    def _():
        gs_ref[:, :, :, 32:752] = low
        gs_ref[:, :, :, 752:1472] = high
        gn_ref[:, :, :, 31:751] = low
        gn_ref[:, :, :, 751:1471] = high

    cosine = angle_ref[0, 0:1]
    inverse = angle_ref[1, 0:1]
    orders = [order_ref[base + step * GROUP + o].astype(jnp.float32) for o in range(GROUP)]
    sums = []
    for o in range(GROUP):
        gap = jnp.maximum((degree + 1.0) * (degree + 1.0) - orders[o] * orders[o], 0.0)
        slope = decay_ref[2] * jnp.sqrt(gap)
        g = [gs_ref[k, o].astype(jnp.float32) for k in range(2)]
        n = [gn_ref[k, o].astype(jnp.float32) for k in range(2)]
        weights = jnp.concatenate(
            [g[0] * decay_ref[1], g[1] * decay_ref[1], g[0] * decay_ref[0], g[1] * decay_ref[0],
             n[0] * slope, n[1] * slope], 0).astype(jnp.bfloat16)
        sums.append(lax.dot_general(
            weights, table_ref[o], (((1,), (1,)), ((), ())), preferred_element_type=jnp.float32))
    mixed = []
    for o in range(GROUP):
        main, bare, tilt = sums[o][0:32], sums[o][32:64], sums[o][64:96]
        polar = (tilt - cosine * (main - bare)) * inverse
        bare = orders[o] * inverse * bare
        mixed.append(jnp.concatenate([main, polar, -bare[16:32], bare[0:16]], 0).T)
    for o in range(GROUP):
        keep_ref[o] = mixed[o][:16]
        send_ref[o] = mixed[o][16:].astype(jnp.bfloat16)


def partial_sums(spot, orders, height, cycle, own, other, panel, far, after, base, count):
    skip = base // GROUP
    smem = pl.BlockSpec(memory_space=pltpu.SMEM)
    out = pl.BlockSpec((GROUP, 16, 96), lambda i, spot: (i, 0, 0))
    return pl.pallas_call(
        functools.partial(sums_kernel, base=base),
        out_shape=[jax.ShapeDtypeStruct((count, 16, 96), jnp.float32),
                   jax.ShapeDtypeStruct((count, 16, 96), jnp.bfloat16)],
        grid_spec=pltpu.PrefetchScalarGridSpec(
            num_scalar_prefetch=1,
            grid=(count // GROUP,),
            in_specs=[
                smem, pl.BlockSpec((16, 1), lambda i, spot: (0, 0)),
                pl.BlockSpec((16, 1), lambda i, spot: (0, 0)),
                pl.BlockSpec((2, GROUP, 16, QUARTER), lambda i, spot: (0, i + skip, 0, 0)),
                pl.BlockSpec((1, 16, GAUSS_LANES), lambda i, spot: (i, 0, 0)),
            ] + panel_specs(skip, lambda blk: blk // 2)
            + [pl.BlockSpec((1, 16, PANEL_LANES), lambda i, spot: (i, 0, 0))]
            + [pl.BlockSpec(memory_space=pl.ANY)] * len(after),
            out_specs=[out, out],
            scratch_shapes=[
                pltpu.VMEM((2, GROUP, 16, WIDE), jnp.bfloat16),
                pltpu.VMEM((2, GROUP, 16, WIDE), jnp.bfloat16),
                pltpu.VMEM((3, 16, WIDE), jnp.float32),
                pltpu.VMEM((GROUP, 32, WIDE), jnp.bfloat16),
                pltpu.VMEM((2, GROUP, 16, QUARTER), jnp.bfloat16),
                pltpu.VMEM((2, 8, 32), jnp.float32),
            ],
        ),
        compiler_params=pltpu.CompilerParams(vmem_limit_bytes=24 << 20),
        cost_estimate=pl.CostEstimate(
            flops=count * 32 * 128 * WIDE * 2, bytes_accessed=count * 200000, transcendentals=0),
        name="partial_sums",
    )(spot, orders, height, cycle, own, other, panel, panel, far, *after)


def turn(phase, period):
    angle = (phase % period).astype(jnp.float32) * (2.0 * math.pi / period)
    return jnp.cos(angle), jnp.sin(angle)


def body(panel, gauss, height, order_map, cycle_map):
    count, cycles, _ = panel.shape
    shells = height.shape[0]
    here = lax.axis_index("ord")
    spot = lax.axis_index("blk").astype(jnp.int32).reshape(1)
    cycle = cycle_map[:, None]
    own = jnp.transpose(gauss, (0, 2, 1, 3))
    spans = list(zip(CHUNKS[:-1], CHUNKS[1:]))
    arrived, packed = [], ()
    for a, b in spans:
        packed = pack(spot, cycle, own, panel, packed[:1], a, b - a)
        arrived.append((lax.ppermute(packed[0], "blk", GAUSS_PAIRS),
                        lax.ppermute(packed[1], "blk", PANEL_PAIRS)))
    orders_int = lax.dynamic_slice_in_dim(order_map, here * count, count, 0)
    kept, added = [], []
    for c, ((a, b), (other, far)) in enumerate(zip(spans, arrived)):
        after = (kept[-1:] or [own]) + (added[c - 2:c - 1] if c >= 2 else [])
        keep, send = partial_sums(
            spot, orders_int, height[:, None], cycle, own, other, panel, far, after, a, b - a)
        kept.append(keep)
        added.append(lax.ppermute(send, "blk", PANEL_PAIRS))
    total = jnp.concatenate(kept, 0) + jnp.concatenate(added, 0).astype(jnp.float32)
    total = lax.optimization_barrier(total.astype(jnp.bfloat16))
    split = (count, cycles, 3, 2, 4, shells // 4)
    chunk = jnp.transpose(total.reshape(split), (1, 4, 3, 2, 5, 0))

    parts = ORDERS // count
    items = cycles * 3 * shells // parts
    runs = order_map[::RUN] // RUN
    b = jnp.arange(128)
    q = jnp.arange(RUN)
    cos1, sin1 = turn(b[:, None] * runs[None, :], 128)
    table = jnp.concatenate(
        [jnp.concatenate([cos1, sin1], 1), jnp.concatenate([sin1, -cos1], 1)], 0)
    cos2, sin2 = turn(b[:, None] * q[None, :], NLON)
    cos3, sin3 = turn(q[:, None] * q[None, :], RUN)
    last = jnp.concatenate([cos3, -sin3], 1)

    chunk = chunk.reshape(parts, 2, items * count)
    chunk, table, cos2, sin2, last = lax.optimization_barrier((chunk, table, cos2, sin2, last))
    spread = lax.all_to_all(chunk, "ord", 0, 0, tiled=True).astype(jnp.float32)
    flat = jnp.concatenate([spread[:, 0], spread[:, 1]], 0)
    mid = jnp.dot(table, flat, precision=lax.Precision.HIGHEST).reshape(2, 128, items, count)
    cos2, sin2 = cos2[:, None, :], sin2[:, None, :]
    real = mid[0] * cos2 - mid[1] * sin2
    imag = mid[0] * sin2 + mid[1] * cos2
    field = lax.dot_general(
        last, jnp.concatenate([real, imag], 2),
        (((1,), (2,)), ((), ())), precision=lax.Precision.HIGHEST)
    field = field.reshape(parts, NLON // parts, items).astype(jnp.bfloat16)
    field = lax.all_to_all(field, "ord", 0, 0, tiled=True)
    field = field.reshape(cycles, 4, NLON // parts, 3, shells // 4)
    return jnp.transpose(field, (2, 0, 3, 1, 4)).reshape(NLON // parts, cycles * 3 * shells)


def solution(mesh):
    return jax.shard_map(
        body,
        mesh=mesh,
        in_specs=(P("ord", "blk", None), P(None, None, "ord", "blk"), P(), P(), P("blk")),
        out_specs=P("ord", "blk"),
        check_vma=False,
    )
```

```python
import functools
import math

import jax
import jax.numpy as jnp
from jax import lax
from jax.experimental import pallas as pl
from jax.experimental.pallas import tpu as pltpu
from jax.sharding import PartitionSpec as P

ORDERS = 2880
RUN = 45
QUARTER = 720
START = 1408
WIDE = 1536
KEPT = 1472
NLON = 5760
GROUP = 5
CHUNKS = (0, 15, 30, 40, 45)
GAUSS_TAIL = 2 * GROUP * 640
GAUSS_LANES = GAUSS_TAIL + 896
PANEL_TAIL = GROUP * START
PANEL_LANES = PANEL_TAIL + 384
CYCLE_LANE = PANEL_TAIL + 320
GAUSS_PAIRS = [(0, 1), (1, 0), (2, 3), (3, 2)]
PANEL_PAIRS = [(1, 2), (2, 1), (3, 0), (0, 3)]


def pack_kernel(spot_ref, cycle_ref, gauss_ref, main_ref, tail_ref, *rest):
    gauss_out, panel_out = rest[-2:]
    row = lax.broadcasted_iota(jnp.int32, (16, 2), 0)
    column = lax.broadcasted_iota(jnp.int32, (16, 2), 1)
    digits = jnp.zeros((16, 2), jnp.int32)
    for i in range(16):
        value = jnp.where(column == 0, cycle_ref[i] // 64, cycle_ref[i] % 64)
        digits = jnp.where(row == i, value, digits)
    panel_out[0, :, CYCLE_LANE:CYCLE_LANE + 2] = digits.astype(jnp.float32).astype(jnp.bfloat16)
    for o in range(GROUP):
        for k in range(2):
            j = k * GROUP + o
            gauss_out[0, :, 640 * j:640 * (j + 1)] = gauss_ref[k, o, :, 0:640]
            gauss_out[0, :, GAUSS_TAIL + 80 * j:GAUSS_TAIL + 80 * (j + 1)] = gauss_ref[k, o, :, 640:720]
        panel_out[0, :, START * o:START * (o + 1)] = main_ref[o]
        panel_out[0, :, PANEL_TAIL + 64 * o:PANEL_TAIL + 64 * (o + 1)] = tail_ref[o, :, 0:64]


def panel_specs(skip, upper):
    return [
        pl.BlockSpec((GROUP, 16, START), lambda i, spot: (i + skip, 0, upper(spot[0]))),
        pl.BlockSpec((GROUP, 16, 128), lambda i, spot: (i + skip, 0, 11 + 11 * upper(spot[0]))),
    ]


def pack(spot, cycle, own, panel, after, base, count):
    skip = base // GROUP
    steps = count // GROUP
    return pl.pallas_call(
        pack_kernel,
        out_shape=[jax.ShapeDtypeStruct((steps, 16, GAUSS_LANES), jnp.bfloat16),
                   jax.ShapeDtypeStruct((steps, 16, PANEL_LANES), jnp.bfloat16)],
        grid_spec=pltpu.PrefetchScalarGridSpec(
            num_scalar_prefetch=1,
            grid=(steps,),
            in_specs=[pl.BlockSpec(memory_space=pltpu.SMEM),
                      pl.BlockSpec((2, GROUP, 16, QUARTER), lambda i, spot: (0, i + skip, 0, 0))]
            + panel_specs(skip, lambda blk: 1 - blk // 2)
            + [pl.BlockSpec(memory_space=pl.ANY)] * len(after),
            out_specs=[pl.BlockSpec((1, 16, GAUSS_LANES), lambda i, spot: (i, 0, 0)),
                       pl.BlockSpec((1, 16, PANEL_LANES), lambda i, spot: (i, 0, 0))],
        ),
        compiler_params=pltpu.CompilerParams(vmem_limit_bytes=10 << 20),
        cost_estimate=pl.CostEstimate(flops=0, bytes_accessed=count * 200000, transcendentals=0),
        name="pack",
    )(spot, cycle, own, panel, panel, *after)


def sums_kernel(spot_ref, order_ref, height_ref, cycle_ref, own_ref, other_ref, main_ref, tail_ref,
                far_ref, *rest, base):
    keep_ref, send_ref, gs_ref, gn_ref, decay_ref, table_ref, mate_ref, angle_ref = rest[-8:]
    step = pl.program_id(0)
    half = spot_ref[0] // 2
    odd = spot_ref[0] % 2 == 1
    first = (half * START).astype(jnp.float32)
    degree = lax.broadcasted_iota(jnp.int32, (1, WIDE), 1).astype(jnp.float32) + first

    @pl.when(step == 0)
    def _():
        gs_ref[...] = jnp.zeros_like(gs_ref)
        gn_ref[...] = jnp.zeros_like(gn_ref)
        table_ref[...] = jnp.zeros_like(table_ref)
        height = height_ref[...]
        here = jnp.exp(-(degree + 2.0) * height / ORDERS)
        decay_ref[0] = here
        decay_ref[1] = here * (degree + 1.0)
        decay_ref[2] = jnp.exp(-(degree + 3.0) * height / ORDERS)
        digits = far_ref[0, :, CYCLE_LANE:CYCLE_LANE + 2].astype(jnp.float32)
        mates = digits[:, 0:1] * 64.0 + digits[:, 1:2]
        cycles = jnp.broadcast_to(mates, (16, 128)).T[0:8, :]
        cycles = jnp.concatenate([jnp.zeros((8, 16), jnp.float32), cycles], 1)
        lane = lax.broadcasted_iota(jnp.int32, (8, 32), 1)
        for i in range(16):
            cycles = jnp.where(lane == i, cycle_ref[i].astype(jnp.float32), cycles)
        theta = math.pi * (cycles + 0.5) / ORDERS
        angle_ref[0] = jnp.cos(theta)
        angle_ref[1] = 1.0 / jnp.sin(theta)

    for o in range(GROUP):
        for k in range(2):
            j = k * GROUP + o
            mate_ref[k, o, :, 0:640] = other_ref[0, :, 640 * j:640 * (j + 1)]
            mate_ref[k, o, :, 640:720] = other_ref[0, :, GAUSS_TAIL + 80 * j:GAUSS_TAIL + 80 * (j + 1)]
        table_ref[o, 0:16, 0:START] = main_ref[o]
        table_ref[o, 0:16, START:KEPT] = tail_ref[o, :, 0:64]
        table_ref[o, 16:32, 0:START] = far_ref[0, :, START * o:START * (o + 1)]
        table_ref[o, 16:32, START:KEPT] = far_ref[0, :, PANEL_TAIL + 64 * o:PANEL_TAIL + 64 * (o + 1)]
    low = jnp.where(odd, mate_ref[...], own_ref[...])
    high = jnp.where(odd, own_ref[...], mate_ref[...])

    @pl.when(half == 0)
    def _():
        gs_ref[:, :, :, 0:720] = low
        gs_ref[:, :, :, 720:1440] = high
        gn_ref[:, :, :, 0:719] = low[:, :, :, 1:]
        gn_ref[:, :, :, 719:1439] = high

    @pl.when(half == 1)
    def _():
        gs_ref[:, :, :, 32:752] = low
        gs_ref[:, :, :, 752:1472] = high
        gn_ref[:, :, :, 31:751] = low
        gn_ref[:, :, :, 751:1471] = high

    cosine = angle_ref[0, 0:1]
    inverse = angle_ref[1, 0:1]
    orders = [order_ref[base + step * GROUP + o].astype(jnp.float32) for o in range(GROUP)]
    sums = []
    for o in range(GROUP):
        gap = jnp.maximum((degree + 1.0) * (degree + 1.0) - orders[o] * orders[o], 0.0)
        slope = decay_ref[2] * jnp.sqrt(gap)
        g = [gs_ref[k, o].astype(jnp.float32) for k in range(2)]
        n = [gn_ref[k, o].astype(jnp.float32) for k in range(2)]
        weights = jnp.concatenate(
            [g[0] * decay_ref[1], g[1] * decay_ref[1], g[0] * decay_ref[0], g[1] * decay_ref[0],
             n[0] * slope, n[1] * slope], 0).astype(jnp.bfloat16)
        sums.append(lax.dot_general(
            weights, table_ref[o], (((1,), (1,)), ((), ())), preferred_element_type=jnp.float32))
    mixed = []
    for o in range(GROUP):
        main, bare, tilt = sums[o][0:32], sums[o][32:64], sums[o][64:96]
        polar = (tilt - cosine * (main - bare)) * inverse
        bare = orders[o] * inverse * bare
        mixed.append(jnp.concatenate([main, polar, -bare[16:32], bare[0:16]], 0).T)
    for o in range(GROUP):
        keep_ref[o] = mixed[o][:16]
        send_ref[o] = mixed[o][16:].astype(jnp.bfloat16)


def partial_sums(spot, orders, height, cycle, own, other, panel, far, after, base, count, size, begun):
    skip = base // GROUP
    into = begun[0].shape[0] // GROUP - count // GROUP if begun else 0
    total = begun[0].shape[0] if begun else size
    smem = pl.BlockSpec(memory_space=pltpu.SMEM)
    out = pl.BlockSpec((GROUP, 16, 96), lambda i, spot: (i + into, 0, 0))
    return pl.pallas_call(
        functools.partial(sums_kernel, base=base),
        out_shape=[jax.ShapeDtypeStruct((total, 16, 96), jnp.float32),
                   jax.ShapeDtypeStruct((total, 16, 96), jnp.bfloat16)],
        input_output_aliases={9: 0, 10: 1} if begun else {},
        grid_spec=pltpu.PrefetchScalarGridSpec(
            num_scalar_prefetch=1,
            grid=(count // GROUP,),
            in_specs=[
                smem, pl.BlockSpec((16, 1), lambda i, spot: (0, 0)), smem,
                pl.BlockSpec((2, GROUP, 16, QUARTER), lambda i, spot: (0, i + skip, 0, 0)),
                pl.BlockSpec((1, 16, GAUSS_LANES), lambda i, spot: (i, 0, 0)),
            ] + panel_specs(skip, lambda blk: blk // 2)
            + [pl.BlockSpec((1, 16, PANEL_LANES), lambda i, spot: (i, 0, 0))]
            + [pl.BlockSpec(memory_space=pl.ANY)] * (len(begun) + len(after)),
            out_specs=[out, out],
            scratch_shapes=[
                pltpu.VMEM((2, GROUP, 16, WIDE), jnp.bfloat16),
                pltpu.VMEM((2, GROUP, 16, WIDE), jnp.bfloat16),
                pltpu.VMEM((3, 16, WIDE), jnp.float32),
                pltpu.VMEM((GROUP, 32, WIDE), jnp.bfloat16),
                pltpu.VMEM((2, GROUP, 16, QUARTER), jnp.bfloat16),
                pltpu.VMEM((2, 8, 32), jnp.float32),
            ],
        ),
        compiler_params=pltpu.CompilerParams(vmem_limit_bytes=16 << 20),
        cost_estimate=pl.CostEstimate(
            flops=count * 32 * 128 * WIDE * 2, bytes_accessed=count * 200000, transcendentals=0),
        name="partial_sums",
    )(spot, orders, height, cycle, own, other, panel, panel, far, *begun, *after)


def turn(phase, period):
    angle = (phase % period).astype(jnp.float32) * (2.0 * math.pi / period)
    return jnp.cos(angle), jnp.sin(angle)


def body(panel, gauss, height, order_map, cycle_map):
    count, cycles, _ = panel.shape
    shells = height.shape[0]
    here = lax.axis_index("ord")
    spot = lax.axis_index("blk").astype(jnp.int32).reshape(1)
    own = jnp.transpose(gauss, (0, 2, 1, 3))
    own = pltpu.with_memory_space_constraint(own, pltpu.HBM)
    panel = pltpu.with_memory_space_constraint(panel, pltpu.HBM)
    spans = list(zip(CHUNKS[:-1], CHUNKS[1:]))
    orders_int = lax.dynamic_slice_in_dim(order_map, here * count, count, 0)
    packed, kept, sent, added = [], [], [], []

    def start(c):
        a, b = spans[c]
        after = [[], [], kept[0:1], kept[1:2]][c] + ([packed[-1][2]] if packed else [])
        coef, part = pack(spot, cycle_map, own, panel, after, a, b - a)
        packed.append((lax.ppermute(coef, "blk", GAUSS_PAIRS),
                       lax.ppermute(part, "blk", PANEL_PAIRS), coef))

    start(0)
    start(1)
    for c, (a, b) in enumerate(spans):
        begun = [kept.pop(), sent.pop()] if c == 3 else []
        size = CHUNKS[4] - CHUNKS[2] if c == 2 else b - a
        after = kept[-1:] + (added[c - 2:c - 1] if c >= 2 else [])
        keep, send = partial_sums(
            spot, orders_int, height[:, None], cycle_map, own, packed[c][0], panel, packed[c][1],
            after, a, b - a, size, begun)
        kept.append(keep)
        sent.append(send)
        if c != 2:
            added.append(lax.ppermute(send, "blk", PANEL_PAIRS))
        if c < 2:
            start(c + 2)
    total = jnp.concatenate(kept, 0) + jnp.concatenate(added, 0).astype(jnp.float32)
    total = lax.optimization_barrier(total.astype(jnp.bfloat16))
    split = (count, cycles, 3, 2, 4, shells // 4)
    chunk = jnp.transpose(total.reshape(split), (1, 4, 3, 2, 5, 0))

    parts = ORDERS // count
    items = cycles * 3 * shells // parts
    runs = order_map[::RUN] // RUN
    b = jnp.arange(128)
    q = jnp.arange(RUN)
    cos1, sin1 = turn(b[:, None] * runs[None, :], 128)
    table = jnp.concatenate(
        [jnp.concatenate([cos1, sin1], 1), jnp.concatenate([sin1, -cos1], 1)], 0)
    cos2, sin2 = turn(b[:, None] * q[None, :], NLON)
    cos3, sin3 = turn(q[:, None] * q[None, :], RUN)
    last = jnp.concatenate([cos3, -sin3], 1)

    chunk = chunk.reshape(parts, 2, items * count)
    chunk, table, cos2, sin2, last = lax.optimization_barrier((chunk, table, cos2, sin2, last))
    spread = lax.all_to_all(chunk, "ord", 0, 0, tiled=True).astype(jnp.float32)
    flat = jnp.concatenate([spread[:, 0], spread[:, 1]], 0)
    mid = jnp.dot(table, flat, precision=lax.Precision.HIGHEST).reshape(2, 128, items, count)
    cos2, sin2 = cos2[:, None, :], sin2[:, None, :]
    real = mid[0] * cos2 - mid[1] * sin2
    imag = mid[0] * sin2 + mid[1] * cos2
    field = lax.dot_general(
        last, jnp.concatenate([real, imag], 2),
        (((1,), (2,)), ((), ())), precision=lax.Precision.HIGHEST)
    field = field.reshape(parts, NLON // parts, items).astype(jnp.bfloat16)
    field = lax.all_to_all(field, "ord", 0, 0, tiled=True)
    field = field.reshape(cycles, 4, NLON // parts, 3, shells // 4)
    return jnp.transpose(field, (2, 0, 3, 1, 4)).reshape(NLON // parts, cycles * 3 * shells)


def solution(mesh):
    return jax.shard_map(
        body,
        mesh=mesh,
        in_specs=(P("ord", "blk", None), P(None, None, "ord", "blk"), P(), P(), P("blk")),
        out_specs=P("ord", "blk"),
        check_vma=False,
    )
```

```python
import functools
import math

import jax
import jax.numpy as jnp
from jax import lax
from jax.experimental import pallas as pl
from jax.experimental.pallas import tpu as pltpu
from jax.sharding import PartitionSpec as P

ORDERS = 2880
RUN = 45
QUARTER = 720
START = 1408
WIDE = 1536
KEPT = 1472
NLON = 5760
GROUP = 5
CHUNKS = (0, 15, 30, 40, 45)
GAUSS_TAIL = 2 * GROUP * 640
GAUSS_LANES = GAUSS_TAIL + 896
PANEL_TAIL = GROUP * START
PANEL_LANES = PANEL_TAIL + 384
CYCLE_LANE = PANEL_TAIL + 320
GAUSS_PAIRS = [(0, 1), (1, 0), (2, 3), (3, 2)]
PANEL_PAIRS = [(1, 2), (2, 1), (3, 0), (0, 3)]


def pack_panel(spot_ref, cycle_ref, main_ref, tail_ref, *rest):
    out_ref = rest[-1]
    row = lax.broadcasted_iota(jnp.int32, (16, 2), 0)
    column = lax.broadcasted_iota(jnp.int32, (16, 2), 1)
    digits = jnp.zeros((16, 2), jnp.int32)
    for i in range(16):
        value = jnp.where(column == 0, cycle_ref[i] // 64, cycle_ref[i] % 64)
        digits = jnp.where(row == i, value, digits)
    out_ref[0, :, CYCLE_LANE:CYCLE_LANE + 2] = digits.astype(jnp.float32).astype(jnp.bfloat16)
    for o in range(GROUP):
        out_ref[0, :, START * o:START * (o + 1)] = main_ref[o]
        out_ref[0, :, PANEL_TAIL + 64 * o:PANEL_TAIL + 64 * (o + 1)] = tail_ref[o, :, 0:64]


def pack_gauss(gauss_ref, *rest):
    out_ref = rest[-1]
    for o in range(GROUP):
        for k in range(2):
            j = k * GROUP + o
            out_ref[0, :, 640 * j:640 * (j + 1)] = gauss_ref[k, o, :, 0:640]
            out_ref[0, :, GAUSS_TAIL + 80 * j:GAUSS_TAIL + 80 * (j + 1)] = gauss_ref[k, o, :, 640:720]


def panel_specs(skip, upper):
    return [
        pl.BlockSpec((GROUP, 16, START), lambda i, spot: (i + skip, 0, upper(spot[0]))),
        pl.BlockSpec((GROUP, 16, 128), lambda i, spot: (i + skip, 0, 11 + 11 * upper(spot[0]))),
    ]


def packed_panel(spot, cycle, panel, after, base, count):
    steps = count // GROUP
    return pl.pallas_call(
        pack_panel,
        out_shape=jax.ShapeDtypeStruct((steps, 16, PANEL_LANES), jnp.bfloat16),
        grid_spec=pltpu.PrefetchScalarGridSpec(
            num_scalar_prefetch=1,
            grid=(steps,),
            in_specs=[pl.BlockSpec(memory_space=pltpu.SMEM)]
            + panel_specs(base // GROUP, lambda blk: 1 - blk // 2)
            + [pl.BlockSpec(memory_space=pl.ANY)] * len(after),
            out_specs=pl.BlockSpec((1, 16, PANEL_LANES), lambda i, spot: (i, 0, 0)),
        ),
        compiler_params=pltpu.CompilerParams(vmem_limit_bytes=10 << 20),
        cost_estimate=pl.CostEstimate(flops=0, bytes_accessed=count * 100000, transcendentals=0),
        name="pack_panel",
    )(spot, cycle, panel, panel, *after)


def packed_gauss(own, after, base, count):
    steps, skip = count // GROUP, base // GROUP
    return pl.pallas_call(
        pack_gauss,
        out_shape=jax.ShapeDtypeStruct((steps, 16, GAUSS_LANES), jnp.bfloat16),
        grid=(steps,),
        in_specs=[pl.BlockSpec((2, GROUP, 16, QUARTER), lambda i: (0, i + skip, 0, 0))]
        + [pl.BlockSpec(memory_space=pl.ANY)] * len(after),
        out_specs=pl.BlockSpec((1, 16, GAUSS_LANES), lambda i: (i, 0, 0)),
        compiler_params=pltpu.CompilerParams(vmem_limit_bytes=10 << 20),
        cost_estimate=pl.CostEstimate(flops=0, bytes_accessed=count * 100000, transcendentals=0),
        name="pack_gauss",
    )(own, *after)


def sums_kernel(spot_ref, order_ref, decay_ref, cycle_ref, own_ref, other_ref, main_ref, tail_ref,
                far_ref, *rest, base):
    keep_ref, send_ref, gs_ref, gn_ref, table_ref, mate_ref, angle_ref = rest[-7:]
    step = pl.program_id(0)
    half = spot_ref[0] // 2
    odd = spot_ref[0] % 2 == 1
    first = (half * START).astype(jnp.float32)
    degree = lax.broadcasted_iota(jnp.int32, (1, WIDE), 1).astype(jnp.float32) + first

    @pl.when(step == 0)
    def _():
        gs_ref[...] = jnp.zeros_like(gs_ref)
        gn_ref[...] = jnp.zeros_like(gn_ref)
        table_ref[...] = jnp.zeros_like(table_ref)
        digits = far_ref[0, :, CYCLE_LANE:CYCLE_LANE + 2].astype(jnp.float32)
        mates = digits[:, 0:1] * 64.0 + digits[:, 1:2]
        cycles = jnp.broadcast_to(mates, (16, 128)).T[0:8, :]
        cycles = jnp.concatenate([jnp.zeros((8, 16), jnp.float32), cycles], 1)
        lane = lax.broadcasted_iota(jnp.int32, (8, 32), 1)
        for i in range(16):
            cycles = jnp.where(lane == i, cycle_ref[i].astype(jnp.float32), cycles)
        theta = math.pi * (cycles + 0.5) / ORDERS
        angle_ref[0] = jnp.cos(theta)
        angle_ref[1] = 1.0 / jnp.sin(theta)

    for o in range(GROUP):
        for k in range(2):
            j = k * GROUP + o
            mate_ref[k, o, :, 0:640] = other_ref[0, :, 640 * j:640 * (j + 1)]
            mate_ref[k, o, :, 640:720] = other_ref[0, :, GAUSS_TAIL + 80 * j:GAUSS_TAIL + 80 * (j + 1)]
        table_ref[o, 0:16, 0:START] = main_ref[o]
        table_ref[o, 0:16, START:KEPT] = tail_ref[o, :, 0:64]
        table_ref[o, 16:32, 0:START] = far_ref[0, :, START * o:START * (o + 1)]
        table_ref[o, 16:32, START:KEPT] = far_ref[0, :, PANEL_TAIL + 64 * o:PANEL_TAIL + 64 * (o + 1)]
    low = jnp.where(odd, mate_ref[...], own_ref[...])
    high = jnp.where(odd, own_ref[...], mate_ref[...])

    @pl.when(half == 0)
    def _():
        gs_ref[:, :, :, 0:720] = low
        gs_ref[:, :, :, 720:1440] = high
        gn_ref[:, :, :, 0:719] = low[:, :, :, 1:]
        gn_ref[:, :, :, 719:1439] = high

    @pl.when(half == 1)
    def _():
        gs_ref[:, :, :, 32:752] = low
        gs_ref[:, :, :, 752:1472] = high
        gn_ref[:, :, :, 31:751] = low
        gn_ref[:, :, :, 751:1471] = high

    cosine = angle_ref[0, 0:1]
    inverse = angle_ref[1, 0:1]
    orders = [order_ref[base + step * GROUP + o].astype(jnp.float32) for o in range(GROUP)]
    sums = []
    for o in range(GROUP):
        gap = jnp.maximum((degree + 1.0) * (degree + 1.0) - orders[o] * orders[o], 0.0)
        slope = decay_ref[2] * jnp.sqrt(gap)
        g = [gs_ref[k, o].astype(jnp.float32) for k in range(2)]
        n = [gn_ref[k, o].astype(jnp.float32) for k in range(2)]
        weights = jnp.concatenate(
            [g[0] * decay_ref[1], g[1] * decay_ref[1], g[0] * decay_ref[0], g[1] * decay_ref[0],
             n[0] * slope, n[1] * slope], 0).astype(jnp.bfloat16)
        sums.append(lax.dot_general(
            weights, table_ref[o], (((1,), (1,)), ((), ())), preferred_element_type=jnp.float32))
    mixed = []
    for o in range(GROUP):
        main, bare, tilt = sums[o][0:32], sums[o][32:64], sums[o][64:96]
        polar = (tilt - cosine * (main - bare)) * inverse
        bare = orders[o] * inverse * bare
        mixed.append(jnp.concatenate([main, polar, -bare[16:32], bare[0:16]], 0).T)
    for o in range(GROUP):
        keep_ref[o] = mixed[o][:16]
        send_ref[o] = mixed[o][16:].astype(jnp.bfloat16)


def partial_sums(spot, orders, decay, cycle, own, other, panel, far, after, base, count, place, size, begun):
    skip = base // GROUP
    into = place // GROUP
    total = begun[0].shape[0] if begun else size
    smem = pl.BlockSpec(memory_space=pltpu.SMEM)
    out = pl.BlockSpec((GROUP, 16, 96), lambda i, spot: (i + into, 0, 0))
    return pl.pallas_call(
        functools.partial(sums_kernel, base=base),
        out_shape=[jax.ShapeDtypeStruct((total, 16, 96), jnp.float32),
                   jax.ShapeDtypeStruct((total, 16, 96), jnp.bfloat16)],
        input_output_aliases={9: 0, 10: 1} if begun else {},
        grid_spec=pltpu.PrefetchScalarGridSpec(
            num_scalar_prefetch=1,
            grid=(count // GROUP,),
            in_specs=[
                smem, pl.BlockSpec((3, 16, WIDE), lambda i, spot: (0, 0, 0)), smem,
                pl.BlockSpec((2, GROUP, 16, QUARTER), lambda i, spot: (0, i + skip, 0, 0)),
                pl.BlockSpec((1, 16, GAUSS_LANES), lambda i, spot: (i, 0, 0)),
            ] + panel_specs(skip, lambda blk: blk // 2)
            + [pl.BlockSpec((1, 16, PANEL_LANES), lambda i, spot: (i, 0, 0))]
            + [pl.BlockSpec(memory_space=pl.ANY)] * (len(begun) + len(after)),
            out_specs=[out, out],
            scratch_shapes=[
                pltpu.VMEM((2, GROUP, 16, WIDE), jnp.bfloat16),
                pltpu.VMEM((2, GROUP, 16, WIDE), jnp.bfloat16),
                pltpu.VMEM((GROUP, 32, WIDE), jnp.bfloat16),
                pltpu.VMEM((2, GROUP, 16, QUARTER), jnp.bfloat16),
                pltpu.VMEM((2, 8, 32), jnp.float32),
            ],
        ),
        compiler_params=pltpu.CompilerParams(vmem_limit_bytes=16 << 20),
        cost_estimate=pl.CostEstimate(
            flops=count * 32 * 128 * WIDE * 2, bytes_accessed=count * 200000, transcendentals=0),
        name="partial_sums",
    )(spot, orders, decay, cycle, own, other, panel, panel, far, *begun, *after)


def turn(phase, period):
    angle = (phase % period).astype(jnp.float32) * (2.0 * math.pi / period)
    return jnp.cos(angle), jnp.sin(angle)


def body(panel, gauss, height, order_map, cycle_map):
    count, cycles, _ = panel.shape
    shells = height.shape[0]
    here = lax.axis_index("ord")
    spot = lax.axis_index("blk").astype(jnp.int32).reshape(1)
    own = jnp.transpose(gauss, (0, 2, 1, 3))
    own = pltpu.with_memory_space_constraint(own, pltpu.HBM)
    panel = pltpu.with_memory_space_constraint(panel, pltpu.HBM)
    spans = list(zip(CHUNKS[:-1], CHUNKS[1:]))
    orders_int = lax.dynamic_slice_in_dim(order_map, here * count, count, 0)
    degree = (spot // 2 * START + jnp.arange(WIDE)).astype(jnp.float32)[None, :]
    here_ = jnp.exp(-(degree + 2.0) * height[:, None] / ORDERS)
    next_ = jnp.exp(-(degree + 3.0) * height[:, None] / ORDERS)
    decay = jnp.stack([here_, here_ * (degree + 1.0), next_])
    packed, kept, sent, added = [], [], [], []

    def start(c):
        a, b = spans[c]
        after = (kept[-1:] if c >= 2 else []) + ([packed[-1][2]] if packed else [])
        part = packed_panel(spot, cycle_map, panel, after, a, b - a)
        far = lax.ppermute(part, "blk", PANEL_PAIRS)
        coef = packed_gauss(own, [part], a, b - a)
        packed.append((lax.ppermute(coef, "blk", GAUSS_PAIRS), far, coef))

    start(0)
    start(1)
    for c, (a, b) in enumerate(spans):
        begun = [kept.pop(), sent.pop()] if c >= 2 else []
        size = CHUNKS[4] - CHUNKS[1] if c == 1 else b - a
        after = kept[-1:] + (added if c == 3 else [])
        keep, send = partial_sums(
            spot, orders_int, decay, cycle_map, own, packed[c][0], panel, packed[c][1],
            after, a, b - a, a - CHUNKS[1] if c else 0, size, begun)
        kept.append(keep)
        sent.append(send)
        if c in (0, 3):
            added.append(lax.ppermute(send, "blk", PANEL_PAIRS))
        if c < 2:
            start(c + 2)
    total = jnp.concatenate(kept, 0) + jnp.concatenate(added, 0).astype(jnp.float32)
    total = lax.optimization_barrier(total.astype(jnp.bfloat16))
    split = (count, cycles, 3, 2, 4, shells // 4)
    chunk = jnp.transpose(total.reshape(split), (1, 4, 3, 2, 5, 0))

    parts = ORDERS // count
    items = cycles * 3 * shells // parts
    runs = order_map[::RUN] // RUN
    b = jnp.arange(128)
    q = jnp.arange(RUN)
    cos1, sin1 = turn(b[:, None] * runs[None, :], 128)
    table = jnp.concatenate(
        [jnp.concatenate([cos1, sin1], 1), jnp.concatenate([sin1, -cos1], 1)], 0)
    cos2, sin2 = turn(b[:, None] * q[None, :], NLON)
    cos3, sin3 = turn(q[:, None] * q[None, :], RUN)
    last = jnp.concatenate([cos3, -sin3], 1)

    chunk = chunk.reshape(parts, 2, items * count)
    chunk, table, cos2, sin2, last = lax.optimization_barrier((chunk, table, cos2, sin2, last))
    spread = lax.all_to_all(chunk, "ord", 0, 0, tiled=True).astype(jnp.float32)
    flat = jnp.concatenate([spread[:, 0], spread[:, 1]], 0)
    mid = jnp.dot(table, flat, precision=lax.Precision.HIGHEST).reshape(2, 128, items, count)
    cos2, sin2 = cos2[:, None, :], sin2[:, None, :]
    real = mid[0] * cos2 - mid[1] * sin2
    imag = mid[0] * sin2 + mid[1] * cos2
    field = lax.dot_general(
        last, jnp.concatenate([real, imag], 2),
        (((1,), (2,)), ((), ())), precision=lax.Precision.HIGHEST)
    field = field.reshape(parts, NLON // parts, items).astype(jnp.bfloat16)
    field = lax.all_to_all(field, "ord", 0, 0, tiled=True)
    field = field.reshape(cycles, 4, NLON // parts, 3, shells // 4)
    return jnp.transpose(field, (2, 0, 3, 1, 4)).reshape(NLON // parts, cycles * 3 * shells)


def solution(mesh):
    return jax.shard_map(
        body,
        mesh=mesh,
        in_specs=(P("ord", "blk", None), P(None, None, "ord", "blk"), P(), P(), P("blk")),
        out_specs=P("ord", "blk"),
        check_vma=False,
    )
```

```python
import functools
import math

import jax
import jax.numpy as jnp
from jax import lax
from jax.experimental import pallas as pl
from jax.experimental.pallas import tpu as pltpu
from jax.sharding import PartitionSpec as P

ORDERS = 2880
RUN = 45
QUARTER = 720
START = 1408
WIDE = 1536
KEPT = 1472
NLON = 5760
GROUP = 5
CHUNKS = (0, 15, 30, 40, 45)
GAUSS_TAIL = 2 * GROUP * 640
GAUSS_LANES = GAUSS_TAIL + 896
PANEL_TAIL = GROUP * START
PANEL_LANES = PANEL_TAIL + 384
CYCLE_LANE = PANEL_TAIL + 320
GAUSS_PAIRS = [(0, 1), (1, 0), (2, 3), (3, 2)]
PANEL_PAIRS = [(1, 2), (2, 1), (3, 0), (0, 3)]


def pack_panel(spot_ref, cycle_ref, main_ref, tail_ref, *rest):
    out_ref = rest[-1]
    row = lax.broadcasted_iota(jnp.int32, (16, 2), 0)
    column = lax.broadcasted_iota(jnp.int32, (16, 2), 1)
    digits = jnp.zeros((16, 2), jnp.int32)
    for i in range(16):
        value = jnp.where(column == 0, cycle_ref[i] // 64, cycle_ref[i] % 64)
        digits = jnp.where(row == i, value, digits)
    out_ref[0, :, CYCLE_LANE:CYCLE_LANE + 2] = digits.astype(jnp.float32).astype(jnp.bfloat16)
    for o in range(GROUP):
        out_ref[0, :, START * o:START * (o + 1)] = main_ref[o]
        out_ref[0, :, PANEL_TAIL + 64 * o:PANEL_TAIL + 64 * (o + 1)] = tail_ref[o, :, 0:64]


def pack_gauss(gauss_ref, *rest):
    out_ref = rest[-1]
    for o in range(GROUP):
        for k in range(2):
            j = k * GROUP + o
            out_ref[0, :, 640 * j:640 * (j + 1)] = gauss_ref[k, o, :, 0:640]
            out_ref[0, :, GAUSS_TAIL + 80 * j:GAUSS_TAIL + 80 * (j + 1)] = gauss_ref[k, o, :, 640:720]


def panel_specs(skip, upper):
    return [
        pl.BlockSpec((GROUP, 16, START), lambda i, spot: (i + skip, 0, upper(spot[0]))),
        pl.BlockSpec((GROUP, 16, 128), lambda i, spot: (i + skip, 0, 11 + 11 * upper(spot[0]))),
    ]


def packed_panel(spot, cycle, panel, after, base, count):
    steps = count // GROUP
    return pl.pallas_call(
        pack_panel,
        out_shape=jax.ShapeDtypeStruct((steps, 16, PANEL_LANES), jnp.bfloat16),
        grid_spec=pltpu.PrefetchScalarGridSpec(
            num_scalar_prefetch=1,
            grid=(steps,),
            in_specs=[pl.BlockSpec(memory_space=pltpu.SMEM)]
            + panel_specs(base // GROUP, lambda blk: 1 - blk // 2)
            + [pl.BlockSpec(memory_space=pl.ANY)] * len(after),
            out_specs=pl.BlockSpec((1, 16, PANEL_LANES), lambda i, spot: (i, 0, 0)),
        ),
        compiler_params=pltpu.CompilerParams(vmem_limit_bytes=10 << 20),
        cost_estimate=pl.CostEstimate(flops=0, bytes_accessed=count * 100000, transcendentals=0),
        name="pack_panel",
    )(spot, cycle, panel, panel, *after)


def packed_gauss(own, after, base, count):
    steps, skip = count // GROUP, base // GROUP
    return pl.pallas_call(
        pack_gauss,
        out_shape=jax.ShapeDtypeStruct((steps, 16, GAUSS_LANES), jnp.bfloat16),
        grid=(steps,),
        in_specs=[pl.BlockSpec((2, GROUP, 16, QUARTER), lambda i: (0, i + skip, 0, 0))]
        + [pl.BlockSpec(memory_space=pl.ANY)] * len(after),
        out_specs=pl.BlockSpec((1, 16, GAUSS_LANES), lambda i: (i, 0, 0)),
        compiler_params=pltpu.CompilerParams(vmem_limit_bytes=10 << 20),
        cost_estimate=pl.CostEstimate(flops=0, bytes_accessed=count * 100000, transcendentals=0),
        name="pack_gauss",
    )(own, *after)


def sums_kernel(spot_ref, order_ref, decay_ref, cycle_ref, own_ref, other_ref, main_ref, tail_ref,
                far_ref, *rest, base):
    keep_ref, send_ref, gs_ref, gn_ref, table_ref, mate_ref, angle_ref = rest[-7:]
    step = pl.program_id(0)
    half = spot_ref[0] // 2
    odd = spot_ref[0] % 2 == 1
    first = (half * START).astype(jnp.float32)
    degree = lax.broadcasted_iota(jnp.int32, (1, WIDE), 1).astype(jnp.float32) + first

    @pl.when(step == 0)
    def _():
        gs_ref[...] = jnp.zeros_like(gs_ref)
        gn_ref[...] = jnp.zeros_like(gn_ref)
        table_ref[...] = jnp.zeros_like(table_ref)
        digits = far_ref[0, :, CYCLE_LANE:CYCLE_LANE + 2].astype(jnp.float32)
        mates = digits[:, 0:1] * 64.0 + digits[:, 1:2]
        cycles = jnp.broadcast_to(mates, (16, 128)).T[0:8, :]
        cycles = jnp.concatenate([jnp.zeros((8, 16), jnp.float32), cycles], 1)
        lane = lax.broadcasted_iota(jnp.int32, (8, 32), 1)
        for i in range(16):
            cycles = jnp.where(lane == i, cycle_ref[i].astype(jnp.float32), cycles)
        theta = math.pi * (cycles + 0.5) / ORDERS
        angle_ref[0] = jnp.cos(theta)
        angle_ref[1] = 1.0 / jnp.sin(theta)

    for o in range(GROUP):
        for k in range(2):
            j = k * GROUP + o
            mate_ref[k, o, :, 0:640] = other_ref[0, :, 640 * j:640 * (j + 1)]
            mate_ref[k, o, :, 640:720] = other_ref[0, :, GAUSS_TAIL + 80 * j:GAUSS_TAIL + 80 * (j + 1)]
        table_ref[o, 0:16, 0:START] = main_ref[o]
        table_ref[o, 0:16, START:KEPT] = tail_ref[o, :, 0:64]
        table_ref[o, 16:32, 0:START] = far_ref[0, :, START * o:START * (o + 1)]
        table_ref[o, 16:32, START:KEPT] = far_ref[0, :, PANEL_TAIL + 64 * o:PANEL_TAIL + 64 * (o + 1)]
    low = jnp.where(odd, mate_ref[...], own_ref[...])
    high = jnp.where(odd, own_ref[...], mate_ref[...])

    @pl.when(half == 0)
    def _():
        gs_ref[:, :, :, 0:720] = low
        gs_ref[:, :, :, 720:1440] = high
        gn_ref[:, :, :, 0:719] = low[:, :, :, 1:]
        gn_ref[:, :, :, 719:1439] = high

    @pl.when(half == 1)
    def _():
        gs_ref[:, :, :, 32:752] = low
        gs_ref[:, :, :, 752:1472] = high
        gn_ref[:, :, :, 31:751] = low
        gn_ref[:, :, :, 751:1471] = high

    cosine = angle_ref[0, 0:1]
    inverse = angle_ref[1, 0:1]
    orders = [order_ref[base + step * GROUP + o].astype(jnp.float32) for o in range(GROUP)]
    sums = []
    for o in range(GROUP):
        gap = jnp.maximum((degree + 1.0) * (degree + 1.0) - orders[o] * orders[o], 0.0)
        slope = decay_ref[2] * jnp.sqrt(gap)
        g = [gs_ref[k, o].astype(jnp.float32) for k in range(2)]
        n = [gn_ref[k, o].astype(jnp.float32) for k in range(2)]
        weights = jnp.concatenate(
            [g[0] * decay_ref[1], g[1] * decay_ref[1], g[0] * decay_ref[0], g[1] * decay_ref[0],
             n[0] * slope, n[1] * slope], 0).astype(jnp.bfloat16)
        sums.append(lax.dot_general(
            weights, table_ref[o], (((1,), (1,)), ((), ())), preferred_element_type=jnp.float32))
    mixed = []
    for o in range(GROUP):
        main, bare, tilt = sums[o][0:32], sums[o][32:64], sums[o][64:96]
        polar = (tilt - cosine * (main - bare)) * inverse
        bare = orders[o] * inverse * bare
        mixed.append(jnp.concatenate([main, polar, -bare[16:32], bare[0:16]], 0).T)
    for o in range(GROUP):
        keep_ref[o] = mixed[o][:16]
        send_ref[o] = mixed[o][16:].astype(jnp.bfloat16)


def partial_sums(spot, orders, decay, cycle, own, other, panel, far, after, base, count, place, size, begun):
    skip = base // GROUP
    into = place // GROUP
    total = begun[0].shape[0] if begun else size
    smem = pl.BlockSpec(memory_space=pltpu.SMEM)
    out = pl.BlockSpec((GROUP, 16, 96), lambda i, spot: (i + into, 0, 0))
    return pl.pallas_call(
        functools.partial(sums_kernel, base=base),
        out_shape=[jax.ShapeDtypeStruct((total, 16, 96), jnp.float32),
                   jax.ShapeDtypeStruct((total, 16, 96), jnp.bfloat16)],
        input_output_aliases={9: 0, 10: 1} if begun else {},
        grid_spec=pltpu.PrefetchScalarGridSpec(
            num_scalar_prefetch=1,
            grid=(count // GROUP,),
            in_specs=[
                smem, pl.BlockSpec((3, 16, WIDE), lambda i, spot: (0, 0, 0)), smem,
                pl.BlockSpec((2, GROUP, 16, QUARTER), lambda i, spot: (0, i + skip, 0, 0)),
                pl.BlockSpec((1, 16, GAUSS_LANES), lambda i, spot: (i, 0, 0)),
            ] + panel_specs(skip, lambda blk: blk // 2)
            + [pl.BlockSpec((1, 16, PANEL_LANES), lambda i, spot: (i, 0, 0))]
            + [pl.BlockSpec(memory_space=pl.ANY)] * (len(begun) + len(after)),
            out_specs=[out, out],
            scratch_shapes=[
                pltpu.VMEM((2, GROUP, 16, WIDE), jnp.bfloat16),
                pltpu.VMEM((2, GROUP, 16, WIDE), jnp.bfloat16),
                pltpu.VMEM((GROUP, 32, WIDE), jnp.bfloat16),
                pltpu.VMEM((2, GROUP, 16, QUARTER), jnp.bfloat16),
                pltpu.VMEM((2, 8, 32), jnp.float32),
            ],
        ),
        compiler_params=pltpu.CompilerParams(vmem_limit_bytes=16 << 20),
        cost_estimate=pl.CostEstimate(
            flops=count * 32 * 128 * WIDE * 2, bytes_accessed=count * 200000, transcendentals=0),
        name="partial_sums",
    )(spot, orders, decay, cycle, own, other, panel, panel, far, *begun, *after)


def turn(phase, period):
    angle = (phase % period).astype(jnp.float32) * (2.0 * math.pi / period)
    return jnp.cos(angle), jnp.sin(angle)


def body(panel, gauss, height, order_map, cycle_map):
    count, cycles, _ = panel.shape
    shells = height.shape[0]
    here = lax.axis_index("ord")
    spot = lax.axis_index("blk").astype(jnp.int32).reshape(1)
    own = jnp.transpose(gauss, (0, 2, 1, 3))
    own = pltpu.with_memory_space_constraint(own, pltpu.HBM)
    panel = pltpu.with_memory_space_constraint(panel, pltpu.HBM)
    spans = list(zip(CHUNKS[:-1], CHUNKS[1:]))
    orders_int = lax.dynamic_slice_in_dim(order_map, here * count, count, 0)
    degree = (spot // 2 * START + jnp.arange(WIDE)).astype(jnp.float32)[None, :]
    here_ = jnp.exp(-(degree + 2.0) * height[:, None] / ORDERS)
    next_ = jnp.exp(-(degree + 3.0) * height[:, None] / ORDERS)
    decay = jnp.stack([here_, here_ * (degree + 1.0), next_])
    packed, kept, sent, added = [], [], [], []

    def start(c):
        a, b = spans[c]
        after = (kept[0:1] if c >= 2 else []) + ([packed[-1][2]] if packed else [])
        part = packed_panel(spot, cycle_map, panel, after, a, b - a)
        far = lax.ppermute(part, "blk", PANEL_PAIRS)
        coef = packed_gauss(own, [part], a, b - a)
        packed.append((lax.ppermute(coef, "blk", GAUSS_PAIRS), far, coef))

    start(0)
    start(1)
    for c, (a, b) in enumerate(spans):
        begun = [kept.pop(), sent.pop()] if c >= 2 else []
        size = CHUNKS[4] - CHUNKS[1] if c == 1 else b - a
        after = kept[-1:] + (added if c == 3 else [])
        keep, send = partial_sums(
            spot, orders_int, decay, cycle_map, own, packed[c][0], panel, packed[c][1],
            after, a, b - a, a - CHUNKS[1] if c else 0, size, begun)
        kept.append(keep)
        sent.append(send)
        if c in (0, 3):
            added.append(lax.ppermute(send, "blk", PANEL_PAIRS))
        if c < 2:
            start(c + 2)
    total = jnp.concatenate(kept, 0) + jnp.concatenate(added, 0).astype(jnp.float32)
    total = lax.optimization_barrier(total.astype(jnp.bfloat16))
    split = (count, cycles, 3, 2, 4, shells // 4)
    chunk = jnp.transpose(total.reshape(split), (1, 4, 3, 2, 5, 0))

    parts = ORDERS // count
    items = cycles * 3 * shells // parts
    runs = order_map[::RUN] // RUN
    b = jnp.arange(128)
    q = jnp.arange(RUN)
    cos1, sin1 = turn(b[:, None] * runs[None, :], 128)
    table = jnp.concatenate(
        [jnp.concatenate([cos1, sin1], 1), jnp.concatenate([sin1, -cos1], 1)], 0)
    cos2, sin2 = turn(b[:, None] * q[None, :], NLON)
    cos3, sin3 = turn(q[:, None] * q[None, :], RUN)
    last = jnp.concatenate([cos3, -sin3], 1)

    chunk = chunk.reshape(parts, 2, items * count)
    chunk, table, cos2, sin2, last = lax.optimization_barrier((chunk, table, cos2, sin2, last))
    spread = lax.all_to_all(chunk, "ord", 0, 0, tiled=True).astype(jnp.float32)
    flat = jnp.concatenate([spread[:, 0], spread[:, 1]], 0)
    mid = jnp.dot(table, flat, precision=lax.Precision.HIGHEST).reshape(2, 128, items, count)
    cos2, sin2 = cos2[:, None, :], sin2[:, None, :]
    real = mid[0] * cos2 - mid[1] * sin2
    imag = mid[0] * sin2 + mid[1] * cos2
    field = lax.dot_general(
        last, jnp.concatenate([real, imag], 2),
        (((1,), (2,)), ((), ())), precision=lax.Precision.HIGHEST)
    field = field.reshape(parts, NLON // parts, 3, shells // 4).astype(jnp.bfloat16)
    field = jnp.transpose(field, (0, 2, 3, 1)).reshape(parts * 3, shells // 4, NLON // parts)
    field = lax.all_to_all(field, "ord", 0, 0, tiled=True)
    field = field.reshape(cycles, 4, 3, shells // 4, NLON // parts)
    return jnp.transpose(field, (4, 0, 2, 1, 3)).reshape(NLON // parts, cycles * 3 * shells)


def solution(mesh):
    return jax.shard_map(
        body,
        mesh=mesh,
        in_specs=(P("ord", "blk", None), P(None, None, "ord", "blk"), P(), P(), P("blk")),
        out_specs=P("ord", "blk"),
        check_vma=False,
    )
```

```python
import functools
import math

import jax
import jax.numpy as jnp
from jax import lax
from jax.experimental import pallas as pl
from jax.experimental.pallas import tpu as pltpu
from jax.sharding import PartitionSpec as P

ORDERS = 2880
RUN = 45
QUARTER = 720
START = 1408
WIDE = 1536
KEPT = 1472
NLON = 5760
GROUP = 5
CHUNKS = (0, 15, 30, 40, 45)
GAUSS_TAIL = 2 * GROUP * 640
GAUSS_LANES = GAUSS_TAIL + 896
PANEL_TAIL = GROUP * START
PANEL_LANES = PANEL_TAIL + 384
CYCLE_LANE = PANEL_TAIL + 320
GAUSS_PAIRS = [(0, 1), (1, 0), (2, 3), (3, 2)]
PANEL_PAIRS = [(1, 2), (2, 1), (3, 0), (0, 3)]


def pack_panel(spot_ref, cycle_hbm, *rest, steps):
    out_ref, cycle_ref, sem = rest[-3:]
    copy = pltpu.make_async_copy(cycle_hbm, cycle_ref, sem)
    copy.start()
    for g in range(steps):
        main_ref, tail_ref = rest[2 * g:2 * g + 2]
        for o in range(GROUP):
            out_ref[g, :, START * o:START * (o + 1)] = main_ref[o]
            out_ref[g, :, PANEL_TAIL + 64 * o:PANEL_TAIL + 64 * (o + 1)] = tail_ref[o, :, 0:64]
    copy.wait()
    row = lax.broadcasted_iota(jnp.int32, (16, 2), 0)
    column = lax.broadcasted_iota(jnp.int32, (16, 2), 1)
    digits = jnp.zeros((16, 2), jnp.int32)
    for i in range(16):
        value = jnp.where(column == 0, cycle_ref[i] // 64, cycle_ref[i] % 64)
        digits = jnp.where(row == i, value, digits)
    digits = digits.astype(jnp.float32).astype(jnp.bfloat16)
    for g in range(steps):
        out_ref[g, :, CYCLE_LANE:CYCLE_LANE + 2] = digits


def pack_gauss(*rest, steps):
    out_ref = rest[-1]
    for g in range(steps):
        for k in range(2):
            for o in range(GROUP):
                j = k * GROUP + o
                plane = rest[2 * g + k]
                out_ref[g, :, 640 * j:640 * (j + 1)] = plane[0, o, :, 0:640]
                out_ref[g, :, GAUSS_TAIL + 80 * j:GAUSS_TAIL + 80 * (j + 1)] = plane[0, o, :, 640:720]


def panel_specs(skip, upper):
    return [
        pl.BlockSpec((GROUP, 16, START), lambda i, spot: (i + skip, 0, upper(spot[0]))),
        pl.BlockSpec((GROUP, 16, 128), lambda i, spot: (i + skip, 0, 11 + 11 * upper(spot[0]))),
    ]


def packed_panel(spot, cycle, panel, after, base, count):
    steps = count // GROUP
    specs = []
    for g in range(steps):
        specs += panel_specs(base // GROUP + g, lambda blk: 1 - blk // 2)
    return pl.pallas_call(
        functools.partial(pack_panel, steps=steps),
        out_shape=jax.ShapeDtypeStruct((steps, 16, PANEL_LANES), jnp.bfloat16),
        grid_spec=pltpu.PrefetchScalarGridSpec(
            num_scalar_prefetch=1,
            grid=(1,),
            in_specs=[pl.BlockSpec(memory_space=pl.ANY)] + specs
            + [pl.BlockSpec(memory_space=pl.ANY)] * len(after),
            out_specs=pl.BlockSpec(memory_space=pltpu.VMEM),
            scratch_shapes=[pltpu.SMEM((16,), jnp.int32), pltpu.SemaphoreType.DMA(())],
        ),
        compiler_params=pltpu.CompilerParams(vmem_limit_bytes=10 << 20),
        cost_estimate=pl.CostEstimate(flops=0, bytes_accessed=count * 100000, transcendentals=0),
        name="pack_panel",
    )(spot, cycle, *[panel] * (2 * steps), *after)


def packed_gauss(own, after, base, count):
    steps, skip = count // GROUP, base // GROUP
    specs = []
    for g in range(steps):
        for k in range(2):
            specs.append(pl.BlockSpec(
                (1, GROUP, 16, QUARTER), lambda i, k=k, at=skip + g: (k, at, 0, 0)))
    return pl.pallas_call(
        functools.partial(pack_gauss, steps=steps),
        out_shape=jax.ShapeDtypeStruct((steps, 16, GAUSS_LANES), jnp.bfloat16),
        grid=(1,),
        in_specs=specs + [pl.BlockSpec(memory_space=pl.ANY)] * len(after),
        out_specs=pl.BlockSpec(memory_space=pltpu.VMEM),
        compiler_params=pltpu.CompilerParams(vmem_limit_bytes=10 << 20),
        cost_estimate=pl.CostEstimate(flops=0, bytes_accessed=count * 100000, transcendentals=0),
        name="pack_gauss",
    )(*[own] * (2 * steps), *after)


def sums_kernel(spot_ref, order_ref, decay_ref, cycle_ref, own_ref, other_ref, main_ref, tail_ref,
                far_ref, *rest, base):
    keep_ref, send_ref, gs_ref, gn_ref, table_ref, mate_ref, angle_ref = rest[-7:]
    step = pl.program_id(0)
    half = spot_ref[0] // 2
    odd = spot_ref[0] % 2 == 1
    first = (half * START).astype(jnp.float32)
    degree = lax.broadcasted_iota(jnp.int32, (1, WIDE), 1).astype(jnp.float32) + first

    @pl.when(step == 0)
    def _():
        gs_ref[...] = jnp.zeros_like(gs_ref)
        gn_ref[...] = jnp.zeros_like(gn_ref)
        table_ref[...] = jnp.zeros_like(table_ref)
        digits = far_ref[0, :, CYCLE_LANE:CYCLE_LANE + 2].astype(jnp.float32)
        mates = digits[:, 0:1] * 64.0 + digits[:, 1:2]
        cycles = jnp.broadcast_to(mates, (16, 128)).T[0:8, :]
        cycles = jnp.concatenate([jnp.zeros((8, 16), jnp.float32), cycles], 1)
        lane = lax.broadcasted_iota(jnp.int32, (8, 32), 1)
        for i in range(16):
            cycles = jnp.where(lane == i, cycle_ref[i].astype(jnp.float32), cycles)
        theta = math.pi * (cycles + 0.5) / ORDERS
        angle_ref[0] = jnp.cos(theta)
        angle_ref[1] = 1.0 / jnp.sin(theta)

    for o in range(GROUP):
        for k in range(2):
            j = k * GROUP + o
            mate_ref[k, o, :, 0:640] = other_ref[0, :, 640 * j:640 * (j + 1)]
            mate_ref[k, o, :, 640:720] = other_ref[0, :, GAUSS_TAIL + 80 * j:GAUSS_TAIL + 80 * (j + 1)]
        table_ref[o, 0:16, 0:START] = main_ref[o]
        table_ref[o, 0:16, START:KEPT] = tail_ref[o, :, 0:64]
        table_ref[o, 16:32, 0:START] = far_ref[0, :, START * o:START * (o + 1)]
        table_ref[o, 16:32, START:KEPT] = far_ref[0, :, PANEL_TAIL + 64 * o:PANEL_TAIL + 64 * (o + 1)]
    low = jnp.where(odd, mate_ref[...], own_ref[...])
    high = jnp.where(odd, own_ref[...], mate_ref[...])

    @pl.when(half == 0)
    def _():
        gs_ref[:, :, :, 0:720] = low
        gs_ref[:, :, :, 720:1440] = high
        gn_ref[:, :, :, 0:719] = low[:, :, :, 1:]
        gn_ref[:, :, :, 719:1439] = high

    @pl.when(half == 1)
    def _():
        gs_ref[:, :, :, 32:752] = low
        gs_ref[:, :, :, 752:1472] = high
        gn_ref[:, :, :, 31:751] = low
        gn_ref[:, :, :, 751:1471] = high

    cosine = angle_ref[0, 0:1]
    inverse = angle_ref[1, 0:1]
    orders = [order_ref[base + step * GROUP + o].astype(jnp.float32) for o in range(GROUP)]
    sums = []
    for o in range(GROUP):
        gap = jnp.maximum((degree + 1.0) * (degree + 1.0) - orders[o] * orders[o], 0.0)
        slope = decay_ref[2] * jnp.sqrt(gap)
        g = [gs_ref[k, o].astype(jnp.float32) for k in range(2)]
        n = [gn_ref[k, o].astype(jnp.float32) for k in range(2)]
        weights = jnp.concatenate(
            [g[0] * decay_ref[1], g[1] * decay_ref[1], g[0] * decay_ref[0], g[1] * decay_ref[0],
             n[0] * slope, n[1] * slope], 0).astype(jnp.bfloat16)
        sums.append(lax.dot_general(
            weights, table_ref[o], (((1,), (1,)), ((), ())), preferred_element_type=jnp.float32))
    mixed = []
    for o in range(GROUP):
        main, bare, tilt = sums[o][0:32], sums[o][32:64], sums[o][64:96]
        polar = (tilt - cosine * (main - bare)) * inverse
        bare = orders[o] * inverse * bare
        mixed.append(jnp.concatenate([main, polar, -bare[16:32], bare[0:16]], 0).T)
    for o in range(GROUP):
        keep_ref[o] = mixed[o][:16]
        send_ref[o] = mixed[o][16:].astype(jnp.bfloat16)


def partial_sums(spot, orders, decay, cycle, own, other, panel, far, after, base, count, place, size, begun):
    skip = base // GROUP
    into = place // GROUP
    total = begun[0].shape[0] if begun else size
    smem = pl.BlockSpec(memory_space=pltpu.SMEM)
    out = pl.BlockSpec((GROUP, 16, 96), lambda i, spot: (i + into, 0, 0))
    return pl.pallas_call(
        functools.partial(sums_kernel, base=base),
        out_shape=[jax.ShapeDtypeStruct((total, 16, 96), jnp.float32),
                   jax.ShapeDtypeStruct((total, 16, 96), jnp.bfloat16)],
        input_output_aliases={9: 0, 10: 1} if begun else {},
        grid_spec=pltpu.PrefetchScalarGridSpec(
            num_scalar_prefetch=1,
            grid=(count // GROUP,),
            in_specs=[
                smem, pl.BlockSpec((3, 16, WIDE), lambda i, spot: (0, 0, 0)), smem,
                pl.BlockSpec((2, GROUP, 16, QUARTER), lambda i, spot: (0, i + skip, 0, 0)),
                pl.BlockSpec((1, 16, GAUSS_LANES), lambda i, spot: (i, 0, 0)),
            ] + panel_specs(skip, lambda blk: blk // 2)
            + [pl.BlockSpec((1, 16, PANEL_LANES), lambda i, spot: (i, 0, 0))]
            + [pl.BlockSpec(memory_space=pl.ANY)] * (len(begun) + len(after)),
            out_specs=[out, out],
            scratch_shapes=[
                pltpu.VMEM((2, GROUP, 16, WIDE), jnp.bfloat16),
                pltpu.VMEM((2, GROUP, 16, WIDE), jnp.bfloat16),
                pltpu.VMEM((GROUP, 32, WIDE), jnp.bfloat16),
                pltpu.VMEM((2, GROUP, 16, QUARTER), jnp.bfloat16),
                pltpu.VMEM((2, 8, 32), jnp.float32),
            ],
        ),
        compiler_params=pltpu.CompilerParams(vmem_limit_bytes=16 << 20),
        cost_estimate=pl.CostEstimate(
            flops=count * 32 * 128 * WIDE * 2, bytes_accessed=count * 200000, transcendentals=0),
        name="partial_sums",
    )(spot, orders, decay, cycle, own, other, panel, panel, far, *begun, *after)


def turn(phase, period):
    angle = (phase % period).astype(jnp.float32) * (2.0 * math.pi / period)
    return jnp.cos(angle), jnp.sin(angle)


def body(panel, gauss, height, order_map, cycle_map):
    count, cycles, _ = panel.shape
    shells = height.shape[0]
    here = lax.axis_index("ord")
    spot = lax.axis_index("blk").astype(jnp.int32).reshape(1)
    own = jnp.transpose(gauss, (0, 2, 1, 3))
    own = pltpu.with_memory_space_constraint(own, pltpu.HBM)
    panel = pltpu.with_memory_space_constraint(panel, pltpu.HBM)
    cycle_hbm = pltpu.with_memory_space_constraint(cycle_map, pltpu.HBM)
    spans = list(zip(CHUNKS[:-1], CHUNKS[1:]))
    orders_int = lax.dynamic_slice_in_dim(order_map, here * count, count, 0)
    degree = (spot // 2 * START + jnp.arange(WIDE)).astype(jnp.float32)[None, :]
    here_ = jnp.exp(-(degree + 2.0) * height[:, None] / ORDERS)
    next_ = jnp.exp(-(degree + 3.0) * height[:, None] / ORDERS)
    decay = jnp.stack([here_, here_ * (degree + 1.0), next_])
    packed, kept, sent, added = [], [], [], []

    def start(c):
        a, b = spans[c]
        after = (kept[0:1] if c >= 2 else []) + ([packed[-1][2]] if packed else [])
        part = packed_panel(spot, cycle_hbm, panel, after, a, b - a)
        far = lax.ppermute(part, "blk", PANEL_PAIRS)
        coef = packed_gauss(own, [part], a, b - a)
        packed.append((lax.ppermute(coef, "blk", GAUSS_PAIRS), far, coef))

    start(0)
    start(1)
    for c, (a, b) in enumerate(spans):
        begun = [kept.pop(), sent.pop()] if c >= 2 else []
        size = CHUNKS[4] - CHUNKS[1] if c == 1 else b - a
        after = kept[-1:] + (added if c == 3 else [])
        keep, send = partial_sums(
            spot, orders_int, decay, cycle_map, own, packed[c][0], panel, packed[c][1],
            after, a, b - a, a - CHUNKS[1] if c else 0, size, begun)
        kept.append(keep)
        sent.append(send)
        if c in (0, 3):
            added.append(lax.ppermute(send, "blk", PANEL_PAIRS))
        if c < 2:
            start(c + 2)
    total = jnp.concatenate(kept, 0) + jnp.concatenate(added, 0).astype(jnp.float32)
    total = lax.optimization_barrier(total.astype(jnp.bfloat16))
    split = (count, cycles, 3, 2, 4, shells // 4)
    chunk = jnp.transpose(total.reshape(split), (1, 4, 3, 2, 5, 0))

    parts = ORDERS // count
    items = cycles * 3 * shells // parts
    runs = order_map[::RUN] // RUN
    b = jnp.arange(128)
    q = jnp.arange(RUN)
    cos1, sin1 = turn(b[:, None] * runs[None, :], 128)
    table = jnp.concatenate(
        [jnp.concatenate([cos1, sin1], 1), jnp.concatenate([sin1, -cos1], 1)], 0)
    cos2, sin2 = turn(b[:, None] * q[None, :], NLON)
    cos3, sin3 = turn(q[:, None] * q[None, :], RUN)
    last = jnp.concatenate([cos3, -sin3], 1)

    chunk = chunk.reshape(parts, 2, items * count)
    chunk, table, cos2, sin2, last = lax.optimization_barrier((chunk, table, cos2, sin2, last))
    spread = lax.all_to_all(chunk, "ord", 0, 0, tiled=True).astype(jnp.float32)
    flat = jnp.concatenate([spread[:, 0], spread[:, 1]], 0)
    mid = jnp.dot(table, flat, precision=lax.Precision.HIGHEST).reshape(2, 128, items, count)
    cos2, sin2 = cos2[:, None, :], sin2[:, None, :]
    real = mid[0] * cos2 - mid[1] * sin2
    imag = mid[0] * sin2 + mid[1] * cos2
    field = lax.dot_general(
        last, jnp.concatenate([real, imag], 2),
        (((1,), (2,)), ((), ())), precision=lax.Precision.HIGHEST)
    field = field.reshape(parts, NLON // parts, 3, shells // 4).astype(jnp.bfloat16)
    field = jnp.transpose(field, (0, 2, 3, 1)).reshape(parts * 3, shells // 4, NLON // parts)
    field = lax.all_to_all(field, "ord", 0, 0, tiled=True)
    field = field.reshape(cycles, 4, 3, shells // 4, NLON // parts)
    return jnp.transpose(field, (4, 0, 2, 1, 3)).reshape(NLON // parts, cycles * 3 * shells)


def solution(mesh):
    return jax.shard_map(
        body,
        mesh=mesh,
        in_specs=(P("ord", "blk", None), P(None, None, "ord", "blk"), P(), P(), P("blk")),
        out_specs=P("ord", "blk"),
        check_vma=False,
    )
```

```python
import functools
import math

import jax
import jax.numpy as jnp
from jax import lax
from jax.experimental import pallas as pl
from jax.experimental.pallas import tpu as pltpu
from jax.sharding import PartitionSpec as P

ORDERS = 2880
RUN = 45
QUARTER = 720
START = 1408
WIDE = 1536
KEPT = 1472
NLON = 5760
GROUP = 5
CHUNKS = (0, 15, 30, 40, 45)
GAUSS_TAIL = 2 * GROUP * 640
GAUSS_LANES = GAUSS_TAIL + 896
PANEL_TAIL = GROUP * START
PANEL_LANES = PANEL_TAIL + 384
CYCLE_LANE = PANEL_TAIL + 320
GAUSS_PAIRS = [(0, 1), (1, 0), (2, 3), (3, 2)]
PANEL_PAIRS = [(1, 2), (2, 1), (3, 0), (0, 3)]


def pack_panel(spot_ref, cycle_ref, *rest, steps):
    out_ref = rest[-1]
    cycle = cycle_ref[...]
    row = lax.broadcasted_iota(jnp.int32, (16, 16), 0)
    lane = lax.broadcasted_iota(jnp.int32, (16, 16), 1)
    digits = []
    for digit in (cycle // 64, cycle % 64):
        spread = jnp.broadcast_to(digit.astype(jnp.float32), (16, 16))
        digits.append(jnp.sum(jnp.where(row == lane, spread, 0.0), 1, keepdims=True))
    digits = jnp.concatenate(digits, 1).astype(jnp.bfloat16)
    for g in range(steps):
        main_ref, tail_ref = rest[2 * g:2 * g + 2]
        out_ref[g, :, CYCLE_LANE:CYCLE_LANE + 2] = digits
        for o in range(GROUP):
            out_ref[g, :, START * o:START * (o + 1)] = main_ref[o]
            out_ref[g, :, PANEL_TAIL + 64 * o:PANEL_TAIL + 64 * (o + 1)] = tail_ref[o, :, 0:64]


def pack_gauss(*rest, steps):
    out_ref = rest[-1]
    for g in range(steps):
        for k in range(2):
            for o in range(GROUP):
                j = k * GROUP + o
                plane = rest[2 * g + k]
                out_ref[g, :, 640 * j:640 * (j + 1)] = plane[0, o, :, 0:640]
                out_ref[g, :, GAUSS_TAIL + 80 * j:GAUSS_TAIL + 80 * (j + 1)] = plane[0, o, :, 640:720]


def panel_specs(skip, upper):
    return [
        pl.BlockSpec((GROUP, 16, START), lambda i, spot: (i + skip, 0, upper(spot[0]))),
        pl.BlockSpec((GROUP, 16, 128), lambda i, spot: (i + skip, 0, 11 + 11 * upper(spot[0]))),
    ]


def packed_panel(spot, cycle, panel, after, base, count):
    steps = count // GROUP
    specs = []
    for g in range(steps):
        specs += panel_specs(base // GROUP + g, lambda blk: 1 - blk // 2)
    return pl.pallas_call(
        functools.partial(pack_panel, steps=steps),
        out_shape=jax.ShapeDtypeStruct((steps, 16, PANEL_LANES), jnp.bfloat16),
        grid_spec=pltpu.PrefetchScalarGridSpec(
            num_scalar_prefetch=1,
            grid=(1,),
            in_specs=[pl.BlockSpec((1, 16), lambda i, spot: (0, 0))] + specs
            + [pl.BlockSpec(memory_space=pl.ANY)] * len(after),
            out_specs=pl.BlockSpec(memory_space=pltpu.VMEM),
        ),
        compiler_params=pltpu.CompilerParams(vmem_limit_bytes=10 << 20),
        cost_estimate=pl.CostEstimate(flops=0, bytes_accessed=count * 100000, transcendentals=0),
        name="pack_panel",
    )(spot, cycle, *[panel] * (2 * steps), *after)


def packed_gauss(own, after, base, count):
    steps, skip = count // GROUP, base // GROUP
    specs = []
    for g in range(steps):
        for k in range(2):
            specs.append(pl.BlockSpec(
                (1, GROUP, 16, QUARTER), lambda i, k=k, at=skip + g: (k, at, 0, 0)))
    return pl.pallas_call(
        functools.partial(pack_gauss, steps=steps),
        out_shape=jax.ShapeDtypeStruct((steps, 16, GAUSS_LANES), jnp.bfloat16),
        grid=(1,),
        in_specs=specs + [pl.BlockSpec(memory_space=pl.ANY)] * len(after),
        out_specs=pl.BlockSpec(memory_space=pltpu.VMEM),
        compiler_params=pltpu.CompilerParams(vmem_limit_bytes=10 << 20),
        cost_estimate=pl.CostEstimate(flops=0, bytes_accessed=count * 100000, transcendentals=0),
        name="pack_gauss",
    )(*[own] * (2 * steps), *after)


def sums_kernel(spot_ref, order_ref, decay_ref, cycle_ref, own_ref, other_ref, main_ref, tail_ref,
                far_ref, *rest, base):
    keep_ref, send_ref, gs_ref, gn_ref, table_ref, mate_ref, angle_ref = rest[-7:]
    step = pl.program_id(0)
    half = spot_ref[0] // 2
    odd = spot_ref[0] % 2 == 1
    first = (half * START).astype(jnp.float32)
    degree = lax.broadcasted_iota(jnp.int32, (1, WIDE), 1).astype(jnp.float32) + first

    @pl.when(step == 0)
    def _():
        gs_ref[...] = jnp.zeros_like(gs_ref)
        gn_ref[...] = jnp.zeros_like(gn_ref)
        table_ref[...] = jnp.zeros_like(table_ref)
        digits = far_ref[0, :, CYCLE_LANE:CYCLE_LANE + 2].astype(jnp.float32)
        mates = digits[:, 0:1] * 64.0 + digits[:, 1:2]
        cycles = jnp.broadcast_to(mates, (16, 128)).T[0:8, :]
        cycles = jnp.concatenate([jnp.zeros((8, 16), jnp.float32), cycles], 1)
        lane = lax.broadcasted_iota(jnp.int32, (8, 32), 1)
        for i in range(16):
            cycles = jnp.where(lane == i, cycle_ref[i].astype(jnp.float32), cycles)
        theta = math.pi * (cycles + 0.5) / ORDERS
        angle_ref[0] = jnp.cos(theta)
        angle_ref[1] = 1.0 / jnp.sin(theta)

    for o in range(GROUP):
        for k in range(2):
            j = k * GROUP + o
            mate_ref[k, o, :, 0:640] = other_ref[0, :, 640 * j:640 * (j + 1)]
            mate_ref[k, o, :, 640:720] = other_ref[0, :, GAUSS_TAIL + 80 * j:GAUSS_TAIL + 80 * (j + 1)]
        table_ref[o, 0:16, 0:START] = main_ref[o]
        table_ref[o, 0:16, START:KEPT] = tail_ref[o, :, 0:64]
        table_ref[o, 16:32, 0:START] = far_ref[0, :, START * o:START * (o + 1)]
        table_ref[o, 16:32, START:KEPT] = far_ref[0, :, PANEL_TAIL + 64 * o:PANEL_TAIL + 64 * (o + 1)]
    low = jnp.where(odd, mate_ref[...], own_ref[...])
    high = jnp.where(odd, own_ref[...], mate_ref[...])

    @pl.when(half == 0)
    def _():
        gs_ref[:, :, :, 0:720] = low
        gs_ref[:, :, :, 720:1440] = high
        gn_ref[:, :, :, 0:719] = low[:, :, :, 1:]
        gn_ref[:, :, :, 719:1439] = high

    @pl.when(half == 1)
    def _():
        gs_ref[:, :, :, 32:752] = low
        gs_ref[:, :, :, 752:1472] = high
        gn_ref[:, :, :, 31:751] = low
        gn_ref[:, :, :, 751:1471] = high

    cosine = angle_ref[0, 0:1]
    inverse = angle_ref[1, 0:1]
    orders = [order_ref[base + step * GROUP + o].astype(jnp.float32) for o in range(GROUP)]
    sums = []
    for o in range(GROUP):
        gap = jnp.maximum((degree + 1.0) * (degree + 1.0) - orders[o] * orders[o], 0.0)
        slope = decay_ref[2] * jnp.sqrt(gap)
        g = [gs_ref[k, o].astype(jnp.float32) for k in range(2)]
        n = [gn_ref[k, o].astype(jnp.float32) for k in range(2)]
        weights = jnp.concatenate(
            [g[0] * decay_ref[1], g[1] * decay_ref[1], g[0] * decay_ref[0], g[1] * decay_ref[0],
             n[0] * slope, n[1] * slope], 0).astype(jnp.bfloat16)
        sums.append(lax.dot_general(
            weights, table_ref[o], (((1,), (1,)), ((), ())), preferred_element_type=jnp.float32))
    mixed = []
    for o in range(GROUP):
        main, bare, tilt = sums[o][0:32], sums[o][32:64], sums[o][64:96]
        polar = (tilt - cosine * (main - bare)) * inverse
        bare = orders[o] * inverse * bare
        mixed.append(jnp.concatenate([main, polar, -bare[16:32], bare[0:16]], 0).T)
    for o in range(GROUP):
        keep_ref[o] = mixed[o][:16]
        send_ref[o] = mixed[o][16:].astype(jnp.bfloat16)


def partial_sums(spot, orders, decay, cycle, own, other, panel, far, after, base, count, place, size, begun):
    skip = base // GROUP
    into = place // GROUP
    total = begun[0].shape[0] if begun else size
    smem = pl.BlockSpec(memory_space=pltpu.SMEM)
    here = pl.BlockSpec(memory_space=pltpu.VMEM)
    out = pl.BlockSpec((GROUP, 16, 96), lambda i, spot: (i + into, 0, 0))
    return pl.pallas_call(
        functools.partial(sums_kernel, base=base),
        out_shape=[jax.ShapeDtypeStruct((total, 16, 96), jnp.float32),
                   jax.ShapeDtypeStruct((total, 16, 96), jnp.bfloat16)],
        input_output_aliases={9: 0, 10: 1} if begun else {},
        grid_spec=pltpu.PrefetchScalarGridSpec(
            num_scalar_prefetch=1,
            grid=(count // GROUP,),
            in_specs=[
                smem, here, smem,
                pl.BlockSpec((2, GROUP, 16, QUARTER), lambda i, spot: (0, i + skip, 0, 0)),
                here if count == GROUP else pl.BlockSpec((1, 16, GAUSS_LANES), lambda i, spot: (i, 0, 0)),
            ] + panel_specs(skip, lambda blk: blk // 2)
            + [here if count == GROUP else pl.BlockSpec((1, 16, PANEL_LANES), lambda i, spot: (i, 0, 0))]
            + [pl.BlockSpec(memory_space=pl.ANY)] * (len(begun) + len(after)),
            out_specs=[out, out],
            scratch_shapes=[
                pltpu.VMEM((2, GROUP, 16, WIDE), jnp.bfloat16),
                pltpu.VMEM((2, GROUP, 16, WIDE), jnp.bfloat16),
                pltpu.VMEM((GROUP, 32, WIDE), jnp.bfloat16),
                pltpu.VMEM((2, GROUP, 16, QUARTER), jnp.bfloat16),
                pltpu.VMEM((2, 8, 32), jnp.float32),
            ],
        ),
        compiler_params=pltpu.CompilerParams(vmem_limit_bytes=16 << 20),
        cost_estimate=pl.CostEstimate(
            flops=count * 32 * 128 * WIDE * 2, bytes_accessed=count * 200000, transcendentals=0),
        name="partial_sums",
    )(spot, orders, decay, cycle, own, other, panel, panel, far, *begun, *after)


def turn(phase, period):
    angle = (phase % period).astype(jnp.float32) * (2.0 * math.pi / period)
    return jnp.cos(angle), jnp.sin(angle)


def body(panel, gauss, height, order_map, cycle_map):
    count, cycles, _ = panel.shape
    shells = height.shape[0]
    here = lax.axis_index("ord")
    spot = lax.axis_index("blk").astype(jnp.int32).reshape(1)
    own = jnp.transpose(gauss, (0, 2, 1, 3))
    own = pltpu.with_memory_space_constraint(own, pltpu.HBM)
    panel = pltpu.with_memory_space_constraint(panel, pltpu.HBM)
    cycle_row = pltpu.with_memory_space_constraint(cycle_map[None, :], pltpu.HBM)
    spans = list(zip(CHUNKS[:-1], CHUNKS[1:]))
    orders_int = lax.dynamic_slice_in_dim(order_map, here * count, count, 0)
    degree = (spot // 2 * START + jnp.arange(WIDE)).astype(jnp.float32)[None, :]
    here_ = jnp.exp(-(degree + 2.0) * height[:, None] / ORDERS)
    next_ = jnp.exp(-(degree + 3.0) * height[:, None] / ORDERS)
    decay = jnp.stack([here_, here_ * (degree + 1.0), next_])
    packed, kept, sent, added = [], [], [], []

    def start(c):
        a, b = spans[c]
        after = (kept[0:1] if c >= 2 else []) + ([packed[-1][2]] if packed else [])
        part = packed_panel(spot, cycle_row, panel, after, a, b - a)
        far = lax.ppermute(part, "blk", PANEL_PAIRS)
        coef = packed_gauss(own, [part], a, b - a)
        packed.append((lax.ppermute(coef, "blk", GAUSS_PAIRS), far, coef))

    start(0)
    start(1)
    for c, (a, b) in enumerate(spans):
        begun = [kept.pop(), sent.pop()] if c >= 2 else []
        size = CHUNKS[4] - CHUNKS[1] if c == 1 else b - a
        after = kept[-1:] + (added if c == 3 else [])
        keep, send = partial_sums(
            spot, orders_int, decay, cycle_map, own, packed[c][0], panel, packed[c][1],
            after, a, b - a, a - CHUNKS[1] if c else 0, size, begun)
        kept.append(keep)
        sent.append(send)
        if c in (0, 3):
            added.append(lax.ppermute(send, "blk", PANEL_PAIRS))
        if c < 2:
            start(c + 2)
    total = jnp.concatenate(kept, 0) + jnp.concatenate(added, 0).astype(jnp.float32)
    total = lax.optimization_barrier(total.astype(jnp.bfloat16))
    split = (count, cycles, 3, 2, 4, shells // 4)
    chunk = jnp.transpose(total.reshape(split), (1, 4, 3, 2, 5, 0))

    parts = ORDERS // count
    items = cycles * 3 * shells // parts
    runs = order_map[::RUN] // RUN
    b = jnp.arange(128)
    q = jnp.arange(RUN)
    cos1, sin1 = turn(b[:, None] * runs[None, :], 128)
    table = jnp.concatenate(
        [jnp.concatenate([cos1, sin1], 1), jnp.concatenate([sin1, -cos1], 1)], 0)
    cos2, sin2 = turn(b[:, None] * q[None, :], NLON)
    cos3, sin3 = turn(q[:, None] * q[None, :], RUN)
    last = jnp.concatenate([cos3, -sin3], 1)

    chunk = chunk.reshape(parts, 2, items * count)
    chunk, table, cos2, sin2, last = lax.optimization_barrier((chunk, table, cos2, sin2, last))
    spread = lax.all_to_all(chunk, "ord", 0, 0, tiled=True).astype(jnp.float32)
    flat = jnp.concatenate([spread[:, 0], spread[:, 1]], 0)
    mid = jnp.dot(table, flat, precision=lax.Precision.HIGHEST).reshape(2, 128, items, count)
    cos2, sin2 = cos2[:, None, :], sin2[:, None, :]
    real = mid[0] * cos2 - mid[1] * sin2
    imag = mid[0] * sin2 + mid[1] * cos2
    field = lax.dot_general(
        last, jnp.concatenate([real, imag], 2),
        (((1,), (2,)), ((), ())), precision=lax.Precision.HIGHEST)
    field = field.reshape(parts, NLON // parts, 3, shells // 4).astype(jnp.bfloat16)
    field = jnp.transpose(field, (0, 2, 3, 1)).reshape(parts * 3, shells // 4, NLON // parts)
    field = lax.all_to_all(field, "ord", 0, 0, tiled=True)
    field = field.reshape(cycles, 4, 3, shells // 4, NLON // parts)
    return jnp.transpose(field, (4, 0, 2, 1, 3)).reshape(NLON // parts, cycles * 3 * shells)


def solution(mesh):
    return jax.shard_map(
        body,
        mesh=mesh,
        in_specs=(P("ord", "blk", None), P(None, None, "ord", "blk"), P(), P(), P("blk")),
        out_specs=P("ord", "blk"),
        check_vma=False,
    )
```

```python
import functools
import math

import jax
import jax.numpy as jnp
from jax import lax
from jax.experimental import pallas as pl
from jax.experimental.pallas import tpu as pltpu
from jax.sharding import PartitionSpec as P

ORDERS = 2880
RUN = 45
QUARTER = 720
START = 1408
WIDE = 1536
KEPT = 1472
NLON = 5760
GROUP = 5
CHUNKS = (0, 15, 30, 40, 45)
GAUSS_TAIL = 2 * GROUP * 640
GAUSS_LANES = GAUSS_TAIL + 896
PANEL_TAIL = GROUP * START
PANEL_LANES = PANEL_TAIL + 384
CYCLE_LANE = PANEL_TAIL + 320
GAUSS_PAIRS = [(0, 1), (1, 0), (2, 3), (3, 2)]
PANEL_PAIRS = [(1, 2), (2, 1), (3, 0), (0, 3)]


def pack_panel(spot_ref, cycle_ref, *rest, steps):
    out_ref = rest[-1]
    cycle = cycle_ref[...]
    row = lax.broadcasted_iota(jnp.int32, (16, 16), 0)
    lane = lax.broadcasted_iota(jnp.int32, (16, 16), 1)
    digits = []
    for digit in (cycle // 64, cycle % 64):
        spread = jnp.broadcast_to(digit.astype(jnp.float32), (16, 16))
        digits.append(jnp.sum(jnp.where(row == lane, spread, 0.0), 1, keepdims=True))
    digits = jnp.concatenate(digits, 1).astype(jnp.bfloat16)
    for g in range(steps):
        main_ref, tail_ref = rest[2 * g:2 * g + 2]
        out_ref[g, :, CYCLE_LANE:CYCLE_LANE + 2] = digits
        for o in range(GROUP):
            out_ref[g, :, START * o:START * (o + 1)] = main_ref[o]
            out_ref[g, :, PANEL_TAIL + 64 * o:PANEL_TAIL + 64 * (o + 1)] = tail_ref[o, :, 0:64]


def pack_gauss(*rest, steps):
    out_ref = rest[-1]
    for g in range(steps):
        for k in range(2):
            for o in range(GROUP):
                j = k * GROUP + o
                plane = rest[2 * g + k]
                out_ref[g, :, 640 * j:640 * (j + 1)] = plane[0, o, :, 0:640]
                out_ref[g, :, GAUSS_TAIL + 80 * j:GAUSS_TAIL + 80 * (j + 1)] = plane[0, o, :, 640:720]


def panel_specs(skip, upper):
    return [
        pl.BlockSpec((GROUP, 16, START), lambda i, spot: (i + skip, 0, upper(spot[0]))),
        pl.BlockSpec((GROUP, 16, 128), lambda i, spot: (i + skip, 0, 11 + 11 * upper(spot[0]))),
    ]


def packed_panel(spot, cycle, panel, after, base, count):
    steps = count // GROUP
    specs = []
    for g in range(steps):
        specs += panel_specs(base // GROUP + g, lambda blk: 1 - blk // 2)
    return pl.pallas_call(
        functools.partial(pack_panel, steps=steps),
        out_shape=jax.ShapeDtypeStruct((steps, 16, PANEL_LANES), jnp.bfloat16),
        grid_spec=pltpu.PrefetchScalarGridSpec(
            num_scalar_prefetch=1,
            grid=(1,),
            in_specs=[pl.BlockSpec((1, 16), lambda i, spot: (0, 0))] + specs
            + [pl.BlockSpec(memory_space=pl.ANY)] * len(after),
            out_specs=pl.BlockSpec(memory_space=pltpu.VMEM),
        ),
        compiler_params=pltpu.CompilerParams(vmem_limit_bytes=10 << 20),
        cost_estimate=pl.CostEstimate(flops=0, bytes_accessed=count * 100000, transcendentals=0),
        name="pack_panel",
    )(spot, cycle, *[panel] * (2 * steps), *after)


def packed_gauss(own, after, base, count):
    steps, skip = count // GROUP, base // GROUP
    specs = []
    for g in range(steps):
        for k in range(2):
            specs.append(pl.BlockSpec(
                (1, GROUP, 16, QUARTER), lambda i, k=k, at=skip + g: (k, at, 0, 0)))
    return pl.pallas_call(
        functools.partial(pack_gauss, steps=steps),
        out_shape=jax.ShapeDtypeStruct((steps, 16, GAUSS_LANES), jnp.bfloat16),
        grid=(1,),
        in_specs=specs + [pl.BlockSpec(memory_space=pl.ANY)] * len(after),
        out_specs=pl.BlockSpec(memory_space=pltpu.VMEM),
        compiler_params=pltpu.CompilerParams(vmem_limit_bytes=10 << 20),
        cost_estimate=pl.CostEstimate(flops=0, bytes_accessed=count * 100000, transcendentals=0),
        name="pack_gauss",
    )(*[own] * (2 * steps), *after)


def sums_kernel(spot_ref, order_ref, decay_ref, cycle_ref, own_ref, other_ref, main_ref, tail_ref,
                far_ref, *rest, base):
    keep_ref, send_ref, gs_ref, gn_ref, table_ref, mate_ref, angle_ref = rest[-7:]
    step = pl.program_id(0)
    half = spot_ref[0] // 2
    odd = spot_ref[0] % 2 == 1
    first = (half * START).astype(jnp.float32)
    degree = lax.broadcasted_iota(jnp.int32, (1, WIDE), 1).astype(jnp.float32) + first

    @pl.when(step == 0)
    def _():
        gs_ref[...] = jnp.zeros_like(gs_ref)
        gn_ref[...] = jnp.zeros_like(gn_ref)
        table_ref[...] = jnp.zeros_like(table_ref)
        digits = far_ref[0, :, CYCLE_LANE:CYCLE_LANE + 2].astype(jnp.float32)
        mates = digits[:, 0:1] * 64.0 + digits[:, 1:2]
        cycles = jnp.broadcast_to(mates, (16, 128)).T[0:8, :]
        cycles = jnp.concatenate([jnp.zeros((8, 16), jnp.float32), cycles], 1)
        lane = lax.broadcasted_iota(jnp.int32, (8, 32), 1)
        for i in range(16):
            cycles = jnp.where(lane == i, cycle_ref[i].astype(jnp.float32), cycles)
        theta = math.pi * (cycles + 0.5) / ORDERS
        angle_ref[0] = jnp.cos(theta)
        angle_ref[1] = 1.0 / jnp.sin(theta)

    for o in range(GROUP):
        for k in range(2):
            j = k * GROUP + o
            mate_ref[k, o, :, 0:640] = other_ref[0, :, 640 * j:640 * (j + 1)]
            mate_ref[k, o, :, 640:720] = other_ref[0, :, GAUSS_TAIL + 80 * j:GAUSS_TAIL + 80 * (j + 1)]
        table_ref[o, 0:16, 0:START] = main_ref[o]
        table_ref[o, 0:16, START:KEPT] = tail_ref[o, :, 0:64]
        table_ref[o, 16:32, 0:START] = far_ref[0, :, START * o:START * (o + 1)]
        table_ref[o, 16:32, START:KEPT] = far_ref[0, :, PANEL_TAIL + 64 * o:PANEL_TAIL + 64 * (o + 1)]
    low = jnp.where(odd, mate_ref[...], own_ref[...])
    high = jnp.where(odd, own_ref[...], mate_ref[...])

    @pl.when(half == 0)
    def _():
        gs_ref[:, :, :, 0:720] = low
        gs_ref[:, :, :, 720:1440] = high
        gn_ref[:, :, :, 0:719] = low[:, :, :, 1:]
        gn_ref[:, :, :, 719:1439] = high

    @pl.when(half == 1)
    def _():
        gs_ref[:, :, :, 32:752] = low
        gs_ref[:, :, :, 752:1472] = high
        gn_ref[:, :, :, 31:751] = low
        gn_ref[:, :, :, 751:1471] = high

    cosine = angle_ref[0, 0:1]
    inverse = angle_ref[1, 0:1]
    orders = [order_ref[base + step * GROUP + o].astype(jnp.float32) for o in range(GROUP)]
    sums = []
    for o in range(GROUP):
        gap = jnp.maximum((degree + 1.0) * (degree + 1.0) - orders[o] * orders[o], 0.0)
        slope = decay_ref[2] * jnp.sqrt(gap)
        g = [gs_ref[k, o].astype(jnp.float32) for k in range(2)]
        n = [gn_ref[k, o].astype(jnp.float32) for k in range(2)]
        weights = jnp.concatenate(
            [g[0] * decay_ref[1], g[1] * decay_ref[1], g[0] * decay_ref[0], g[1] * decay_ref[0],
             n[0] * slope, n[1] * slope], 0).astype(jnp.bfloat16)
        sums.append(lax.dot_general(
            weights, table_ref[o], (((1,), (1,)), ((), ())), preferred_element_type=jnp.float32))
    mixed = []
    for o in range(GROUP):
        main, bare, tilt = sums[o][0:32], sums[o][32:64], sums[o][64:96]
        polar = (tilt - cosine * (main - bare)) * inverse
        bare = orders[o] * inverse * bare
        mixed.append(jnp.concatenate([main, polar, -bare[16:32], bare[0:16]], 0).T)
    for o in range(GROUP):
        keep_ref[o] = mixed[o][:16]
        send_ref[o] = mixed[o][16:].astype(jnp.bfloat16)


def partial_sums(spot, orders, decay, cycle, own, other, panel, far, after, base, count, place, size, begun):
    skip = base // GROUP
    into = place // GROUP
    total = begun[0].shape[0] if begun else size
    smem = pl.BlockSpec(memory_space=pltpu.SMEM)
    here = pl.BlockSpec(memory_space=pltpu.VMEM)
    out = pl.BlockSpec((GROUP, 16, 96), lambda i, spot: (i + into, 0, 0))
    return pl.pallas_call(
        functools.partial(sums_kernel, base=base),
        out_shape=[jax.ShapeDtypeStruct((total, 16, 96), jnp.float32),
                   jax.ShapeDtypeStruct((total, 16, 96), jnp.bfloat16)],
        input_output_aliases={9: 0, 10: 1} if begun else {},
        grid_spec=pltpu.PrefetchScalarGridSpec(
            num_scalar_prefetch=1,
            grid=(count // GROUP,),
            in_specs=[
                smem, here, smem,
                pl.BlockSpec((2, GROUP, 16, QUARTER), lambda i, spot: (0, i + skip, 0, 0)),
                here if count == GROUP else pl.BlockSpec((1, 16, GAUSS_LANES), lambda i, spot: (i, 0, 0)),
            ] + panel_specs(skip, lambda blk: blk // 2)
            + [here if count == GROUP else pl.BlockSpec((1, 16, PANEL_LANES), lambda i, spot: (i, 0, 0))]
            + [pl.BlockSpec(memory_space=pl.ANY)] * (len(begun) + len(after)),
            out_specs=[out, out],
            scratch_shapes=[
                pltpu.VMEM((2, GROUP, 16, WIDE), jnp.bfloat16),
                pltpu.VMEM((2, GROUP, 16, WIDE), jnp.bfloat16),
                pltpu.VMEM((GROUP, 32, WIDE), jnp.bfloat16),
                pltpu.VMEM((2, GROUP, 16, QUARTER), jnp.bfloat16),
                pltpu.VMEM((2, 8, 32), jnp.float32),
            ],
        ),
        compiler_params=pltpu.CompilerParams(vmem_limit_bytes=16 << 20),
        cost_estimate=pl.CostEstimate(
            flops=count * 32 * 128 * WIDE * 2, bytes_accessed=count * 200000, transcendentals=0),
        name="partial_sums",
    )(spot, orders, decay, cycle, own, other, panel, panel, far, *begun, *after)


def turn(phase, period):
    angle = (phase % period).astype(jnp.float32) * (2.0 * math.pi / period)
    return jnp.cos(angle), jnp.sin(angle)


def body(panel, gauss, height, order_map, cycle_map):
    count, cycles, _ = panel.shape
    shells = height.shape[0]
    here = lax.axis_index("ord")
    spot = lax.axis_index("blk").astype(jnp.int32).reshape(1)
    own = jnp.transpose(gauss, (0, 2, 1, 3))
    own = pltpu.with_memory_space_constraint(own, pltpu.HBM)
    panel = pltpu.with_memory_space_constraint(panel, pltpu.HBM)
    cycle_row = pltpu.with_memory_space_constraint(cycle_map[None, :], pltpu.HBM)
    spans = list(zip(CHUNKS[:-1], CHUNKS[1:]))
    orders_int = lax.dynamic_slice_in_dim(order_map, here * count, count, 0)
    degree = (spot // 2 * START + jnp.arange(WIDE)).astype(jnp.float32)[None, :]
    here_ = jnp.exp(-(degree + 2.0) * height[:, None] / ORDERS)
    next_ = jnp.exp(-(degree + 3.0) * height[:, None] / ORDERS)
    decay = jnp.stack([here_, here_ * (degree + 1.0), next_])
    packed, kept, sent, added = [], [], [], []

    def start(c):
        a, b = spans[c]
        after = (kept[0:1] if c >= 2 else []) + ([packed[-1][2]] if packed else [])
        part = packed_panel(spot, cycle_row, panel, after, a, b - a)
        far = lax.ppermute(part, "blk", PANEL_PAIRS)
        coef = packed_gauss(own, [part], a, b - a)
        packed.append((lax.ppermute(coef, "blk", GAUSS_PAIRS), far, coef))

    start(0)
    start(1)
    for c, (a, b) in enumerate(spans):
        begun = [kept.pop(), sent.pop()] if c >= 2 else []
        size = CHUNKS[4] - CHUNKS[1] if c == 1 else b - a
        after = kept[-1:] + (added if c == 3 else [])
        keep, send = partial_sums(
            spot, orders_int, decay, cycle_map, own, packed[c][0], panel, packed[c][1],
            after, a, b - a, a - CHUNKS[1] if c else 0, size, begun)
        kept.append(keep)
        sent.append(send)
        if c in (0, 3):
            added.append(lax.ppermute(send, "blk", PANEL_PAIRS))
        if c < 2:
            start(c + 2)
    total = jnp.concatenate(kept, 0) + jnp.concatenate(added, 0).astype(jnp.float32)
    total = lax.optimization_barrier(total.astype(jnp.bfloat16))
    split = (count, cycles, 3, 2, 4, shells // 4)
    chunk = jnp.transpose(total.reshape(split), (1, 4, 3, 2, 5, 0))

    parts = ORDERS // count
    items = cycles * 3 * shells // parts
    runs = order_map[::RUN] // RUN
    b = jnp.arange(128)
    q = jnp.arange(RUN)
    cos1, sin1 = turn(b[:, None] * runs[None, :], 128)
    table = jnp.concatenate([jnp.stack([cos1, sin1], 2), jnp.stack([sin1, -cos1], 2)], 0)
    table = table.reshape(256, 2 * parts).astype(jnp.bfloat16)
    cos2, sin2 = turn(b[:, None] * q[None, :], NLON)
    cos3, sin3 = turn(q[:, None] * q[None, :], RUN)
    last = jnp.concatenate([cos3, -sin3], 1)

    chunk = chunk.reshape(parts, 2, items * count)
    chunk, table, cos2, sin2, last = lax.optimization_barrier((chunk, table, cos2, sin2, last))
    flat = lax.all_to_all(chunk, "ord", 0, 0, tiled=True).reshape(2 * parts, items * count)
    mid = jnp.dot(table, flat, preferred_element_type=jnp.float32).reshape(2, 128, items, count)
    cos2, sin2 = cos2[:, None, :], sin2[:, None, :]
    real = mid[0] * cos2 - mid[1] * sin2
    imag = mid[0] * sin2 + mid[1] * cos2
    field = lax.dot_general(
        last, jnp.concatenate([real, imag], 2),
        (((1,), (2,)), ((), ())), precision=lax.Precision.HIGH)
    field = field.reshape(parts, NLON // parts, 3, shells // 4).astype(jnp.bfloat16)
    field = jnp.transpose(field, (0, 2, 3, 1)).reshape(parts * 3, shells // 4, NLON // parts)
    field = lax.all_to_all(field, "ord", 0, 0, tiled=True)
    field = field.reshape(cycles, 4, 3, shells // 4, NLON // parts)
    return jnp.transpose(field, (4, 0, 2, 1, 3)).reshape(NLON // parts, cycles * 3 * shells)


def solution(mesh):
    return jax.shard_map(
        body,
        mesh=mesh,
        in_specs=(P("ord", "blk", None), P(None, None, "ord", "blk"), P(), P(), P("blk")),
        out_specs=P("ord", "blk"),
        check_vma=False,
    )
```

```python
import functools
import math

import jax
import jax.numpy as jnp
from jax import lax
from jax.experimental import pallas as pl
from jax.experimental.pallas import tpu as pltpu
from jax.sharding import PartitionSpec as P

ORDERS = 2880
RUN = 45
QUARTER = 720
START = 1408
WIDE = 1536
KEPT = 1472
NLON = 5760
GROUP = 5
CHUNKS = (0, 15, 30, 40, 45)
GAUSS_TAIL = 2 * GROUP * 640
GAUSS_LANES = GAUSS_TAIL + 896
PANEL_TAIL = GROUP * START
PANEL_LANES = PANEL_TAIL + 384
CYCLE_LANE = PANEL_TAIL + 320
GAUSS_PAIRS = [(0, 1), (1, 0), (2, 3), (3, 2)]
PANEL_PAIRS = [(1, 2), (2, 1), (3, 0), (0, 3)]


def pack_panel(spot_ref, cycle_ref, *rest, steps):
    out_ref = rest[-1]
    cycle = cycle_ref[...]
    row = lax.broadcasted_iota(jnp.int32, (16, 16), 0)
    lane = lax.broadcasted_iota(jnp.int32, (16, 16), 1)
    digits = []
    for digit in (cycle // 64, cycle % 64):
        spread = jnp.broadcast_to(digit.astype(jnp.float32), (16, 16))
        digits.append(jnp.sum(jnp.where(row == lane, spread, 0.0), 1, keepdims=True))
    digits = jnp.concatenate(digits, 1).astype(jnp.bfloat16)
    for g in range(steps):
        main_ref, tail_ref = rest[2 * g:2 * g + 2]
        out_ref[g, :, CYCLE_LANE:CYCLE_LANE + 2] = digits
        for o in range(GROUP):
            out_ref[g, :, START * o:START * (o + 1)] = main_ref[o]
            out_ref[g, :, PANEL_TAIL + 64 * o:PANEL_TAIL + 64 * (o + 1)] = tail_ref[o, :, 0:64]


def pack_gauss(*rest, steps):
    out_ref = rest[-1]
    for g in range(steps):
        for k in range(2):
            for o in range(GROUP):
                j = k * GROUP + o
                plane = rest[2 * g + k]
                out_ref[g, :, 640 * j:640 * (j + 1)] = plane[0, o, :, 0:640]
                out_ref[g, :, GAUSS_TAIL + 80 * j:GAUSS_TAIL + 80 * (j + 1)] = plane[0, o, :, 640:720]


def panel_specs(skip, upper):
    return [
        pl.BlockSpec((GROUP, 16, START), lambda i, spot: (i + skip, 0, upper(spot[0]))),
        pl.BlockSpec((GROUP, 16, 128), lambda i, spot: (i + skip, 0, 11 + 11 * upper(spot[0]))),
    ]


def packed_panel(spot, cycle, panel, after, base, count):
    steps = count // GROUP
    specs = []
    for g in range(steps):
        specs += panel_specs(base // GROUP + g, lambda blk: 1 - blk // 2)
    return pl.pallas_call(
        functools.partial(pack_panel, steps=steps),
        out_shape=jax.ShapeDtypeStruct((steps, 16, PANEL_LANES), jnp.bfloat16),
        grid_spec=pltpu.PrefetchScalarGridSpec(
            num_scalar_prefetch=1,
            grid=(1,),
            in_specs=[pl.BlockSpec((1, 16), lambda i, spot: (0, 0))] + specs
            + [pl.BlockSpec(memory_space=pl.ANY)] * len(after),
            out_specs=pl.BlockSpec(memory_space=pltpu.VMEM),
        ),
        compiler_params=pltpu.CompilerParams(vmem_limit_bytes=10 << 20),
        cost_estimate=pl.CostEstimate(flops=0, bytes_accessed=count * 100000, transcendentals=0),
        name="pack_panel",
    )(spot, cycle, *[panel] * (2 * steps), *after)


def packed_gauss(own, after, base, count):
    steps, skip = count // GROUP, base // GROUP
    specs = []
    for g in range(steps):
        for k in range(2):
            specs.append(pl.BlockSpec(
                (1, GROUP, 16, QUARTER), lambda i, k=k, at=skip + g: (k, at, 0, 0)))
    return pl.pallas_call(
        functools.partial(pack_gauss, steps=steps),
        out_shape=jax.ShapeDtypeStruct((steps, 16, GAUSS_LANES), jnp.bfloat16),
        grid=(1,),
        in_specs=specs + [pl.BlockSpec(memory_space=pl.ANY)] * len(after),
        out_specs=pl.BlockSpec(memory_space=pltpu.VMEM),
        compiler_params=pltpu.CompilerParams(vmem_limit_bytes=10 << 20),
        cost_estimate=pl.CostEstimate(flops=0, bytes_accessed=count * 100000, transcendentals=0),
        name="pack_gauss",
    )(*[own] * (2 * steps), *after)


def sums_kernel(spot_ref, order_ref, decay_ref, cycle_ref, own_ref, other_ref, main_ref, tail_ref,
                far_ref, *rest, base):
    keep_ref, send_ref, gs_ref, gn_ref, table_ref, mate_ref, angle_ref = rest[-7:]
    step = pl.program_id(0)
    half = spot_ref[0] // 2
    odd = spot_ref[0] % 2 == 1
    first = (half * START).astype(jnp.float32)
    degree = lax.broadcasted_iota(jnp.int32, (1, WIDE), 1).astype(jnp.float32) + first

    @pl.when(step == 0)
    def _():
        gs_ref[...] = jnp.zeros_like(gs_ref)
        gn_ref[...] = jnp.zeros_like(gn_ref)
        table_ref[...] = jnp.zeros_like(table_ref)
        digits = far_ref[0, :, CYCLE_LANE:CYCLE_LANE + 2].astype(jnp.float32)
        mates = digits[:, 0:1] * 64.0 + digits[:, 1:2]
        cycles = jnp.broadcast_to(mates, (16, 128)).T[0:8, :]
        cycles = jnp.concatenate([jnp.zeros((8, 16), jnp.float32), cycles], 1)
        lane = lax.broadcasted_iota(jnp.int32, (8, 32), 1)
        for i in range(16):
            cycles = jnp.where(lane == i, cycle_ref[i].astype(jnp.float32), cycles)
        theta = math.pi * (cycles + 0.5) / ORDERS
        angle_ref[0] = jnp.cos(theta)
        angle_ref[1] = 1.0 / jnp.sin(theta)

    for o in range(GROUP):
        for k in range(2):
            j = k * GROUP + o
            mate_ref[k, o, :, 0:640] = other_ref[0, :, 640 * j:640 * (j + 1)]
            mate_ref[k, o, :, 640:720] = other_ref[0, :, GAUSS_TAIL + 80 * j:GAUSS_TAIL + 80 * (j + 1)]
        table_ref[o, 0:16, 0:START] = main_ref[o]
        table_ref[o, 0:16, START:KEPT] = tail_ref[o, :, 0:64]
        table_ref[o, 16:32, 0:START] = far_ref[0, :, START * o:START * (o + 1)]
        table_ref[o, 16:32, START:KEPT] = far_ref[0, :, PANEL_TAIL + 64 * o:PANEL_TAIL + 64 * (o + 1)]
    low = jnp.where(odd, mate_ref[...], own_ref[...])
    high = jnp.where(odd, own_ref[...], mate_ref[...])

    @pl.when(half == 0)
    def _():
        gs_ref[:, :, :, 0:720] = low
        gs_ref[:, :, :, 720:1440] = high
        gn_ref[:, :, :, 0:719] = low[:, :, :, 1:]
        gn_ref[:, :, :, 719:1439] = high

    @pl.when(half == 1)
    def _():
        gs_ref[:, :, :, 32:752] = low
        gs_ref[:, :, :, 752:1472] = high
        gn_ref[:, :, :, 31:751] = low
        gn_ref[:, :, :, 751:1471] = high

    cosine = angle_ref[0, 0:1]
    inverse = angle_ref[1, 0:1]
    orders = [order_ref[base + step * GROUP + o].astype(jnp.float32) for o in range(GROUP)]
    sums = []
    for o in range(GROUP):
        gap = jnp.maximum((degree + 1.0) * (degree + 1.0) - orders[o] * orders[o], 0.0)
        slope = decay_ref[2] * jnp.sqrt(gap)
        g = [gs_ref[k, o].astype(jnp.float32) for k in range(2)]
        n = [gn_ref[k, o].astype(jnp.float32) for k in range(2)]
        weights = jnp.concatenate(
            [g[0] * decay_ref[1], g[1] * decay_ref[1], g[0] * decay_ref[0], g[1] * decay_ref[0],
             n[0] * slope, n[1] * slope], 0).astype(jnp.bfloat16)
        sums.append(lax.dot_general(
            weights, table_ref[o], (((1,), (1,)), ((), ())), preferred_element_type=jnp.float32))
    mixed = []
    for o in range(GROUP):
        main, bare, tilt = sums[o][0:32], sums[o][32:64], sums[o][64:96]
        polar = (tilt - cosine * (main - bare)) * inverse
        bare = orders[o] * inverse * bare
        mixed.append(jnp.concatenate(
            [main[0:16], polar[0:16], -bare[16:32], main[16:32], polar[16:32], bare[0:16]], 0).T)
    for o in range(GROUP):
        keep_ref[o] = mixed[o][:16]
        send_ref[o] = mixed[o][16:].astype(jnp.bfloat16)


def partial_sums(spot, orders, decay, cycle, own, other, panel, far, after, base, count, place, size, begun):
    skip = base // GROUP
    into = place // GROUP
    total = begun[0].shape[0] if begun else size
    smem = pl.BlockSpec(memory_space=pltpu.SMEM)
    here = pl.BlockSpec(memory_space=pltpu.VMEM)
    out = pl.BlockSpec((GROUP, 16, 96), lambda i, spot: (i + into, 0, 0))
    return pl.pallas_call(
        functools.partial(sums_kernel, base=base),
        out_shape=[jax.ShapeDtypeStruct((total, 16, 96), jnp.float32),
                   jax.ShapeDtypeStruct((total, 16, 96), jnp.bfloat16)],
        input_output_aliases={9: 0, 10: 1} if begun else {},
        grid_spec=pltpu.PrefetchScalarGridSpec(
            num_scalar_prefetch=1,
            grid=(count // GROUP,),
            in_specs=[
                smem, here, smem,
                pl.BlockSpec((2, GROUP, 16, QUARTER), lambda i, spot: (0, i + skip, 0, 0)),
                here if count == GROUP else pl.BlockSpec((1, 16, GAUSS_LANES), lambda i, spot: (i, 0, 0)),
            ] + panel_specs(skip, lambda blk: blk // 2)
            + [here if count == GROUP else pl.BlockSpec((1, 16, PANEL_LANES), lambda i, spot: (i, 0, 0))]
            + [pl.BlockSpec(memory_space=pl.ANY)] * (len(begun) + len(after)),
            out_specs=[out, out],
            scratch_shapes=[
                pltpu.VMEM((2, GROUP, 16, WIDE), jnp.bfloat16),
                pltpu.VMEM((2, GROUP, 16, WIDE), jnp.bfloat16),
                pltpu.VMEM((GROUP, 32, WIDE), jnp.bfloat16),
                pltpu.VMEM((2, GROUP, 16, QUARTER), jnp.bfloat16),
                pltpu.VMEM((2, 8, 32), jnp.float32),
            ],
        ),
        compiler_params=pltpu.CompilerParams(vmem_limit_bytes=16 << 20),
        cost_estimate=pl.CostEstimate(
            flops=count * 32 * 128 * WIDE * 2, bytes_accessed=count * 200000, transcendentals=0),
        name="partial_sums",
    )(spot, orders, decay, cycle, own, other, panel, panel, far, *begun, *after)


def turn(phase, period):
    angle = (phase % period).astype(jnp.float32) * (2.0 * math.pi / period)
    return jnp.cos(angle), jnp.sin(angle)


def body(panel, gauss, height, order_map, cycle_map):
    count, cycles, _ = panel.shape
    shells = height.shape[0]
    here = lax.axis_index("ord")
    spot = lax.axis_index("blk").astype(jnp.int32).reshape(1)
    own = jnp.transpose(gauss, (0, 2, 1, 3))
    own = pltpu.with_memory_space_constraint(own, pltpu.HBM)
    panel = pltpu.with_memory_space_constraint(panel, pltpu.HBM)
    cycle_row = pltpu.with_memory_space_constraint(cycle_map[None, :], pltpu.HBM)
    spans = list(zip(CHUNKS[:-1], CHUNKS[1:]))
    orders_int = lax.dynamic_slice_in_dim(order_map, here * count, count, 0)
    degree = (spot // 2 * START + jnp.arange(WIDE)).astype(jnp.float32)[None, :]
    here_ = jnp.exp(-(degree + 2.0) * height[:, None] / ORDERS)
    next_ = jnp.exp(-(degree + 3.0) * height[:, None] / ORDERS)
    decay = jnp.stack([here_, here_ * (degree + 1.0), next_])
    packed, kept, sent, added = [], [], [], []

    def start(c):
        a, b = spans[c]
        after = (kept[0:1] if c >= 2 else []) + ([packed[-1][2]] if packed else [])
        part = packed_panel(spot, cycle_row, panel, after, a, b - a)
        far = lax.ppermute(part, "blk", PANEL_PAIRS)
        coef = packed_gauss(own, [part], a, b - a)
        packed.append((lax.ppermute(coef, "blk", GAUSS_PAIRS), far, coef))

    start(0)
    start(1)
    for c, (a, b) in enumerate(spans):
        begun = [kept.pop(), sent.pop()] if c >= 2 else []
        size = CHUNKS[4] - CHUNKS[1] if c == 1 else b - a
        after = kept[-1:] + (added if c == 3 else [])
        keep, send = partial_sums(
            spot, orders_int, decay, cycle_map, own, packed[c][0], panel, packed[c][1],
            after, a, b - a, a - CHUNKS[1] if c else 0, size, begun)
        kept.append(keep)
        sent.append(send)
        if c in (0, 3):
            added.append(lax.ppermute(send, "blk", PANEL_PAIRS))
        if c < 2:
            start(c + 2)
    total = jnp.concatenate(kept, 0) + jnp.concatenate(added, 0).astype(jnp.float32)
    total = lax.optimization_barrier(total.astype(jnp.bfloat16))
    chunk = jnp.transpose(total.reshape(count, cycles, 2, 4, 12), (1, 3, 2, 4, 0))

    parts = ORDERS // count
    items = cycles * 3 * shells // parts
    runs = order_map[::RUN] // RUN
    b = jnp.arange(128)
    q = jnp.arange(RUN)
    cos1, sin1 = turn(b[:, None] * runs[None, :], 128)
    table = jnp.concatenate([jnp.stack([cos1, sin1], 2), jnp.stack([sin1, -cos1], 2)], 0)
    table = table.reshape(256, 2 * parts).astype(jnp.bfloat16)
    cos2, sin2 = turn(b[:, None] * q[None, :], NLON)
    cos3, sin3 = turn(q[:, None] * q[None, :], RUN)
    last = jnp.concatenate([cos3, -sin3], 1)

    chunk = chunk.reshape(parts, 2, items * count)
    chunk, table, cos2, sin2, last = lax.optimization_barrier((chunk, table, cos2, sin2, last))
    flat = lax.all_to_all(chunk, "ord", 0, 0, tiled=True).reshape(2 * parts, items * count)
    mid = jnp.dot(table, flat, preferred_element_type=jnp.float32).reshape(2, 128, items, count)
    cos2, sin2 = cos2[:, None, :], sin2[:, None, :]
    real = mid[0] * cos2 - mid[1] * sin2
    imag = mid[0] * sin2 + mid[1] * cos2
    field = lax.dot_general(
        last, jnp.concatenate([real, imag], 2),
        (((1,), (2,)), ((), ())), precision=lax.Precision.HIGH)
    field = field.reshape(parts, NLON // parts, 3, 4).astype(jnp.bfloat16)
    field = jnp.transpose(field, (0, 2, 3, 1)).reshape(parts * 3, 4, NLON // parts)
    field = lax.all_to_all(field, "ord", 0, 0, tiled=True)
    return jnp.transpose(field, (2, 0, 1)).reshape(NLON // parts, cycles * 3 * shells)


def solution(mesh):
    return jax.shard_map(
        body,
        mesh=mesh,
        in_specs=(P("ord", "blk", None), P(None, None, "ord", "blk"), P(), P(), P("blk")),
        out_specs=P("ord", "blk"),
        check_vma=False,
    )
```

```python
import functools
import math

import jax
import jax.numpy as jnp
from jax import lax
from jax.experimental import pallas as pl
from jax.experimental.pallas import tpu as pltpu
from jax.sharding import PartitionSpec as P

ORDERS = 2880
RUN = 45
QUARTER = 720
START = 1408
WIDE = 1536
KEPT = 1472
NLON = 5760
GROUP = 5
CHUNKS = (0, 15, 30, 40, 45)
GAUSS_TAIL = 2 * GROUP * 640
GAUSS_LANES = GAUSS_TAIL + 896
PANEL_TAIL = GROUP * START
PANEL_LANES = PANEL_TAIL + 384
CYCLE_LANE = PANEL_TAIL + 320
GAUSS_PAIRS = [(0, 1), (1, 0), (2, 3), (3, 2)]
PANEL_PAIRS = [(1, 2), (2, 1), (3, 0), (0, 3)]


def pack_panel(spot_ref, cycle_ref, *rest, steps):
    out_ref = rest[-1]
    cycle = cycle_ref[...]
    row = lax.broadcasted_iota(jnp.int32, (16, 16), 0)
    lane = lax.broadcasted_iota(jnp.int32, (16, 16), 1)
    digits = []
    for digit in (cycle // 64, cycle % 64):
        spread = jnp.broadcast_to(digit.astype(jnp.float32), (16, 16))
        digits.append(jnp.sum(jnp.where(row == lane, spread, 0.0), 1, keepdims=True))
    digits = jnp.concatenate(digits, 1).astype(jnp.bfloat16)
    for g in range(steps):
        main_ref, tail_ref = rest[2 * g:2 * g + 2]
        out_ref[g, :, CYCLE_LANE:CYCLE_LANE + 2] = digits
        for o in range(GROUP):
            out_ref[g, :, START * o:START * (o + 1)] = main_ref[o]
            out_ref[g, :, PANEL_TAIL + 64 * o:PANEL_TAIL + 64 * (o + 1)] = tail_ref[o, :, 0:64]


def pack_gauss(*rest, steps):
    out_ref = rest[-1]
    for g in range(steps):
        for k in range(2):
            for o in range(GROUP):
                j = k * GROUP + o
                plane = rest[2 * g + k]
                out_ref[g, :, 640 * j:640 * (j + 1)] = plane[0, o, :, 0:640]
                out_ref[g, :, GAUSS_TAIL + 80 * j:GAUSS_TAIL + 80 * (j + 1)] = plane[0, o, :, 640:720]


def panel_specs(skip, upper):
    return [
        pl.BlockSpec((GROUP, 16, START), lambda i, spot: (i + skip, 0, upper(spot[0]))),
        pl.BlockSpec((GROUP, 16, 128), lambda i, spot: (i + skip, 0, 11 + 11 * upper(spot[0]))),
    ]


def packed_panel(spot, cycle, panel, after, base, count):
    steps = count // GROUP
    specs = []
    for g in range(steps):
        specs += panel_specs(base // GROUP + g, lambda blk: 1 - blk // 2)
    return pl.pallas_call(
        functools.partial(pack_panel, steps=steps),
        out_shape=jax.ShapeDtypeStruct((steps, 16, PANEL_LANES), jnp.bfloat16),
        grid_spec=pltpu.PrefetchScalarGridSpec(
            num_scalar_prefetch=1,
            grid=(1,),
            in_specs=[pl.BlockSpec((1, 16), lambda i, spot: (0, 0))] + specs
            + [pl.BlockSpec(memory_space=pl.ANY)] * len(after),
            out_specs=pl.BlockSpec(memory_space=pltpu.VMEM),
        ),
        compiler_params=pltpu.CompilerParams(vmem_limit_bytes=10 << 20),
        cost_estimate=pl.CostEstimate(flops=0, bytes_accessed=count * 100000, transcendentals=0),
        name="pack_panel",
    )(spot, cycle, *[panel] * (2 * steps), *after)


def packed_gauss(own, after, base, count):
    steps, skip = count // GROUP, base // GROUP
    specs = []
    for g in range(steps):
        for k in range(2):
            specs.append(pl.BlockSpec(
                (1, GROUP, 16, QUARTER), lambda i, k=k, at=skip + g: (k, at, 0, 0)))
    return pl.pallas_call(
        functools.partial(pack_gauss, steps=steps),
        out_shape=jax.ShapeDtypeStruct((steps, 16, GAUSS_LANES), jnp.bfloat16),
        grid=(1,),
        in_specs=specs + [pl.BlockSpec(memory_space=pl.ANY)] * len(after),
        out_specs=pl.BlockSpec(memory_space=pltpu.VMEM),
        compiler_params=pltpu.CompilerParams(vmem_limit_bytes=10 << 20),
        cost_estimate=pl.CostEstimate(flops=0, bytes_accessed=count * 100000, transcendentals=0),
        name="pack_gauss",
    )(*[own] * (2 * steps), *after)


def sums_kernel(spot_ref, order_ref, decay_ref, cycle_ref, own_ref, other_ref, main_ref, tail_ref,
                far_ref, *rest, base):
    keep_ref, send_ref, gs_ref, gn_ref, table_ref, mate_ref, angle_ref = rest[-7:]
    step = pl.program_id(0)
    half = spot_ref[0] // 2
    odd = spot_ref[0] % 2 == 1
    first = (half * START).astype(jnp.float32)
    degree = lax.broadcasted_iota(jnp.int32, (1, WIDE), 1).astype(jnp.float32) + first

    @pl.when(step == 0)
    def _():
        edge = jnp.zeros((2, GROUP, 16, 128), jnp.bfloat16)
        for ref in (gs_ref, gn_ref):
            ref[:, :, :, 0:128] = edge
            ref[:, :, :, START:WIDE] = edge
        table_ref[:, :, START:WIDE] = jnp.zeros((GROUP, 32, 128), jnp.bfloat16)
        digits = far_ref[0, :, CYCLE_LANE:CYCLE_LANE + 2].astype(jnp.float32)
        mates = digits[:, 0:1] * 64.0 + digits[:, 1:2]
        cycles = jnp.broadcast_to(mates, (16, 128)).T[0:8, :]
        cycles = jnp.concatenate([jnp.zeros((8, 16), jnp.float32), cycles], 1)
        lane = lax.broadcasted_iota(jnp.int32, (8, 32), 1)
        for i in range(16):
            cycles = jnp.where(lane == i, cycle_ref[i].astype(jnp.float32), cycles)
        theta = math.pi * (cycles + 0.5) / ORDERS
        angle_ref[0] = jnp.cos(theta)
        angle_ref[1] = 1.0 / jnp.sin(theta)

    for o in range(GROUP):
        for k in range(2):
            j = k * GROUP + o
            mate_ref[k, o, :, 0:640] = other_ref[0, :, 640 * j:640 * (j + 1)]
            mate_ref[k, o, :, 640:720] = other_ref[0, :, GAUSS_TAIL + 80 * j:GAUSS_TAIL + 80 * (j + 1)]
        table_ref[o, 0:16, 0:START] = main_ref[o]
        table_ref[o, 0:16, START:KEPT] = tail_ref[o, :, 0:64]
        table_ref[o, 16:32, 0:START] = far_ref[0, :, START * o:START * (o + 1)]
        table_ref[o, 16:32, START:KEPT] = far_ref[0, :, PANEL_TAIL + 64 * o:PANEL_TAIL + 64 * (o + 1)]
    low = jnp.where(odd, mate_ref[...], own_ref[...])
    high = jnp.where(odd, own_ref[...], mate_ref[...])

    @pl.when(half == 0)
    def _():
        gs_ref[:, :, :, 0:720] = low
        gs_ref[:, :, :, 720:1440] = high
        gn_ref[:, :, :, 0:719] = low[:, :, :, 1:]
        gn_ref[:, :, :, 719:1439] = high

    @pl.when(half == 1)
    def _():
        gs_ref[:, :, :, 32:752] = low
        gs_ref[:, :, :, 752:1472] = high
        gn_ref[:, :, :, 31:751] = low
        gn_ref[:, :, :, 751:1471] = high

    cosine = angle_ref[0, 0:1]
    inverse = angle_ref[1, 0:1]
    orders = [order_ref[base + step * GROUP + o].astype(jnp.float32) for o in range(GROUP)]
    sums = []
    for o in range(GROUP):
        gap = jnp.maximum((degree + 1.0) * (degree + 1.0) - orders[o] * orders[o], 0.0)
        slope = decay_ref[2] * jnp.sqrt(gap)
        g = [gs_ref[k, o].astype(jnp.float32) for k in range(2)]
        n = [gn_ref[k, o].astype(jnp.float32) for k in range(2)]
        weights = jnp.concatenate(
            [g[0] * decay_ref[1], g[1] * decay_ref[1], g[0] * decay_ref[0], g[1] * decay_ref[0],
             n[0] * slope, n[1] * slope], 0).astype(jnp.bfloat16)
        sums.append(lax.dot_general(
            weights, table_ref[o], (((1,), (1,)), ((), ())), preferred_element_type=jnp.float32))
    mixed = []
    for o in range(GROUP):
        main, bare, tilt = sums[o][0:32], sums[o][32:64], sums[o][64:96]
        polar = (tilt - cosine * (main - bare)) * inverse
        bare = orders[o] * inverse * bare
        mixed.append(jnp.concatenate(
            [main[0:16], polar[0:16], -bare[16:32], main[16:32], polar[16:32], bare[0:16]], 0).T)
    for o in range(GROUP):
        keep_ref[o] = mixed[o][:16]
        send_ref[o] = mixed[o][16:].astype(jnp.bfloat16)


def partial_sums(spot, orders, decay, cycle, own, other, panel, far, after, base, count, place, size, begun):
    skip = base // GROUP
    into = place // GROUP
    total = begun[0].shape[0] if begun else size
    smem = pl.BlockSpec(memory_space=pltpu.SMEM)
    here = pl.BlockSpec(memory_space=pltpu.VMEM)
    out = pl.BlockSpec((GROUP, 16, 96), lambda i, spot: (i + into, 0, 0))
    return pl.pallas_call(
        functools.partial(sums_kernel, base=base),
        out_shape=[jax.ShapeDtypeStruct((total, 16, 96), jnp.float32),
                   jax.ShapeDtypeStruct((total, 16, 96), jnp.bfloat16)],
        input_output_aliases={9: 0, 10: 1} if begun else {},
        grid_spec=pltpu.PrefetchScalarGridSpec(
            num_scalar_prefetch=1,
            grid=(count // GROUP,),
            in_specs=[
                smem, here, smem,
                pl.BlockSpec((2, GROUP, 16, QUARTER), lambda i, spot: (0, i + skip, 0, 0)),
                here if count == GROUP else pl.BlockSpec((1, 16, GAUSS_LANES), lambda i, spot: (i, 0, 0)),
            ] + panel_specs(skip, lambda blk: blk // 2)
            + [here if count == GROUP else pl.BlockSpec((1, 16, PANEL_LANES), lambda i, spot: (i, 0, 0))]
            + [pl.BlockSpec(memory_space=pl.ANY)] * (len(begun) + len(after)),
            out_specs=[out, out],
            scratch_shapes=[
                pltpu.VMEM((2, GROUP, 16, WIDE), jnp.bfloat16),
                pltpu.VMEM((2, GROUP, 16, WIDE), jnp.bfloat16),
                pltpu.VMEM((GROUP, 32, WIDE), jnp.bfloat16),
                pltpu.VMEM((2, GROUP, 16, QUARTER), jnp.bfloat16),
                pltpu.VMEM((2, 8, 32), jnp.float32),
            ],
        ),
        compiler_params=pltpu.CompilerParams(vmem_limit_bytes=16 << 20),
        cost_estimate=pl.CostEstimate(
            flops=count * 32 * 128 * WIDE * 2, bytes_accessed=count * 200000, transcendentals=0),
        name="partial_sums",
    )(spot, orders, decay, cycle, own, other, panel, panel, far, *begun, *after)


def turn(phase, period):
    angle = (phase % period).astype(jnp.float32) * (2.0 * math.pi / period)
    return jnp.cos(angle), jnp.sin(angle)


def body(panel, gauss, height, order_map, cycle_map):
    count, cycles, _ = panel.shape
    shells = height.shape[0]
    here = lax.axis_index("ord")
    spot = lax.axis_index("blk").astype(jnp.int32).reshape(1)
    own = jnp.transpose(gauss, (0, 2, 1, 3))
    own = pltpu.with_memory_space_constraint(own, pltpu.HBM)
    panel = pltpu.with_memory_space_constraint(panel, pltpu.HBM)
    cycle_row = pltpu.with_memory_space_constraint(cycle_map[None, :], pltpu.HBM)
    spans = list(zip(CHUNKS[:-1], CHUNKS[1:]))
    orders_int = lax.dynamic_slice_in_dim(order_map, here * count, count, 0)
    degree = (spot // 2 * START + jnp.arange(WIDE)).astype(jnp.float32)[None, :]
    here_ = jnp.exp(-(degree + 2.0) * height[:, None] / ORDERS)
    next_ = jnp.exp(-(degree + 3.0) * height[:, None] / ORDERS)
    decay = jnp.stack([here_, here_ * (degree + 1.0), next_])
    packed, kept, sent, added = [], [], [], []

    def start(c):
        a, b = spans[c]
        after = (kept[0:1] if c >= 2 else []) + ([packed[-1][2]] if packed else [])
        part = packed_panel(spot, cycle_row, panel, after, a, b - a)
        far = lax.ppermute(part, "blk", PANEL_PAIRS)
        coef = packed_gauss(own, [part], a, b - a)
        packed.append((lax.ppermute(coef, "blk", GAUSS_PAIRS), far, coef))

    start(0)
    start(1)
    for c, (a, b) in enumerate(spans):
        begun = [kept.pop(), sent.pop()] if c >= 2 else []
        size = CHUNKS[4] - CHUNKS[1] if c == 1 else b - a
        after = kept[-1:] + (added if c == 3 else [])
        keep, send = partial_sums(
            spot, orders_int, decay, cycle_map, own, packed[c][0], panel, packed[c][1],
            after, a, b - a, a - CHUNKS[1] if c else 0, size, begun)
        kept.append(keep)
        sent.append(send)
        if c in (0, 3):
            added.append(lax.ppermute(send, "blk", PANEL_PAIRS))
        if c < 2:
            start(c + 2)
    total = jnp.concatenate(kept, 0) + jnp.concatenate(added, 0).astype(jnp.float32)
    total = lax.optimization_barrier(total.astype(jnp.bfloat16))
    chunk = jnp.transpose(total.reshape(count, cycles, 2, 4, 12), (1, 3, 2, 4, 0))

    parts = ORDERS // count
    items = cycles * 3 * shells // parts
    runs = order_map[::RUN] // RUN
    b = jnp.arange(128)
    q = jnp.arange(RUN)
    cos1, sin1 = turn(b[:, None] * runs[None, :], 128)
    table = jnp.concatenate([jnp.stack([cos1, sin1], 2), jnp.stack([sin1, -cos1], 2)], 0)
    table = table.reshape(256, 2 * parts).astype(jnp.bfloat16)
    cos2, sin2 = turn(b[:, None] * q[None, :], NLON)
    cos3, sin3 = turn(q[:, None] * q[None, :], RUN)
    last = jnp.concatenate([cos3, -sin3], 1)

    chunk = chunk.reshape(parts, 2, items * count)
    chunk, table, cos2, sin2, last = lax.optimization_barrier((chunk, table, cos2, sin2, last))
    flat = lax.all_to_all(chunk, "ord", 0, 0, tiled=True).reshape(2 * parts, items * count)
    mid = jnp.dot(table, flat, preferred_element_type=jnp.float32).reshape(2, 128, items, count)
    cos2, sin2 = cos2[:, None, :], sin2[:, None, :]
    real = mid[0] * cos2 - mid[1] * sin2
    imag = mid[0] * sin2 + mid[1] * cos2
    field = lax.dot_general(
        last, jnp.concatenate([real, imag], 2),
        (((1,), (2,)), ((), ())), precision=lax.Precision.HIGH)
    field = field.reshape(parts, NLON // parts, 3, 4).astype(jnp.bfloat16)
    field = jnp.transpose(field, (0, 2, 3, 1)).reshape(parts * 3, 4, NLON // parts)
    field = lax.all_to_all(field, "ord", 0, 0, tiled=True)
    return jnp.transpose(field, (2, 0, 1)).reshape(NLON // parts, cycles * 3 * shells)


def solution(mesh):
    return jax.shard_map(
        body,
        mesh=mesh,
        in_specs=(P("ord", "blk", None), P(None, None, "ord", "blk"), P(), P(), P("blk")),
        out_specs=P("ord", "blk"),
        check_vma=False,
    )
```

```python
import functools
import math

import jax
import jax.numpy as jnp
from jax import lax
from jax.experimental import pallas as pl
from jax.experimental.pallas import tpu as pltpu
from jax.sharding import PartitionSpec as P

ORDERS = 2880
RUN = 45
QUARTER = 720
START = 1408
WIDE = 1536
KEPT = 1472
NLON = 5760
GROUP = 5
CHUNKS = (0, 20, 30, 40, 45)
GAUSS_TAIL = 2 * GROUP * 640
GAUSS_LANES = GAUSS_TAIL + 896
PANEL_TAIL = GROUP * START
PANEL_LANES = PANEL_TAIL + 384
CYCLE_LANE = PANEL_TAIL + 320
GAUSS_PAIRS = [(0, 1), (1, 0), (2, 3), (3, 2)]
PANEL_PAIRS = [(1, 2), (2, 1), (3, 0), (0, 3)]


def pack_panel(spot_ref, cycle_ref, *rest, steps):
    out_ref = rest[-1]
    cycle = cycle_ref[...]
    row = lax.broadcasted_iota(jnp.int32, (16, 16), 0)
    lane = lax.broadcasted_iota(jnp.int32, (16, 16), 1)
    digits = []
    for digit in (cycle // 64, cycle % 64):
        spread = jnp.broadcast_to(digit.astype(jnp.float32), (16, 16))
        digits.append(jnp.sum(jnp.where(row == lane, spread, 0.0), 1, keepdims=True))
    digits = jnp.concatenate(digits, 1).astype(jnp.bfloat16)
    for g in range(steps):
        main_ref, tail_ref = rest[2 * g:2 * g + 2]
        out_ref[g, :, CYCLE_LANE:CYCLE_LANE + 2] = digits
        for o in range(GROUP):
            out_ref[g, :, START * o:START * (o + 1)] = main_ref[o]
            out_ref[g, :, PANEL_TAIL + 64 * o:PANEL_TAIL + 64 * (o + 1)] = tail_ref[o, :, 0:64]


def pack_gauss(*rest, steps):
    out_ref = rest[-1]
    for g in range(steps):
        for k in range(2):
            for o in range(GROUP):
                j = k * GROUP + o
                plane = rest[2 * g + k]
                out_ref[g, :, 640 * j:640 * (j + 1)] = plane[0, o, :, 0:640]
                out_ref[g, :, GAUSS_TAIL + 80 * j:GAUSS_TAIL + 80 * (j + 1)] = plane[0, o, :, 640:720]


def panel_specs(skip, upper):
    return [
        pl.BlockSpec((GROUP, 16, START), lambda i, spot: (i + skip, 0, upper(spot[0]))),
        pl.BlockSpec((GROUP, 16, 128), lambda i, spot: (i + skip, 0, 11 + 11 * upper(spot[0]))),
    ]


def packed_panel(spot, cycle, panel, after, base, count):
    steps = count // GROUP
    specs = []
    for g in range(steps):
        specs += panel_specs(base // GROUP + g, lambda blk: 1 - blk // 2)
    return pl.pallas_call(
        functools.partial(pack_panel, steps=steps),
        out_shape=jax.ShapeDtypeStruct((steps, 16, PANEL_LANES), jnp.bfloat16),
        grid_spec=pltpu.PrefetchScalarGridSpec(
            num_scalar_prefetch=1,
            grid=(1,),
            in_specs=[pl.BlockSpec((1, 16), lambda i, spot: (0, 0))] + specs
            + [pl.BlockSpec(memory_space=pl.ANY)] * len(after),
            out_specs=pl.BlockSpec(memory_space=pltpu.VMEM),
        ),
        compiler_params=pltpu.CompilerParams(vmem_limit_bytes=10 << 20),
        cost_estimate=pl.CostEstimate(flops=0, bytes_accessed=count * 100000, transcendentals=0),
        name="pack_panel",
    )(spot, cycle, *[panel] * (2 * steps), *after)


def packed_gauss(own, after, base, count):
    steps, skip = count // GROUP, base // GROUP
    specs = []
    for g in range(steps):
        for k in range(2):
            specs.append(pl.BlockSpec(
                (1, GROUP, 16, QUARTER), lambda i, k=k, at=skip + g: (k, at, 0, 0)))
    return pl.pallas_call(
        functools.partial(pack_gauss, steps=steps),
        out_shape=jax.ShapeDtypeStruct((steps, 16, GAUSS_LANES), jnp.bfloat16),
        grid=(1,),
        in_specs=specs + [pl.BlockSpec(memory_space=pl.ANY)] * len(after),
        out_specs=pl.BlockSpec(memory_space=pltpu.VMEM),
        compiler_params=pltpu.CompilerParams(vmem_limit_bytes=10 << 20),
        cost_estimate=pl.CostEstimate(flops=0, bytes_accessed=count * 100000, transcendentals=0),
        name="pack_gauss",
    )(*[own] * (2 * steps), *after)


def sums_kernel(spot_ref, order_ref, decay_ref, cycle_ref, own_ref, other_ref, main_ref, tail_ref,
                far_ref, *rest, base):
    keep_ref, send_ref, gs_ref, gn_ref, table_ref, mate_ref, angle_ref = rest[-7:]
    step = pl.program_id(0)
    half = spot_ref[0] // 2
    odd = spot_ref[0] % 2 == 1
    first = (half * START).astype(jnp.float32)
    degree = lax.broadcasted_iota(jnp.int32, (1, WIDE), 1).astype(jnp.float32) + first

    @pl.when(step == 0)
    def _():
        edge = jnp.zeros((2, GROUP, 16, 128), jnp.bfloat16)
        for ref in (gs_ref, gn_ref):
            ref[:, :, :, 0:128] = edge
            ref[:, :, :, START:WIDE] = edge
        table_ref[:, :, START:WIDE] = jnp.zeros((GROUP, 32, 128), jnp.bfloat16)
        digits = far_ref[0, :, CYCLE_LANE:CYCLE_LANE + 2].astype(jnp.float32)
        mates = digits[:, 0:1] * 64.0 + digits[:, 1:2]
        cycles = jnp.broadcast_to(mates, (16, 128)).T[0:8, :]
        cycles = jnp.concatenate([jnp.zeros((8, 16), jnp.float32), cycles], 1)
        lane = lax.broadcasted_iota(jnp.int32, (8, 32), 1)
        for i in range(16):
            cycles = jnp.where(lane == i, cycle_ref[i].astype(jnp.float32), cycles)
        theta = math.pi * (cycles + 0.5) / ORDERS
        angle_ref[0] = jnp.cos(theta)
        angle_ref[1] = 1.0 / jnp.sin(theta)

    for o in range(GROUP):
        for k in range(2):
            j = k * GROUP + o
            mate_ref[k, o, :, 0:640] = other_ref[0, :, 640 * j:640 * (j + 1)]
            mate_ref[k, o, :, 640:720] = other_ref[0, :, GAUSS_TAIL + 80 * j:GAUSS_TAIL + 80 * (j + 1)]
        table_ref[o, 0:16, 0:START] = main_ref[o]
        table_ref[o, 0:16, START:KEPT] = tail_ref[o, :, 0:64]
        table_ref[o, 16:32, 0:START] = far_ref[0, :, START * o:START * (o + 1)]
        table_ref[o, 16:32, START:KEPT] = far_ref[0, :, PANEL_TAIL + 64 * o:PANEL_TAIL + 64 * (o + 1)]
    low = jnp.where(odd, mate_ref[...], own_ref[...])
    high = jnp.where(odd, own_ref[...], mate_ref[...])

    @pl.when(half == 0)
    def _():
        gs_ref[:, :, :, 0:720] = low
        gs_ref[:, :, :, 720:1440] = high
        gn_ref[:, :, :, 0:719] = low[:, :, :, 1:]
        gn_ref[:, :, :, 719:1439] = high

    @pl.when(half == 1)
    def _():
        gs_ref[:, :, :, 32:752] = low
        gs_ref[:, :, :, 752:1472] = high
        gn_ref[:, :, :, 31:751] = low
        gn_ref[:, :, :, 751:1471] = high

    cosine = angle_ref[0, 0:1]
    inverse = angle_ref[1, 0:1]
    orders = [order_ref[base + step * GROUP + o].astype(jnp.float32) for o in range(GROUP)]
    sums = []
    for o in range(GROUP):
        gap = jnp.maximum((degree + 1.0) * (degree + 1.0) - orders[o] * orders[o], 0.0)
        slope = decay_ref[2] * jnp.sqrt(gap)
        g = [gs_ref[k, o].astype(jnp.float32) for k in range(2)]
        n = [gn_ref[k, o].astype(jnp.float32) for k in range(2)]
        weights = jnp.concatenate(
            [g[0] * decay_ref[1], g[1] * decay_ref[1], g[0] * decay_ref[0], g[1] * decay_ref[0],
             n[0] * slope, n[1] * slope], 0).astype(jnp.bfloat16)
        sums.append(lax.dot_general(
            weights, table_ref[o], (((1,), (1,)), ((), ())), preferred_element_type=jnp.float32))
    mixed = []
    for o in range(GROUP):
        main, bare, tilt = sums[o][0:32], sums[o][32:64], sums[o][64:96]
        polar = (tilt - cosine * (main - bare)) * inverse
        bare = orders[o] * inverse * bare
        mixed.append(jnp.concatenate(
            [main[0:16], polar[0:16], -bare[16:32], main[16:32], polar[16:32], bare[0:16]], 0).T)
    for o in range(GROUP):
        keep_ref[o] = mixed[o][:16]
        send_ref[o] = mixed[o][16:].astype(jnp.bfloat16)


def partial_sums(spot, orders, decay, cycle, own, other, panel, far, after, base, count, place, size, begun):
    skip = base // GROUP
    into = place // GROUP
    total = begun[0].shape[0] if begun else size
    smem = pl.BlockSpec(memory_space=pltpu.SMEM)
    here = pl.BlockSpec(memory_space=pltpu.VMEM)
    out = pl.BlockSpec((GROUP, 16, 96), lambda i, spot: (i + into, 0, 0))
    return pl.pallas_call(
        functools.partial(sums_kernel, base=base),
        out_shape=[jax.ShapeDtypeStruct((total, 16, 96), jnp.float32),
                   jax.ShapeDtypeStruct((total, 16, 96), jnp.bfloat16)],
        input_output_aliases={9: 0, 10: 1} if begun else {},
        grid_spec=pltpu.PrefetchScalarGridSpec(
            num_scalar_prefetch=1,
            grid=(count // GROUP,),
            in_specs=[
                smem, here, smem,
                pl.BlockSpec((2, GROUP, 16, QUARTER), lambda i, spot: (0, i + skip, 0, 0)),
                here if count == GROUP else pl.BlockSpec((1, 16, GAUSS_LANES), lambda i, spot: (i, 0, 0)),
            ] + panel_specs(skip, lambda blk: blk // 2)
            + [here if count == GROUP else pl.BlockSpec((1, 16, PANEL_LANES), lambda i, spot: (i, 0, 0))]
            + [pl.BlockSpec(memory_space=pl.ANY)] * (len(begun) + len(after)),
            out_specs=[out, out],
            scratch_shapes=[
                pltpu.VMEM((2, GROUP, 16, WIDE), jnp.bfloat16),
                pltpu.VMEM((2, GROUP, 16, WIDE), jnp.bfloat16),
                pltpu.VMEM((GROUP, 32, WIDE), jnp.bfloat16),
                pltpu.VMEM((2, GROUP, 16, QUARTER), jnp.bfloat16),
                pltpu.VMEM((2, 8, 32), jnp.float32),
            ],
        ),
        compiler_params=pltpu.CompilerParams(vmem_limit_bytes=16 << 20),
        cost_estimate=pl.CostEstimate(
            flops=count * 32 * 128 * WIDE * 2, bytes_accessed=count * 200000, transcendentals=0),
        name="partial_sums",
    )(spot, orders, decay, cycle, own, other, panel, panel, far, *begun, *after)


def turn(phase, period):
    angle = (phase % period).astype(jnp.float32) * (2.0 * math.pi / period)
    return jnp.cos(angle), jnp.sin(angle)


def body(panel, gauss, height, order_map, cycle_map):
    count, cycles, _ = panel.shape
    shells = height.shape[0]
    here = lax.axis_index("ord")
    spot = lax.axis_index("blk").astype(jnp.int32).reshape(1)
    own = jnp.transpose(gauss, (0, 2, 1, 3))
    own = pltpu.with_memory_space_constraint(own, pltpu.HBM)
    panel = pltpu.with_memory_space_constraint(panel, pltpu.HBM)
    cycle_row = pltpu.with_memory_space_constraint(cycle_map[None, :], pltpu.HBM)
    spans = list(zip(CHUNKS[:-1], CHUNKS[1:]))
    orders_int = lax.dynamic_slice_in_dim(order_map, here * count, count, 0)
    degree = (spot // 2 * START + jnp.arange(WIDE)).astype(jnp.float32)[None, :]
    here_ = jnp.exp(-(degree + 2.0) * height[:, None] / ORDERS)
    next_ = jnp.exp(-(degree + 3.0) * height[:, None] / ORDERS)
    decay = jnp.stack([here_, here_ * (degree + 1.0), next_])
    packed, kept, sent, added = [], [], [], []

    def start(c):
        a, b = spans[c]
        after = (kept[0:1] if c >= 2 else []) + ([packed[-1][2]] if packed else [])
        part = packed_panel(spot, cycle_row, panel, after, a, b - a)
        far = lax.ppermute(part, "blk", PANEL_PAIRS)
        coef = packed_gauss(own, [part], a, b - a)
        packed.append((lax.ppermute(coef, "blk", GAUSS_PAIRS), far, coef))

    start(0)
    start(1)
    for c, (a, b) in enumerate(spans):
        begun = [kept.pop(), sent.pop()] if c >= 2 else []
        size = CHUNKS[4] - CHUNKS[1] if c == 1 else b - a
        after = kept[-1:] + (added if c == 3 else [])
        keep, send = partial_sums(
            spot, orders_int, decay, cycle_map, own, packed[c][0], panel, packed[c][1],
            after, a, b - a, a - CHUNKS[1] if c else 0, size, begun)
        kept.append(keep)
        sent.append(send)
        if c in (0, 3):
            added.append(lax.ppermute(send, "blk", PANEL_PAIRS))
        if c < 2:
            start(c + 2)
    total = jnp.concatenate(kept, 0) + jnp.concatenate(added, 0).astype(jnp.float32)
    total = lax.optimization_barrier(total.astype(jnp.bfloat16))
    chunk = jnp.transpose(total.reshape(count, cycles, 2, 4, 12), (1, 3, 2, 4, 0))

    parts = ORDERS // count
    items = cycles * 3 * shells // parts
    runs = order_map[::RUN] // RUN
    b = jnp.arange(128)
    q = jnp.arange(RUN)
    cos1, sin1 = turn(b[:, None] * runs[None, :], 128)
    table = jnp.concatenate([jnp.stack([cos1, sin1], 2), jnp.stack([sin1, -cos1], 2)], 0)
    table = table.reshape(256, 2 * parts).astype(jnp.bfloat16)
    cos2, sin2 = turn(b[:, None] * q[None, :], NLON)
    cos3, sin3 = turn(q[:, None] * q[None, :], RUN)
    last = jnp.concatenate([cos3, -sin3], 1)

    chunk = chunk.reshape(parts, 2, items * count)
    chunk, table, cos2, sin2, last = lax.optimization_barrier((chunk, table, cos2, sin2, last))
    flat = lax.all_to_all(chunk, "ord", 0, 0, tiled=True).reshape(2 * parts, items * count)
    mid = jnp.dot(table, flat, preferred_element_type=jnp.float32).reshape(2, 128, items, count)
    cos2, sin2 = cos2[:, None, :], sin2[:, None, :]
    real = mid[0] * cos2 - mid[1] * sin2
    imag = mid[0] * sin2 + mid[1] * cos2
    field = lax.dot_general(
        last, jnp.concatenate([real, imag], 2),
        (((1,), (2,)), ((), ())), precision=lax.Precision.HIGH)
    field = field.reshape(parts, NLON // parts, 3, 4).astype(jnp.bfloat16)
    field = jnp.transpose(field, (0, 2, 3, 1)).reshape(parts * 3, 4, NLON // parts)
    field = lax.all_to_all(field, "ord", 0, 0, tiled=True)
    return jnp.transpose(field, (2, 0, 1)).reshape(NLON // parts, cycles * 3 * shells)


def solution(mesh):
    return jax.shard_map(
        body,
        mesh=mesh,
        in_specs=(P("ord", "blk", None), P(None, None, "ord", "blk"), P(), P(), P("blk")),
        out_specs=P("ord", "blk"),
        check_vma=False,
    )
```
